128 devices in a mesh: row: 16 (over z_hi, y, core), col: 8 (over z_lo, x).
Axes of the slice: x: 4, y: 4, z: 4 (z_hi: 2, z_lo: 2; z = z_hi * 2 + z_lo), core: 2. Of those that a mesh axis runs over, the one named last changes fastest.
Arguments:
- field_in: bfloat16 [512, 512, 256], P('row', 'col'), may hold values from -40 to 40
- cotangent: bfloat16 [512, 512, 256], P('row', 'col'), may hold values from -6 to 6
- gain_conv: float32 [256], replicated, may hold values from 0.1 to 1.9
- w_expand: bfloat16 [256, 1024], replicated, may hold values from -0.375 to 0.375
- w_depth: float32 [3, 3, 1024], replicated, may hold values from -4 to 4
- w_project: bfloat16 [1024, 256], replicated, may hold values from -0.1875 to 0.1875
- gain_attn: float32 [256], replicated, may hold values from 0.1 to 1.9
- w_qkv: bfloat16 [256, 768], replicated, may hold values from -1.25 to 1.25
- w_out: bfloat16 [256, 256], replicated, may hold values from -0.375 to 0.375
Outputs:
- grad_field: bfloat16 [512, 512, 256], P('row', 'col')
- grad_gain_conv: float32 [256], replicated
- grad_expand: float32 [256, 1024], replicated
- grad_depth: float32 [3, 3, 1024], replicated
- grad_project: float32 [1024, 256], replicated
- grad_gain_attn: float32 [256], replicated
- grad_qkv: float32 [256, 768], replicated
- grad_out: float32 [256, 256], replicated
The draws below stay inside these ranges and needn't reach their ends.
All inputs are finite; a program needn't handle non-finite values.
Results may differ from the reference program's by a relative error of at most 0.025.
The reference program's roundings to bfloat16 on the way count: a program that leaves them out, or rounds other values in their place, can miss the bound.
Values may be sent and summed in bfloat16 or wider, within the bound.
No kernel may reach another device: no remote copies, remote signals or barrier semaphores. Data moves between devices by JAX's collectives and lax.ppermute only.
A program may use at most 192 MiB of HBM per device.

```python
import math
import jax
import jax.numpy as jnp
from jax import lax

WIDTH = 256
HEADS = 8
EXPANDED = 1024
GRID = 16
FIELD_ROWS = 512
FIELD_COLS = 512
TOKENS = 262144


def draw_field_in(key, part):
    streams = jax.random.split(jax.random.fold_in(key, 11), 3)
    noise = jnp.clip(jax.random.normal(streams[0], (FIELD_ROWS, FIELD_COLS, WIDTH), jnp.float32), -4.0, 4.0)
    token_scale = jnp.exp(jax.random.uniform(streams[1], (FIELD_ROWS, FIELD_COLS, 1), jnp.float32) * math.log(10.0))
    chan_scale = jnp.exp(jax.random.uniform(streams[2], (WIDTH,), jnp.float32) * math.log(10.0))
    return (noise * token_scale * chan_scale * 0.1).astype(jnp.bfloat16)


def draw_w_qkv(key, part):
    streams = jax.random.split(jax.random.fold_in(key, 23), 1)
    weights = jnp.clip(jax.random.normal(streams[0], (WIDTH, 3 * WIDTH), jnp.float32), -4.0, 4.0) * WIDTH ** (-0.5)
    return weights.astype(jnp.bfloat16)


def steps_of(own_key, shape, cuts, smallest, top_value):
    def one(position, blocks):
        heights = jax.random.uniform(jax.random.fold_in(jax.random.fold_in(own_key, 6), position), (blocks,), jnp.float32, smallest / len(cuts), top_value / len(cuts))
        return jnp.repeat(jnp.exp(heights), shape[position] // blocks).reshape((-1,) + (1,) * (len(shape) - position - 1))

    level = one(*cuts[0])
    for cut in cuts[1:]:
        level = level * one(*cut)
    return level


def normal_values(key, shape, scale, limit, shards=(), kind=jnp.bfloat16):
    gain = steps_of(key, shape, shards, -0.22, 0.18) if shards else 1.0
    result = jax.random.normal(key, shape, jnp.float32) * scale * gain
    return jnp.minimum(jnp.maximum(result, -limit), limit).astype(kind)


def setup_inputs(seed: int = 0) -> dict:
    splits = jax.random.split(jax.random.key(seed), 10)
    return {
        "field_in": draw_field_in(jax.random.fold_in(splits[9], 71), 0),
        "cotangent": normal_values(splits[1], (FIELD_ROWS, FIELD_COLS, WIDTH), 1.0, 6.0, ((0, 16), (1, 8))),
        "gain_conv": jnp.clip(1.0 + 0.18 * jax.random.normal(splits[2], (WIDTH,), jnp.float32), 0.1, 1.9),
        "w_expand": normal_values(splits[3], (WIDTH, EXPANDED), WIDTH ** -0.5, 0.375),
        "w_depth": normal_values(splits[4], (3, 3, EXPANDED), 1.0, 4.0, (), jnp.float32),
        "w_project": normal_values(splits[5], (EXPANDED, WIDTH), EXPANDED ** -0.5, 0.1875),
        "gain_attn": jnp.clip(1.0 + 0.18 * jax.random.normal(splits[6], (WIDTH,), jnp.float32), 0.1, 1.9),
        "w_qkv": draw_w_qkv(jax.random.fold_in(splits[9], 71), 0),
        "w_out": normal_values(splits[8], (WIDTH, WIDTH), WIDTH ** -0.5, 0.375),
    }


norm_eps = 1e-05
root_half = 0.7071067811865476
inv_root_two_pi = 0.3989422804014327

def gelu_value(values):
    return 0.5 * values * (1.0 + lax.erf(values * root_half))

def gelu_slope(values):
    return 0.5 * (1.0 + lax.erf(values * root_half)) + values * jnp.exp(-0.5 * values * values) * inv_root_two_pi

def normalize(values):
    centre = lax.optimization_barrier(jnp.mean(values, axis=-1, keepdims=True))
    centred = values - centre
    inv_dev = lax.rsqrt(lax.optimization_barrier(jnp.mean(centred * centred, axis=-1, keepdims=True)) + norm_eps)
    return (centred * inv_dev, inv_dev)

def normalize_back(grad_normed, normed, inv_dev):
    return inv_dev * (grad_normed - lax.optimization_barrier(jnp.mean(grad_normed, axis=-1, keepdims=True)) - normed * lax.optimization_barrier(jnp.mean(grad_normed * normed, axis=-1, keepdims=True)))

def product(form, left, right):
    return jnp.einsum(form, left.astype(jnp.float32), right.astype(jnp.float32))

def expand_rows(block_in, gain_conv, w_expand):
    flat_rows = block_in.reshape(-1, block_in.shape[-1]).astype(jnp.float32)
    normed, inv_dev = normalize(flat_rows)
    scaled = (normed * gain_conv).astype(jnp.bfloat16)
    pre_act = jnp.dot(scaled, w_expand, preferred_element_type=jnp.float32)
    return (normed, inv_dev, scaled, pre_act)

def depthwise(padded, w_depth, row_count, col_count):
    summed = jnp.zeros((row_count, col_count, padded.shape[-1]), jnp.float32)
    for row_off in range(3):
        for col_off in range(3):
            summed = summed + padded[row_off:row_off + row_count, col_off:col_off + col_count].astype(jnp.float32) * w_depth[row_off, col_off]
    return summed

def spread_back(grad_pad, w_depth, row_count, col_count):
    summed = jnp.zeros((row_count, col_count, grad_pad.shape[-1]), jnp.float32)
    for row_off in range(3):
        for col_off in range(3):
            summed = summed + grad_pad[2 - row_off:2 - row_off + row_count, 2 - col_off:2 - col_off + col_count].astype(jnp.float32) * w_depth[row_off, col_off]
    return summed

def depth_grad(hidden_pad, grad_conv, row_count, col_count):
    grad_wide = grad_conv.astype(jnp.float32)
    pieces = []
    for row_off in range(3):
        for col_off in range(3):
            pieces.append(lax.optimization_barrier(jnp.sum(hidden_pad[row_off:row_off + row_count, col_off:col_off + col_count].astype(jnp.float32) * grad_wide, axis=(0, 1))))
    return jnp.stack(pieces).reshape(3, 3, -1)

def window_back(windows, cot_windows, gain_attn, w_qkv, w_out):
    count, length, chans = windows.shape
    head_size = chans // HEADS
    scale_qk = head_size ** (-0.5)
    normed, inv_dev = normalize(windows.astype(jnp.float32))
    scaled = (normed * gain_attn).astype(jnp.bfloat16)
    projected = product('wtc,cd->wtd', scaled, w_qkv).astype(jnp.bfloat16)
    query = projected[..., :chans].reshape(count, length, HEADS, head_size)
    keys_all = projected[..., chans:2 * chans].reshape(count, length, HEADS, head_size)
    values_all = projected[..., 2 * chans:].reshape(count, length, HEADS, head_size)
    scores = product('wqhd,wkhd->whqk', query, keys_all) * scale_qk
    scores = scores - lax.optimization_barrier(jnp.max(scores, axis=-1, keepdims=True))
    expons = jnp.exp(scores)
    probs = expons / lax.optimization_barrier(jnp.sum(expons, axis=-1, keepdims=True))
    probs_b = probs.astype(jnp.bfloat16)
    attended = product('whqk,wkhd->wqhd', probs_b, values_all).astype(jnp.bfloat16).reshape(count, length, chans)
    grad_att = product('wtd,cd->wtc', cot_windows, w_out).astype(jnp.bfloat16).reshape(count, length, HEADS, head_size)
    grad_out = product('wtc,wtd->cd', attended, cot_windows)
    grad_probs = product('wqhd,wkhd->whqk', grad_att, values_all)
    grad_value = product('whqk,wqhd->wkhd', probs_b, grad_att).astype(jnp.bfloat16)
    grad_scores = (scale_qk * probs * (grad_probs - lax.optimization_barrier(jnp.sum(grad_probs * probs, axis=-1, keepdims=True)))).astype(jnp.bfloat16)
    grad_query = product('whqk,wkhd->wqhd', grad_scores, keys_all).astype(jnp.bfloat16)
    grad_key = product('whqk,wqhd->wkhd', grad_scores, query).astype(jnp.bfloat16)
    grad_proj = jnp.concatenate([grad_query.reshape(count, length, chans), grad_key.reshape(count, length, chans), grad_value.reshape(count, length, chans)], axis=-1)
    grad_qkv = product('wtc,wtd->cd', scaled, grad_proj)
    grad_scaled = product('wtd,cd->wtc', grad_proj, w_qkv)
    grad_gain = lax.optimization_barrier(jnp.sum(grad_scaled * normed, axis=(0, 1)))
    grad_branch = normalize_back(grad_scaled * gain_attn, normed, inv_dev).astype(jnp.bfloat16)
    return (grad_branch, (grad_qkv, grad_out, grad_gain))

def reference(field_in, cotangent, gain_conv, w_expand, w_depth, w_project, gain_attn, w_qkv, w_out):
    height, breadth, chans = field_in.shape
    expand_w = w_expand.shape[1]
    strip_len = 16
    strip_count = height // strip_len
    grad_scale = TOKENS ** (-0.5)
    padded_in = jnp.pad(field_in, ((2, 2), (0, 0), (0, 0)))

    def hidden_rows(start):
        rows_in = lax.dynamic_slice_in_dim(padded_in, start, strip_len + 4, 0)
        normed, inv_dev, scaled, pre_act = expand_rows(rows_in, gain_conv, w_expand)
        row_glob = start - 2 + jnp.arange(strip_len + 4, dtype=jnp.int32)
        inside = ((row_glob >= 0) & (row_glob < height)).astype(jnp.float32)
        hidden = (gelu_value(pre_act).reshape(strip_len + 4, breadth, expand_w) * inside[:, None, None]).astype(jnp.bfloat16)
        hidden_pad = jnp.pad(hidden, ((0, 0), (1, 1), (0, 0)))
        conv = depthwise(hidden_pad, w_depth, strip_len + 2, breadth)
        return (rows_in, normed, inv_dev, scaled, pre_act, hidden_pad, conv)

    def forward_strip(index):
        start = index.astype(jnp.int32) * strip_len
        rows_in, normed, inv_dev, scaled, pre_act, hidden_pad, conv = hidden_rows(start)
        acted = gelu_value(conv[1:strip_len + 1]).astype(jnp.bfloat16).reshape(-1, expand_w)
        core_in = rows_in[2:strip_len + 2].reshape(-1, chans).astype(jnp.float32)
        mixed = core_in + jnp.dot(acted, w_project, preferred_element_type=jnp.float32)
        return mixed.astype(jnp.bfloat16).reshape(strip_len, breadth, chans)
    mid_field = lax.map(forward_strip, jnp.arange(strip_count, dtype=jnp.int32)).reshape(height, breadth, chans)
    span_rows = height // GRID
    span_cols = breadth // GRID
    window_count = span_rows * span_cols
    group = 4 if window_count % 4 == 0 else 2 if window_count % 2 == 0 else 1

    def to_windows(values):
        arranged = values.reshape(GRID, span_rows, GRID, span_cols, chans).transpose(1, 3, 0, 2, 4)
        return arranged.reshape(window_count // group, group, GRID * GRID, chans)

    def attend_step(carry, window_pair):
        grad_branch, sums = window_back(window_pair[0], window_pair[1], gain_attn, w_qkv, w_out)
        return (tuple((before + added for before, added in zip(carry, sums))), grad_branch)
    attn_init = (jnp.zeros((chans, 3 * chans), jnp.float32), jnp.zeros((chans, chans), jnp.float32), jnp.zeros((chans,), jnp.float32))
    attn_sums, grad_windows = lax.scan(attend_step, attn_init, (to_windows(mid_field), to_windows(cotangent)))
    grad_branch = grad_windows.reshape(span_rows, span_cols, GRID, GRID, chans).transpose(2, 0, 3, 1, 4).reshape(height, breadth, chans)
    grad_mid = cotangent.astype(jnp.float32) + grad_branch.astype(jnp.float32)
    padded_grad = jnp.pad(grad_mid.astype(jnp.bfloat16), ((1, 1), (0, 0), (0, 0)))

    def back_strip(carry, index):
        start = index.astype(jnp.int32) * strip_len
        rows_in, normed, inv_dev, scaled, pre_act, hidden_pad, conv = hidden_rows(start)
        grad_rows = lax.dynamic_slice_in_dim(padded_grad, start, strip_len + 2, 0)
        acted = gelu_value(conv[1:strip_len + 1]).astype(jnp.bfloat16).reshape(-1, expand_w)
        grad_acted = jnp.dot(grad_rows.reshape(-1, chans), w_project.T, preferred_element_type=jnp.float32).astype(jnp.bfloat16)
        grad_conv = (grad_acted.astype(jnp.float32).reshape(conv.shape) * gelu_slope(conv)).astype(jnp.bfloat16)
        core_grad = grad_rows[1:strip_len + 1].reshape(-1, chans)
        grad_project = jnp.dot(acted.T, core_grad, preferred_element_type=jnp.float32)
        grad_conv_pad = jnp.pad(grad_conv, ((0, 0), (1, 1), (0, 0)))
        grad_hidden = spread_back(grad_conv_pad, w_depth, strip_len, breadth).reshape(-1, expand_w)
        grad_depth = depth_grad(hidden_pad[1:strip_len + 3], grad_conv[1:strip_len + 1], strip_len, breadth)
        core_pre = pre_act.reshape(strip_len + 4, breadth, expand_w)[2:strip_len + 2].reshape(-1, expand_w)
        grad_pre = (grad_hidden * gelu_slope(core_pre)).astype(jnp.bfloat16)
        core_scaled = scaled.reshape(strip_len + 4, breadth, chans)[2:strip_len + 2].reshape(-1, chans)
        core_normed = normed.reshape(strip_len + 4, breadth, chans)[2:strip_len + 2].reshape(-1, chans)
        core_inv = inv_dev.reshape(strip_len + 4, breadth, 1)[2:strip_len + 2].reshape(-1, 1)
        grad_expand = jnp.dot(core_scaled.T, grad_pre, preferred_element_type=jnp.float32)
        grad_scaled = jnp.dot(grad_pre, w_expand.T, preferred_element_type=jnp.float32)
        grad_gain = lax.optimization_barrier(jnp.sum(grad_scaled * core_normed, axis=0))
        core_mid = lax.dynamic_slice_in_dim(grad_mid, start, strip_len, 0).reshape(-1, chans)
        grad_rows_out = (core_mid + normalize_back(grad_scaled * gain_conv, core_normed, core_inv)).astype(jnp.bfloat16)
        sums = (grad_gain, grad_expand, grad_depth, grad_project)
        return (tuple((before + added for before, added in zip(carry, sums))), grad_rows_out.reshape(strip_len, breadth, chans))
    conv_init = (jnp.zeros((chans,), jnp.float32), jnp.zeros((chans, expand_w), jnp.float32), jnp.zeros((3, 3, expand_w), jnp.float32), jnp.zeros((expand_w, chans), jnp.float32))
    conv_sums, grad_strips = lax.scan(back_strip, conv_init, jnp.arange(strip_count, dtype=jnp.int32))
    grad_field = grad_strips.reshape(height, breadth, chans)
    return (grad_field, conv_sums[0] * grad_scale, conv_sums[1] * grad_scale, conv_sums[2] * grad_scale, conv_sums[3] * grad_scale, attn_sums[2] * grad_scale, attn_sums[0] * grad_scale, attn_sums[1] * grad_scale)
```

```python
import jax
import jax.numpy as jnp
from jax import lax
from jax.sharding import PartitionSpec as P

HEADS = 8
GRID = 16


norm_eps = 1e-05
root_half = 0.7071067811865476
inv_root_two_pi = 0.3989422804014327


def padded_2(block, sides, width):
    for axis, dim in sides:
        count = lax.axis_size(axis)
        forward = [(i, i + 1) for i in range(count - 1)]
        backward = [(target, source) for source, target in forward]
        low = lax.ppermute(
            lax.slice_in_dim(block, block.shape[dim] - width, None, axis=dim), axis, forward
        )
        high = lax.ppermute(lax.slice_in_dim(block, 0, width, axis=dim), axis, backward)
        block = jnp.concatenate([low, block, high], axis=dim)
    return block


def gelu_value(values):
    return 0.5 * values * (1.0 + lax.erf(values * root_half))


def gelu_slope(values):
    return (
        0.5 * (1.0 + lax.erf(values * root_half))
        + values * jnp.exp(-0.5 * values * values) * inv_root_two_pi
    )


def normalize(values):
    centre = jnp.mean(values, axis=-1, keepdims=True)
    centred = values - centre
    inv_dev = lax.rsqrt(jnp.mean(centred * centred, axis=-1, keepdims=True) + norm_eps)
    return (centred * inv_dev, inv_dev)


def normalize_back(grad_normed, normed, inv_dev):
    return inv_dev * (
        grad_normed
        - jnp.mean(grad_normed, axis=-1, keepdims=True)
        - normed * jnp.mean(grad_normed * normed, axis=-1, keepdims=True)
    )


def product(form, left, right):
    return jnp.einsum(form, left, right, preferred_element_type=jnp.float32)


def expand_rows(block_in, gain_conv, w_expand):
    flat_rows = block_in.reshape(-1, block_in.shape[-1]).astype(jnp.float32)
    normed, inv_dev = normalize(flat_rows)
    scaled = (normed * gain_conv).astype(jnp.bfloat16)
    pre_act = jnp.dot(scaled, w_expand, preferred_element_type=jnp.float32)
    return (normed, inv_dev, scaled, pre_act)


def depthwise(padded, w_depth, row_count, col_count):
    summed = jnp.zeros((row_count, col_count, padded.shape[-1]), jnp.float32)
    for row_off in range(3):
        for col_off in range(3):
            summed = (
                summed
                + padded[row_off : row_off + row_count, col_off : col_off + col_count].astype(
                    jnp.float32
                )
                * w_depth[row_off, col_off]
            )
    return summed


def spread_back(grad_pad, w_depth, row_count, col_count):
    summed = jnp.zeros((row_count, col_count, grad_pad.shape[-1]), jnp.float32)
    for row_off in range(3):
        for col_off in range(3):
            summed = (
                summed
                + grad_pad[
                    2 - row_off : 2 - row_off + row_count, 2 - col_off : 2 - col_off + col_count
                ].astype(jnp.float32)
                * w_depth[row_off, col_off]
            )
    return summed


def depth_grad(hidden_pad, grad_conv, row_count, col_count):
    grad_wide = grad_conv.astype(jnp.float32)
    pieces = []
    for row_off in range(3):
        for col_off in range(3):
            pieces.append(
                jnp.sum(
                    hidden_pad[row_off : row_off + row_count, col_off : col_off + col_count].astype(
                        jnp.float32
                    )
                    * grad_wide,
                    axis=(0, 1),
                )
            )
    return jnp.stack(pieces).reshape(3, 3, -1)


def window_back(windows, cot_windows, gain_attn, w_qkv, w_out):
    count, length, chans = windows.shape
    head_size = chans // HEADS
    scale_qk = head_size ** (-0.5)
    normed, inv_dev = normalize(windows.astype(jnp.float32))
    scaled = (normed * gain_attn).astype(jnp.bfloat16)
    projected = product("wtc,cd->wtd", scaled, w_qkv).astype(jnp.bfloat16)
    query = projected[..., :chans].reshape(count, length, HEADS, head_size)
    keys_all = projected[..., chans : 2 * chans].reshape(count, length, HEADS, head_size)
    values_all = projected[..., 2 * chans :].reshape(count, length, HEADS, head_size)
    scores = product("wqhd,wkhd->whqk", query, keys_all) * scale_qk
    scores = scores - jnp.max(scores, axis=-1, keepdims=True)
    expons = jnp.exp(scores)
    probs = expons / jnp.sum(expons, axis=-1, keepdims=True)
    probs_b = probs.astype(jnp.bfloat16)
    attended = (
        product("whqk,wkhd->wqhd", probs_b, values_all)
        .astype(jnp.bfloat16)
        .reshape(count, length, chans)
    )
    grad_att = (
        product("wtd,cd->wtc", cot_windows, w_out)
        .astype(jnp.bfloat16)
        .reshape(count, length, HEADS, head_size)
    )
    grad_out = product("wtc,wtd->cd", attended, cot_windows)
    grad_probs = product("wqhd,wkhd->whqk", grad_att, values_all)
    grad_value = product("whqk,wqhd->wkhd", probs_b, grad_att).astype(jnp.bfloat16)
    grad_scores = (
        scale_qk * probs * (grad_probs - jnp.sum(grad_probs * probs, axis=-1, keepdims=True))
    ).astype(jnp.bfloat16)
    grad_query = product("whqk,wkhd->wqhd", grad_scores, keys_all).astype(jnp.bfloat16)
    grad_key = product("whqk,wqhd->wkhd", grad_scores, query).astype(jnp.bfloat16)
    grad_proj = jnp.concatenate(
        [
            grad_query.reshape(count, length, chans),
            grad_key.reshape(count, length, chans),
            grad_value.reshape(count, length, chans),
        ],
        axis=-1,
    )
    grad_qkv = product("wtc,wtd->cd", scaled, grad_proj)
    grad_scaled = product("wtd,cd->wtc", grad_proj, w_qkv)
    grad_gain = jnp.sum(grad_scaled * normed, axis=(0, 1))
    grad_branch = normalize_back(grad_scaled * gain_attn, normed, inv_dev).astype(jnp.bfloat16)
    return (grad_branch, (grad_qkv, grad_out, grad_gain))


def shards(field_in, cotangent, gain_conv, w_expand, w_depth, w_project, gain_attn, w_qkv, w_out):
    rows_dev, cols_dev, chans = field_in.shape
    expand_w = w_expand.shape[1]
    row_devices = lax.axis_size("row")
    col_devices = lax.axis_size("col")
    grad_scale = (rows_dev * cols_dev * row_devices * col_devices) ** (-0.5)
    normed, inv_dev, scaled, pre_act = expand_rows(field_in, gain_conv, w_expand)
    hidden = gelu_value(pre_act).astype(jnp.bfloat16).reshape(rows_dev, cols_dev, expand_w)
    hidden_pad = padded_2(hidden, (("row", 0), ("col", 1)), 1)
    conv = depthwise(hidden_pad, w_depth, rows_dev, cols_dev).reshape(-1, expand_w)
    acted = gelu_value(conv).astype(jnp.bfloat16)
    mid_flat = field_in.reshape(-1, chans).astype(jnp.float32) + jnp.dot(
        acted, w_project, preferred_element_type=jnp.float32
    )
    mid_tile = mid_flat.astype(jnp.bfloat16).reshape(rows_dev, cols_dev, chans)
    devices = row_devices * col_devices
    halves = GRID // col_devices
    span_cols = cols_dev // halves
    per_dev = rows_dev * span_cols // devices
    blocks = span_cols // per_dev
    window_count = per_dev

    def spread_out(tile):
        split = tile.reshape(rows_dev, halves, blocks, per_dev, chans).transpose(0, 2, 1, 3, 4)
        return split.reshape(devices, halves * per_dev, chans)

    moved = lax.all_to_all(
        jnp.concatenate([spread_out(mid_tile), spread_out(cotangent)], axis=1),
        ("row", "col"),
        split_axis=0,
        concat_axis=0,
        tiled=True,
    )
    paired = moved.reshape(devices, 2, halves, per_dev, chans).transpose(1, 3, 0, 2, 4)
    group = 4
    paired = paired.reshape(2, window_count // group, group, GRID * GRID, chans)

    def attend_step(carry, window_pair):
        grad_branch, sums = window_back(window_pair[0], window_pair[1], gain_attn, w_qkv, w_out)
        return (tuple((before + added for before, added in zip(carry, sums))), grad_branch)

    attn_init = (
        jnp.zeros((chans, 3 * chans), jnp.float32),
        jnp.zeros((chans, chans), jnp.float32),
        jnp.zeros((chans,), jnp.float32),
    )
    attn_sums, grad_windows = lax.scan(attend_step, attn_init, (paired[0], paired[1]))
    grad_qkv_part, grad_out_part, grad_gain_part = attn_sums
    arranged = grad_windows.reshape(per_dev, devices, halves, chans).transpose(1, 2, 0, 3)
    returned = lax.all_to_all(
        arranged.reshape(devices, halves * per_dev, chans),
        ("row", "col"),
        split_axis=0,
        concat_axis=0,
        tiled=True,
    )
    grad_tile = (
        returned.reshape(rows_dev, blocks, halves, per_dev, chans)
        .transpose(0, 2, 1, 3, 4)
        .reshape(rows_dev, cols_dev, chans)
    )
    grad_mid = cotangent.reshape(-1, chans).astype(jnp.float32) + grad_tile.reshape(
        -1, chans
    ).astype(jnp.float32)
    grad_mid_b = grad_mid.astype(jnp.bfloat16)
    grad_project = jnp.dot(acted.T, grad_mid_b, preferred_element_type=jnp.float32)
    grad_acted = jnp.dot(grad_mid_b, w_project.T, preferred_element_type=jnp.float32).astype(
        jnp.bfloat16
    )
    grad_conv = (
        (grad_acted.astype(jnp.float32) * gelu_slope(conv))
        .astype(jnp.bfloat16)
        .reshape(rows_dev, cols_dev, expand_w)
    )
    grad_pad = padded_2(grad_conv, (("row", 0), ("col", 1)), 1)
    grad_depth = depth_grad(hidden_pad, grad_conv, rows_dev, cols_dev)
    grad_hidden = spread_back(grad_pad, w_depth, rows_dev, cols_dev).reshape(-1, expand_w)
    grad_pre = (grad_hidden * gelu_slope(pre_act)).astype(jnp.bfloat16)
    grad_expand = jnp.dot(scaled.T, grad_pre, preferred_element_type=jnp.float32)
    grad_scaled = jnp.dot(grad_pre, w_expand.T, preferred_element_type=jnp.float32)
    grad_gain_conv = jnp.sum(grad_scaled * normed, axis=0)
    grad_field = (
        (grad_mid + normalize_back(grad_scaled * gain_conv, normed, inv_dev))
        .astype(jnp.bfloat16)
        .reshape(rows_dev, cols_dev, chans)
    )
    summed = sum_over_field(
        [
            grad_expand,
            grad_project,
            grad_qkv_part,
            grad_out_part,
            grad_depth,
            grad_gain_conv,
            grad_gain_part,
        ],
        devices,
        grad_scale,
    )
    grad_expand, grad_project, grad_qkv, grad_out, grad_depth, grad_gain_conv, grad_gain = summed
    return (
        grad_field,
        grad_gain_conv,
        grad_expand,
        grad_depth,
        grad_project,
        grad_gain,
        grad_qkv,
        grad_out,
    )


def to_tiles(part):
    rows, cols = part.shape
    return part.reshape(rows // 8, 8, cols // 128, 128).transpose(0, 2, 1, 3).reshape(-1, 8, 128)


def from_tiles(tiles, rows, cols):
    split = tiles.reshape(rows // 8, cols // 128, 8, 128)
    return split.transpose(0, 2, 1, 3).reshape(rows, cols)


def sum_over_field(parts, devices, scale):
    small = jnp.concatenate([p.reshape(-1) for p in parts[4:]])
    small_size = small.size
    big = [to_tiles(p) for p in parts[:4]]
    counts = [t.shape[0] for t in big]
    used = sum(counts)
    per_dev = -(-(used * 1024 + small_size) // (1024 * devices))
    spare = (per_dev * devices - used) * 1024
    small = jnp.pad(small, (0, spare - small_size)).reshape(-1, 8, 128)
    packed = jnp.concatenate(big + [small]).reshape(devices, per_dev * 8, 128)
    swapped = lax.all_to_all(packed, ("row", "col"), split_axis=0, concat_axis=0, tiled=True)
    own = (jnp.sum(swapped, axis=0) * scale).astype(jnp.bfloat16)
    spread = jnp.broadcast_to(own, (devices,) + own.shape)
    gathered = lax.all_to_all(spread, ("row", "col"), split_axis=0, concat_axis=0, tiled=True)
    tiles = gathered.reshape(-1, 8, 128).astype(jnp.float32)
    out, at = [], 0
    for part, count in zip(parts[:4], counts):
        out.append(from_tiles(tiles[at : at + count], *part.shape))
        at += count
    flat, at = tiles[used:].reshape(-1), 0
    for part in parts[4:]:
        out.append(flat[at : at + part.size].reshape(part.shape))
        at += part.size
    return out


def solution(mesh):
    in_specs = (P("row", "col", None), P("row", "col", None), P(), P(), P(), P(), P(), P(), P())
    out_specs = (P("row", "col", None), P(), P(), P(), P(), P(), P(), P())
    return jax.shard_map(shards, mesh=mesh, in_specs=in_specs, out_specs=out_specs, check_vma=False)
```

```python
import jax, jax.numpy as jnp
from jax import lax
from jax.experimental import pallas as pl
from jax.experimental.pallas import tpu as pltpu
from jax.sharding import PartitionSpec as P

GRID = 16
HEADS=8
norm_eps=1e-5
f32=jnp.float32; bf16=jnp.bfloat16


def nt(a,b): return lax.dot_general(a,b,(((1,),(1,)),((),())),preferred_element_type=f32)


def nn(a,b): return jnp.dot(a,b,preferred_element_type=f32)


def swap_order(size, inner):
    rows = lax.broadcasted_iota(jnp.int32, (size, size), 0)
    cols = lax.broadcasted_iota(jnp.int32, (size, size), 1)
    outer = size // inner
    return (cols == lax.rem(rows, outer) * inner + lax.div(rows, outer)).astype(f32).astype(bf16)


def attention_body(moved_ref, gain_ref, w_qkv_ref, w_out_ref, branch_ref, gqkv_ref, gout_ref, ggain_ref, mids, cots, outs):
    devices, lines, chans = moved_ref.shape
    windows = mids.shape[0]
    per = lines // 2
    group = 256 // per
    span = 256 // windows
    head = chans // HEADS
    scale = head ** -0.5
    order = swap_order(256, windows)

    def gather(step, carry):
        base = step * group
        at = pl.multiple_of(step * span, span)
        for kind, dest in ((0, mids), (1, cots)):
            block = moved_ref[pl.ds(base, group), kind * per : (kind + 1) * per, :].reshape(256, chans)
            dest[:, pl.ds(at, span), :] = nn(order, block).astype(bf16).reshape(windows, span, chans)
        return carry

    lax.fori_loop(0, devices // group, gather, 0)
    gqkv_ref[...] = jnp.zeros_like(gqkv_ref)
    gout_ref[...] = jnp.zeros_like(gout_ref)
    ggain_ref[...] = jnp.zeros_like(ggain_ref)
    gain = gain_ref[...]
    lane = lax.broadcasted_iota(jnp.int32, (1, chans), 1) // head

    def window(index, carry):
        wide = mids[index].astype(f32)
        cot = cots[index]
        centred = wide - jnp.mean(wide, axis=-1, keepdims=True)
        inv_dev = lax.rsqrt(jnp.mean(centred * centred, axis=-1, keepdims=True) + norm_eps)
        normed = centred * inv_dev
        scaled = (normed * gain).astype(bf16)
        qkv = nn(scaled, w_qkv_ref[...]).astype(bf16)
        query, keys, values = (qkv[:, i * chans : (i + 1) * chans] for i in range(3))
        grad_att = nt(cot, w_out_ref[...]).astype(bf16)
        keys_t = keys.T
        values_t = values.T
        att_t, grad_query_t = [], []
        grad_key = grad_value = None
        for h in range(HEADS):
            mask = (lane == h).astype(f32).astype(bf16)
            query_h = query * mask
            grad_att_h = grad_att * mask
            scores = nt(keys, query_h) * scale
            expons = jnp.exp(scores - jnp.max(scores, axis=0, keepdims=True))
            probs = expons * (1.0 / jnp.sum(expons, axis=0, keepdims=True))
            probs_b = probs.astype(bf16)
            grad_probs = nt(values, grad_att_h)
            row = jnp.sum(grad_probs * probs, axis=0, keepdims=True)
            grad_scores = (scale * probs * (grad_probs - row)).astype(bf16)
            rows = slice(h * head, (h + 1) * head)
            att_t.append(nn(values_t[rows], probs_b))
            grad_query_t.append(nn(keys_t[rows], grad_scores))
            part_key = nn(grad_scores, query_h)
            part_value = nn(probs_b, grad_att_h)
            grad_key = part_key if h == 0 else grad_key + part_key
            grad_value = part_value if h == 0 else grad_value + part_value
        att_t = jnp.concatenate(att_t, axis=0).astype(bf16)
        grad_query = jnp.concatenate(grad_query_t, axis=0).astype(bf16).T
        grad_proj = jnp.concatenate([grad_query, grad_key.astype(bf16), grad_value.astype(bf16)], axis=1)
        gout_ref[...] += nn(att_t, cot)
        gqkv_ref[...] += nn(scaled.T, grad_proj)
        grad_scaled = nt(grad_proj, w_qkv_ref[...])
        ggain_ref[...] += jnp.sum(grad_scaled * normed, axis=0, keepdims=True)
        grad_normed = grad_scaled * gain
        branch = inv_dev * (
            grad_normed
            - jnp.mean(grad_normed, axis=-1, keepdims=True)
            - normed * jnp.mean(grad_normed * normed, axis=-1, keepdims=True)
        )
        outs[index] = branch.astype(bf16)
        return carry

    lax.fori_loop(0, windows, window, 0)
    back = swap_order(256, span)

    def scatter(step, carry):
        at = pl.multiple_of(step * span, span)
        block = outs[:, pl.ds(at, span), :].reshape(256, chans)
        branch_ref[pl.ds(step * group, group)] = nn(back, block).astype(bf16).reshape(group, per, chans)
        return carry

    lax.fori_loop(0, devices // group, scatter, 0)


def attention(moved, gain_attn, w_qkv, w_out):
    devices, lines, chans = moved.shape
    tokens = devices * lines // 2
    windows = tokens // 256
    vmem = pl.BlockSpec(memory_space=pltpu.VMEM)
    return pl.pallas_call(
        attention_body,
        out_shape=(
            jax.ShapeDtypeStruct((devices, lines // 2, chans), bf16),
            jax.ShapeDtypeStruct(w_qkv.shape, f32),
            jax.ShapeDtypeStruct(w_out.shape, f32),
            jax.ShapeDtypeStruct((1, chans), f32),
        ),
        in_specs=[vmem] * 4,
        out_specs=(vmem,) * 4,
        scratch_shapes=[pltpu.VMEM((windows, 256, chans), bf16)] * 3,
        compiler_params=pltpu.CompilerParams(vmem_limit_bytes=48 << 20),
        name="attention",
    )(moved, gain_attn.reshape(1, -1), w_qkv, w_out)


root_half = 0.7071067811865476
inv_root_two_pi = 0.3989422804014327
BLOCK = 256
LANES = 128


def gelu_parts(values):
    half = 0.5 * (1.0 + lax.erf(values * root_half))
    return values * half, half + values * jnp.exp(-0.5 * values * values) * inv_root_two_pi


def unit_norm(values):
    centred = values - jnp.mean(values, axis=-1, keepdims=True)
    inv_dev = lax.rsqrt(jnp.mean(centred * centred, axis=-1, keepdims=True) + norm_eps)
    return centred * inv_dev, inv_dev


def expand_body(x_ref, gain_ref, w_ref, hidden_ref, slope_ref, scaled):
    tokens = x_ref.shape[0]
    chunk = 256

    @pl.when(pl.program_id(0) == 0)
    def _():
        def step(at, carry):
            rows = pl.ds(pl.multiple_of(at * chunk, chunk), chunk)
            normed, _ = unit_norm(x_ref[rows, :].astype(f32))
            scaled[rows, :] = (normed * gain_ref[...]).astype(bf16)
            return carry

        lax.fori_loop(0, tokens // chunk, step, 0)

    def step(at, carry):
        rows = pl.ds(pl.multiple_of(at * chunk, chunk), chunk)
        value, slope = gelu_parts(nn(scaled[rows, :], w_ref[...]))
        hidden_ref[rows, :] = value.astype(bf16)
        slope_ref[rows, :] = slope
        return carry

    lax.fori_loop(0, tokens // chunk, step, 0)


def whole(shape):
    return pl.BlockSpec(shape, lambda i: (0,) * len(shape))


def last(shape):
    return pl.BlockSpec(shape, lambda i: (0,) * (len(shape) - 1) + (i,))


def params(limit=56):
    return pltpu.CompilerParams(dimension_semantics=("arbitrary",), vmem_limit_bytes=limit << 20)


def cost(micros):
    return pl.CostEstimate(flops=micros * 10**9, bytes_accessed=micros * 3 * 10**6, transcendentals=0)


def expand(flat, gain, w_expand):
    tokens, chans = flat.shape
    wide = w_expand.shape[1]
    return pl.pallas_call(
        expand_body,
        grid=(wide // BLOCK,),
        out_shape=(jax.ShapeDtypeStruct((tokens, wide), bf16), jax.ShapeDtypeStruct((tokens, wide), f32)),
        in_specs=[whole((tokens, chans)), whole((1, chans)), last((chans, BLOCK))],
        out_specs=(last((tokens, BLOCK)), last((tokens, BLOCK))),
        scratch_shapes=[pltpu.VMEM((tokens, chans), bf16)],
        compiler_params=params(),
        cost_estimate=cost(13),
        name="expand",
    )(flat, gain, w_expand)


def fill(pad, core_ref, edge_rows, edge_cols):
    tiles, rows, cols, _ = pad.shape
    rows, cols = rows - 2, cols - 16
    for t in range(tiles):
        lanes = slice(t * LANES, (t + 1) * LANES)
        for i in range(rows):
            pad[t, i + 1, 8 : 8 + cols, :] = core_ref[i, :, lanes].astype(f32)
        pad[t, 0, 8 : 8 + cols, :] = edge_rows[0][:, lanes]
        pad[t, rows + 1, 8 : 8 + cols, :] = edge_rows[1][:, lanes]
        for i in range(rows + 2):
            pad[t, i, 7:8, :] = edge_cols[0][i : i + 1, lanes]
            pad[t, i, 8 + cols : 9 + cols, :] = edge_cols[1][i : i + 1, lanes]


def mix_body(hidden_ref, rows_ref, cols_ref, gain_ref, we_ref, wd_ref, wp_ref, x_ref, cot_ref, acted_ref, slope_ref, sent_ref, pad, acc, edge):
    height, width, _ = hidden_ref.shape
    step = pl.program_id(0)
    near = rows_ref.shape[0]
    normed, _ = unit_norm(jnp.concatenate([rows_ref[...], cols_ref[...]]).astype(f32))
    scaled = (normed * gain_ref[...]).astype(bf16)
    value, _ = gelu_parts(nn(scaled, we_ref[...]))
    edge[...] = value.astype(bf16).astype(f32)
    side = cols_ref.shape[0] // 2
    fill(
        pad,
        hidden_ref,
        [edge.at[0:width], edge.at[width : 2 * width]],
        [edge.at[near : near + side], edge.at[near + side : near + 2 * side]],
    )
    for t in range(BLOCK // LANES):
        lanes = slice(t * LANES, (t + 1) * LANES)
        taps = [jnp.broadcast_to(wd_ref[k : k + 1, lanes], (8, LANES)) for k in range(9)]

        def row(i, carry):
            summed = None
            for p in range(3):
                for q in range(3):
                    piece = pad[t, i + p, 7 + q : 7 + q + width, :].reshape(width // 8, 8, LANES)
                    term = piece * taps[3 * p + q]
                    summed = term if summed is None else summed + term
            value, slope = gelu_parts(summed.reshape(width, LANES))
            acted_ref[i, :, lanes] = value.astype(bf16)
            slope_ref[i, :, lanes] = slope
            return carry

        lax.fori_loop(0, height, row, 0)
    chunk = 4

    def project(at, carry):
        rows = pl.ds(at * chunk, chunk)
        flat = acted_ref[rows].reshape(chunk * width, BLOCK)
        part = nn(flat, wp_ref[...]).reshape(chunk, width, -1)

        @pl.when(step == 0)
        def _():
            acc[rows] = x_ref[rows].astype(f32) + part

        @pl.when(step > 0)
        def _():
            acc[rows] += part

        return carry

    lax.fori_loop(0, height // chunk, project, 0)

    @pl.when(step == pl.num_programs(0) - 1)
    def _():
        halves = 2
        blocks = sent_ref.shape[1]
        per = sent_ref.shape[2] // (2 * halves)
        for half in range(halves):
            for b in range(blocks):
                at = (half * blocks + b) * per
                sent_ref[:, b, half * per : (half + 1) * per, :] = acc[:, at : at + per, :].astype(bf16)
                sent_ref[:, b, (halves + half) * per : (halves + half + 1) * per, :] = cot_ref[:, at : at + per, :]


def mix(hidden, edge_rows, edge_cols, gain, w_expand, w_depth, w_project, field_in, cotangent, blocks, per):
    height, width, wide = hidden.shape
    chans = w_project.shape[1]
    side = edge_cols.shape[0]
    lines = 4 * per
    return pl.pallas_call(
        mix_body,
        grid=(wide // BLOCK,),
        out_shape=(
            jax.ShapeDtypeStruct((height, width, wide), bf16),
            jax.ShapeDtypeStruct((height, width, wide), f32),
            jax.ShapeDtypeStruct((height, blocks, lines, chans), bf16),
        ),
        in_specs=[
            last((height, width, BLOCK)),
            whole(edge_rows.shape),
            whole(edge_cols.shape),
            whole((1, chans)),
            last((chans, BLOCK)),
            last((9, BLOCK)),
            pl.BlockSpec((BLOCK, chans), lambda i: (i, 0)),
            whole((height, width, chans)),
            whole((height, width, chans)),
        ],
        out_specs=(last((height, width, BLOCK)), last((height, width, BLOCK)), whole((height, blocks, lines, chans))),
        scratch_shapes=[
            pltpu.VMEM((BLOCK // LANES, height + 2, width + 16, LANES), f32),
            pltpu.VMEM((height, width, chans), f32),
            pltpu.VMEM((edge_rows.shape[0] + side, BLOCK), f32),
        ],
        compiler_params=params(),
        cost_estimate=cost(25),
        name="mix",
    )(hidden, edge_rows, edge_cols, gain, w_expand, w_depth, w_project, field_in, cotangent)


def grad_total(cot_ref, back_ref, half, b):
    per = back_ref.shape[2] // 2
    at = (half * back_ref.shape[1] + b) * per
    cols = slice(at, at + per)
    return cols, cot_ref[:, cols, :].astype(f32) + back_ref[:, b, half * per : (half + 1) * per, :].astype(f32)


def unmix_body(cot_ref, back_ref, slope_ref, acted_ref, wp_ref, gconv_ref, gproj_ref, total):
    height, width, _ = slope_ref.shape

    @pl.when(pl.program_id(0) == 0)
    def _():
        for half in range(2):
            for b in range(back_ref.shape[1]):
                cols, value = grad_total(cot_ref, back_ref, half, b)
                total[:, cols, :] = value.astype(bf16)

    gproj_ref[...] = jnp.zeros_like(gproj_ref)
    chunk = 4

    def step(at, carry):
        rows = pl.ds(at * chunk, chunk)
        flat = total[rows].reshape(chunk * width, -1)
        grad_acted = nt(flat, wp_ref[...]).astype(bf16).astype(f32).reshape(chunk, width, BLOCK)
        gconv_ref[rows] = (grad_acted * slope_ref[rows]).astype(bf16)
        gproj_ref[...] += nn(acted_ref[rows].reshape(chunk * width, BLOCK).T, flat)
        return carry

    lax.fori_loop(0, height // chunk, step, 0)


def unmix(cotangent, returned, slope, acted, w_project):
    height, width, wide = acted.shape
    chans = w_project.shape[1]
    return pl.pallas_call(
        unmix_body,
        grid=(wide // BLOCK,),
        out_shape=(jax.ShapeDtypeStruct((height, width, wide), bf16), jax.ShapeDtypeStruct((wide, chans), f32)),
        in_specs=[
            whole(cotangent.shape),
            whole(returned.shape),
            last((height, width, BLOCK)),
            last((height, width, BLOCK)),
            pl.BlockSpec((BLOCK, chans), lambda i: (i, 0)),
        ],
        out_specs=(last((height, width, BLOCK)), pl.BlockSpec((BLOCK, chans), lambda i: (i, 0))),
        scratch_shapes=[pltpu.VMEM((height, width, chans), bf16)],
        compiler_params=params(),
        cost_estimate=cost(13),
        name="unmix",
    )(cotangent, returned, slope, acted, w_project)


def spread_body(
    gconv_ref, rows_ref, cols_ref, hidden_ref, slope_ref, wd_ref, we_ref, x_ref, gain_ref, cot_ref, back_ref,
    field_ref, gexp_ref, gdepth_ref, ggain_ref, pad, grad_pre, acc, scaled_t, edge,
):
    height, width, _ = gconv_ref.shape
    chans = x_ref.shape[-1]
    step = pl.program_id(0)
    chunk = 4

    @pl.when(step == 0)
    def _():
        def turn(at, carry):
            rows = x_ref[pl.ds(at * chunk, chunk)].reshape(chunk * width, chans).astype(f32)
            normed, _ = unit_norm(rows)
            cols = pl.ds(pl.multiple_of(at * chunk * width, chunk * width), chunk * width)
            scaled_t[:, cols] = (normed * gain_ref[...]).astype(bf16).T
            return carry

        lax.fori_loop(0, height // chunk, turn, 0)

    near, side = rows_ref.shape[0], cols_ref.shape[0] // 2
    edge[0:near] = rows_ref[...].astype(f32)
    edge[near : near + 2 * side] = cols_ref[...].astype(f32)
    fill(
        pad,
        gconv_ref,
        [edge.at[0:width], edge.at[width : 2 * width]],
        [edge.at[near : near + side], edge.at[near + side : near + 2 * side]],
    )
    for t in range(BLOCK // LANES):
        lanes = slice(t * LANES, (t + 1) * LANES)
        taps = [jnp.broadcast_to(wd_ref[k : k + 1, lanes], (8, LANES)) for k in range(9)]

        def row(i, sums):
            summed, out = None, []
            own = hidden_ref[i, :, lanes].astype(f32).reshape(width // 8, 8, LANES)
            for p in range(3):
                for q in range(3):
                    piece = pad[t, i + 2 - p, 9 - q : 9 - q + width, :].reshape(width // 8, 8, LANES)
                    term = piece * taps[3 * p + q]
                    summed = term if summed is None else summed + term
                    out.append(sums[3 * p + q] + jnp.sum(piece * own, axis=0))
            value = summed.reshape(width, LANES) * slope_ref[i, :, lanes]
            grad_pre[i, :, lanes] = value.astype(bf16)
            return tuple(out)

        sums = lax.fori_loop(0, height, row, (jnp.zeros((8, LANES), f32),) * 9)
        for k in range(9):
            gdepth_ref[k : k + 1, lanes] = jnp.sum(sums[k], axis=0, keepdims=True)
    gexp_ref[...] = jnp.zeros_like(gexp_ref)

    def back(at, carry):
        rows = pl.ds(at * chunk, chunk)
        flat = grad_pre[rows].reshape(chunk * width, BLOCK)
        cols = pl.ds(pl.multiple_of(at * chunk * width, chunk * width), chunk * width)
        gexp_ref[...] += nn(scaled_t[:, cols], flat)
        part = nt(flat, we_ref[...]).reshape(chunk, width, chans)

        @pl.when(step == 0)
        def _():
            acc[rows] = part

        @pl.when(step > 0)
        def _():
            acc[rows] += part

        return carry

    lax.fori_loop(0, height // chunk, back, 0)

    @pl.when(step == pl.num_programs(0) - 1)
    def _():
        ggain_ref[...] = jnp.zeros_like(ggain_ref)
        per = back_ref.shape[2] // 2
        for half in range(2):
            for b in range(back_ref.shape[1]):
                cols, total = grad_total(cot_ref, back_ref, half, b)
                grad_scaled = acc[:, cols, :].reshape(height * per, chans)
                normed, inv_dev = unit_norm(x_ref[:, cols, :].astype(f32).reshape(height * per, chans))
                ggain_ref[...] += jnp.sum(grad_scaled * normed, axis=0, keepdims=True)
                grad_normed = grad_scaled * gain_ref[...]
                value = inv_dev * (
                    grad_normed
                    - jnp.mean(grad_normed, axis=-1, keepdims=True)
                    - normed * jnp.mean(grad_normed * normed, axis=-1, keepdims=True)
                )
                field_ref[:, cols, :] = (total + value.reshape(height, per, chans)).astype(bf16)


def spread(gconv, edge_rows, edge_cols, hidden, slope, w_depth, w_expand, field_in, gain, cotangent, returned):
    height, width, wide = gconv.shape
    chans = w_expand.shape[0]
    near, side = edge_rows.shape[0], edge_cols.shape[0]
    return pl.pallas_call(
        spread_body,
        grid=(wide // BLOCK,),
        out_shape=(
            jax.ShapeDtypeStruct((height, width, chans), bf16),
            jax.ShapeDtypeStruct((chans, wide), f32),
            jax.ShapeDtypeStruct((9, wide), f32),
            jax.ShapeDtypeStruct((1, chans), f32),
        ),
        in_specs=[
            last((height, width, BLOCK)),
            last((near, BLOCK)),
            last((side, BLOCK)),
            last((height, width, BLOCK)),
            last((height, width, BLOCK)),
            last((9, BLOCK)),
            last((chans, BLOCK)),
            whole((height, width, chans)),
            whole((1, chans)),
            whole((height, width, chans)),
            whole(returned.shape),
        ],
        out_specs=(whole((height, width, chans)), last((chans, BLOCK)), last((9, BLOCK)), whole((1, chans))),
        scratch_shapes=[
            pltpu.VMEM((BLOCK // LANES, height + 2, width + 16, LANES), f32),
            pltpu.VMEM((height, width, BLOCK), bf16),
            pltpu.VMEM((height, width, chans), f32),
            pltpu.VMEM((chans, height * width), bf16),
            pltpu.VMEM((near + side, BLOCK), f32),
        ],
        compiler_params=params(),
        cost_estimate=cost(30),
        name="spread",
    )(gconv, edge_rows, edge_cols, hidden, slope, w_depth, w_expand, field_in, gain, cotangent, returned)


def outer_cycle(block, width):
    fill = -(-(width + 2) // 8) * 8 - width - 2
    count = lax.axis_size("row")
    forward = [(i, i + 1) for i in range(count - 1)]
    backward = [(b, a) for a, b in forward]
    above = lax.ppermute(block[-1], "row", forward)
    below = lax.ppermute(block[0], "row", backward)
    count = lax.axis_size("col")
    forward = [(i, i + 1) for i in range(count - 1)]
    backward = [(b, a) for a, b in forward]

    def column(at):
        parts = [above[at : at + 1], block[:, at], below[at : at + 1]]
        return jnp.concatenate(parts + [jnp.zeros((fill, block.shape[-1]), block.dtype)])

    left = lax.ppermute(column(block.shape[1] - 1), "col", forward)
    right = lax.ppermute(column(0), "col", backward)
    return jnp.concatenate([above, below]), jnp.concatenate([left, right])


def swap(values):
    return lax.all_to_all(values, ("row", "col"), split_axis=0, concat_axis=0, tiled=True)


def to_tiles(part):
    rows, cols = part.shape
    return part.reshape(rows // 8, 8, cols // 128, 128).transpose(0, 2, 1, 3).reshape(-1, 8, 128)


def from_tiles(tiles, rows, cols):
    split = tiles.reshape(rows // 8, cols // 128, 8, 128)
    return split.transpose(0, 2, 1, 3).reshape(rows, cols)


class Bundle:
    def __init__(self, parts, devices):
        self.shapes = [p.shape for p in parts]
        tiled, flat = [], []
        for part in parts:
            if part.ndim == 2 and part.shape[0] % 8 == 0 and part.shape[1] % 128 == 0:
                tiled.append(to_tiles(part))
            else:
                flat.append(part.reshape(-1))
        self.counts = [t.shape[0] for t in tiled]
        used = sum(self.counts)
        extra = sum(f.size for f in flat)
        self.per = -(-(used * 1024 + extra) // (1024 * devices))
        spare = (self.per * devices - used) * 1024
        if spare:
            flat.append(jnp.zeros((spare - extra,), jnp.float32))
            tiled.append(jnp.concatenate(flat).reshape(-1, 8, 128))
        self.packed = jnp.concatenate(tiled).reshape(devices, self.per * 8, 128)

    def unpack(self, tiles):
        tiles = tiles.reshape(-1, 8, 128).astype(jnp.float32)
        flat = tiles[sum(self.counts) :].reshape(-1)
        out, at, flat_at, counts = [], 0, 0, list(self.counts)
        for shape in self.shapes:
            if len(shape) == 2 and shape[0] % 8 == 0 and shape[1] % 128 == 0:
                count = counts.pop(0)
                out.append(from_tiles(tiles[at : at + count], *shape))
                at += count
            else:
                size = 1
                for dim in shape:
                    size *= dim
                out.append(flat[flat_at : flat_at + size].reshape(shape))
                flat_at += size
        return out


def shards(field_in, cotangent, gain_conv, w_expand, w_depth, w_project, gain_attn, w_qkv, w_out):
    height, width, chans = field_in.shape
    wide = w_expand.shape[1]
    devices = lax.axis_size("row") * lax.axis_size("col")
    grad_scale = (height * width * devices) ** (-0.5)
    per = height * width // (GRID * GRID)
    blocks = devices // height
    gain_in = gain_conv.reshape(1, -1)
    taps = w_depth.reshape(9, wide)
    edge_rows, edge_cols = outer_cycle(field_in, height)
    hidden, slope_pre = expand(field_in.reshape(-1, chans), gain_in, w_expand)
    hidden = hidden.reshape(height, width, wide)
    slope_pre = slope_pre.reshape(height, width, wide)
    acted, slope_conv, sent = mix(
        hidden, edge_rows, edge_cols, gain_in, w_expand, taps, w_project, field_in, cotangent, blocks, per
    )
    moved = swap(sent.reshape(devices, -1, chans))
    branch, grad_qkv, grad_out, grad_gain = attention(moved, gain_attn, w_qkv, w_out)
    returned = swap(branch).reshape(height, blocks, -1, chans)
    grad_conv, grad_project = unmix(cotangent, returned, slope_conv, acted, w_project)
    early = Bundle([grad_project, grad_qkv, grad_out], devices)
    early_all = swap(early.packed)
    early_own = jnp.sum(early_all, axis=0)
    edge_rows, edge_cols = outer_cycle(grad_conv, height)
    grad_field, grad_expand, grad_depth, grad_gain_conv = spread(
        grad_conv, edge_rows, edge_cols, hidden, slope_pre, taps, w_expand, field_in, gain_in, cotangent, returned
    )
    late = Bundle([grad_expand, grad_depth, grad_gain_conv, grad_gain], devices)
    late_packed, early_own = lax.optimization_barrier((late.packed, early_own))
    late_own = jnp.sum(swap(late_packed), axis=0)
    own = (jnp.concatenate([early_own, late_own]) * grad_scale).astype(jnp.bfloat16)
    totals = swap(jnp.broadcast_to(own, (devices,) + own.shape))
    cut = early_own.shape[0]
    grad_project, grad_qkv, grad_out = early.unpack(totals[:, :cut])
    grad_expand, grad_depth, grad_gain_conv, grad_gain = late.unpack(totals[:, cut:])
    return (
        grad_field,
        grad_gain_conv.reshape(-1),
        grad_expand,
        grad_depth.reshape(w_depth.shape),
        grad_project,
        grad_gain.reshape(-1),
        grad_qkv,
        grad_out,
    )


def solution(mesh):
    in_specs = (P("row", "col", None), P("row", "col", None), P(), P(), P(), P(), P(), P(), P())
    out_specs = (P("row", "col", None), P(), P(), P(), P(), P(), P(), P())

    return jax.shard_map(shards, mesh=mesh, in_specs=in_specs, out_specs=out_specs, check_vma=False)
```

```python
import functools
import jax, jax.numpy as jnp
from jax import lax
from jax.experimental import pallas as pl
from jax.experimental.pallas import tpu as pltpu
from jax.sharding import PartitionSpec as P

GRID = 16
HEADS=8
norm_eps=1e-5
f32=jnp.float32; bf16=jnp.bfloat16


def cost(micros):
    return pl.CostEstimate(flops=micros * 10**9, bytes_accessed=micros * 3 * 10**6, transcendentals=0)


def nt(a,b): return lax.dot_general(a,b,(((1,),(1,)),((),())),preferred_element_type=f32)


def nn(a,b): return jnp.dot(a,b,preferred_element_type=f32)


def swap_order(size, inner):
    rows = lax.broadcasted_iota(jnp.int32, (size, size), 0)
    cols = lax.broadcasted_iota(jnp.int32, (size, size), 1)
    outer = size // inner
    return (cols == lax.rem(rows, outer) * inner + lax.div(rows, outer)).astype(f32).astype(bf16)


def attention_body(first, moved_ref, cot_ref, gain_ref, w_qkv_ref, w_out_ref, branch_ref, gqkv_ref, gout_ref, ggain_ref, mids, cots, outs):
    devices, lines, chans = moved_ref.shape
    windows = mids.shape[0]
    per = lines
    group = 256 // per
    span = 256 // windows
    head = chans // HEADS
    scale = head ** -0.5
    order = swap_order(256, windows)

    def gather(step, carry):
        base = step * group
        at = pl.multiple_of(step * span, span)
        for source, low, dest in ((moved_ref, 0, mids), (cot_ref, first, cots)):
            block = source[pl.ds(base, group), low : low + per, :].reshape(256, chans)
            dest[:, pl.ds(at, span), :] = nn(order, block).astype(bf16).reshape(windows, span, chans)
        return carry

    lax.fori_loop(0, devices // group, gather, 0)
    gqkv_ref[...] = jnp.zeros_like(gqkv_ref)
    gout_ref[...] = jnp.zeros_like(gout_ref)
    ggain_ref[...] = jnp.zeros_like(ggain_ref)
    gain = gain_ref[...]
    lane = lax.broadcasted_iota(jnp.int32, (1, chans), 1) // head

    def window(index, carry):
        wide = mids[index].astype(f32)
        cot = cots[index]
        centred = wide - jnp.mean(wide, axis=-1, keepdims=True)
        inv_dev = lax.rsqrt(jnp.mean(centred * centred, axis=-1, keepdims=True) + norm_eps)
        normed = centred * inv_dev
        scaled = (normed * gain).astype(bf16)
        qkv = nn(scaled, w_qkv_ref[...]).astype(bf16)
        query, keys, values = (qkv[:, i * chans : (i + 1) * chans] for i in range(3))
        grad_att = nt(cot, w_out_ref[...]).astype(bf16)
        keys_t = keys.T
        values_t = values.T
        att_t, grad_query_t = [], []
        grad_key = grad_value = None
        for h in range(HEADS):
            mask = (lane == h).astype(f32).astype(bf16)
            query_h = query * mask
            grad_att_h = grad_att * mask
            scores = nt(keys, query_h) * scale
            expons = jnp.exp(scores - jnp.max(scores, axis=0, keepdims=True))
            probs = expons * (1.0 / jnp.sum(expons, axis=0, keepdims=True))
            probs_b = probs.astype(bf16)
            grad_probs = nt(values, grad_att_h)
            row = jnp.sum(grad_probs * probs, axis=0, keepdims=True)
            grad_scores = (scale * probs * (grad_probs - row)).astype(bf16)
            rows = slice(h * head, (h + 1) * head)
            att_t.append(nn(values_t[rows], probs_b))
            grad_query_t.append(nn(keys_t[rows], grad_scores))
            part_key = nn(grad_scores, query_h)
            part_value = nn(probs_b, grad_att_h)
            grad_key = part_key if h == 0 else grad_key + part_key
            grad_value = part_value if h == 0 else grad_value + part_value
        att_t = jnp.concatenate(att_t, axis=0).astype(bf16)
        grad_query = jnp.concatenate(grad_query_t, axis=0).astype(bf16).T
        grad_proj = jnp.concatenate([grad_query, grad_key.astype(bf16), grad_value.astype(bf16)], axis=1)
        gout_ref[...] += nn(att_t, cot)
        gqkv_ref[...] += nn(scaled.T, grad_proj)
        grad_scaled = nt(grad_proj, w_qkv_ref[...])
        ggain_ref[...] += jnp.sum(grad_scaled * normed, axis=0, keepdims=True)
        grad_normed = grad_scaled * gain
        branch = inv_dev * (
            grad_normed
            - jnp.mean(grad_normed, axis=-1, keepdims=True)
            - normed * jnp.mean(grad_normed * normed, axis=-1, keepdims=True)
        )
        outs[index] = branch.astype(bf16)
        return carry

    lax.fori_loop(0, windows, window, 0)
    back = swap_order(256, span)

    def scatter(step, carry):
        at = pl.multiple_of(step * span, span)
        block = outs[:, pl.ds(at, span), :].reshape(256, chans)
        branch_ref[pl.ds(step * group, group)] = nn(back, block).astype(bf16).reshape(group, per, chans)
        return carry

    lax.fori_loop(0, devices // group, scatter, 0)


def attention(moved, cots, first, gain_attn, w_qkv, w_out):
    devices, lines, chans = moved.shape
    tokens = devices * lines
    windows = tokens // 256
    vmem = pl.BlockSpec(memory_space=pltpu.VMEM)
    return pl.pallas_call(
        functools.partial(attention_body, first),
        out_shape=(
            jax.ShapeDtypeStruct((devices, lines, chans), bf16),
            jax.ShapeDtypeStruct(w_qkv.shape, f32),
            jax.ShapeDtypeStruct(w_out.shape, f32),
            jax.ShapeDtypeStruct((1, chans), f32),
        ),
        in_specs=[vmem] * 5,
        out_specs=(vmem,) * 4,
        scratch_shapes=[pltpu.VMEM((windows, 256, chans), bf16)] * 3,
        compiler_params=pltpu.CompilerParams(vmem_limit_bytes=48 << 20),
        cost_estimate=cost(20),
        name="attention",
    )(moved, cots, gain_attn.reshape(1, -1), w_qkv, w_out)


root_half = 0.7071067811865476
inv_root_two_pi = 0.3989422804014327
BLOCK = 256
LANES = 128


def gelu_parts(values):
    half = 0.5 * (1.0 + lax.erf(values * root_half))
    return values * half, half + values * jnp.exp(-0.5 * values * values) * inv_root_two_pi


def unit_norm(values):
    centred = values - jnp.mean(values, axis=-1, keepdims=True)
    inv_dev = lax.rsqrt(jnp.mean(centred * centred, axis=-1, keepdims=True) + norm_eps)
    return centred * inv_dev, inv_dev


def expand_body(x_ref, gain_ref, w_ref, hidden_ref, slope_ref, scaled):
    tokens = x_ref.shape[0]
    chunk = 256

    @pl.when(pl.program_id(0) == 0)
    def _():
        def step(at, carry):
            rows = pl.ds(pl.multiple_of(at * chunk, chunk), chunk)
            normed, _ = unit_norm(x_ref[rows, :].astype(f32))
            scaled[rows, :] = (normed * gain_ref[...]).astype(bf16)
            return carry

        lax.fori_loop(0, tokens // chunk, step, 0)

    def step(at, carry):
        rows = pl.ds(pl.multiple_of(at * chunk, chunk), chunk)
        value, slope = gelu_parts(nn(scaled[rows, :], w_ref[...]))
        hidden_ref[rows, :] = value.astype(bf16)
        slope_ref[rows, :] = slope
        return carry

    lax.fori_loop(0, tokens // chunk, step, 0)


def whole(shape):
    return pl.BlockSpec(shape, lambda i: (0,) * len(shape))


def last(shape):
    return pl.BlockSpec(shape, lambda i: (0,) * (len(shape) - 1) + (i,))


def params(limit=56):
    return pltpu.CompilerParams(dimension_semantics=("arbitrary",), vmem_limit_bytes=limit << 20)


def expand(k, chunks, flat, gain, w_expand):
    tokens, chans = flat.shape
    tokens //= chunks
    wide = w_expand.shape[1]
    return pl.pallas_call(
        expand_body,
        grid=(wide // BLOCK,),
        out_shape=(jax.ShapeDtypeStruct((tokens, wide), bf16), jax.ShapeDtypeStruct((tokens, wide), f32)),
        in_specs=[pl.BlockSpec((tokens, chans), lambda i: (k, 0)), whole((1, chans)), last((chans, BLOCK))],
        out_specs=(last((tokens, BLOCK)), last((tokens, BLOCK))),
        scratch_shapes=[pltpu.VMEM((tokens, chans), bf16)],
        compiler_params=params(),
        cost_estimate=cost(7),
        name="expand",
    )(flat, gain, w_expand)


def fill(pad, cores, above, below, left, right):
    tiles, rows, cols, _ = pad.shape
    cols = cols - 16
    for t in range(tiles):
        lanes = slice(t * LANES, (t + 1) * LANES)
        at = 1
        for core in cores:
            for i in range(core.shape[0]):
                pad[t, at, 8 : 8 + cols, :] = core[i, :, lanes].astype(f32)
                at += 1
        pad[t, 0, 8 : 8 + cols, :] = above[:, lanes].astype(f32)
        pad[t, rows - 1, 8 : 8 + cols, :] = below[:, lanes].astype(f32)
        for i in range(rows):
            pad[t, i, 7:8, :] = left[i : i + 1, lanes]
            pad[t, i, 8 + cols : 9 + cols, :] = right[i : i + 1, lanes]


def regroup(values, per):
    _, cols, _ = values.shape
    half = cols // 2
    blocks = half // per
    return [
        jnp.concatenate([values[:, b * per : (b + 1) * per], values[:, half + b * per : half + (b + 1) * per]], axis=1)
        for b in range(blocks)
    ]


def ungroup(grouped, per):
    blocks = grouped.shape[1]
    wide = [grouped[:, b].astype(f32) for b in range(blocks)]
    return jnp.concatenate([w[:, :per] for w in wide] + [w[:, per:] for w in wide], axis=1)


def arrange_body(per, chunks, cot_ref, out_ref):
    rows = cot_ref.shape[0] // chunks
    for k in range(chunks):
        for b, piece in enumerate(regroup(cot_ref[k * rows : (k + 1) * rows].astype(f32), per)):
            out_ref[:, b, k * 2 * per : (k + 1) * 2 * per, :] = piece.astype(bf16)


def arrange(cotangent, per, chunks):
    rows, cols, chans = cotangent.shape
    vmem = pl.BlockSpec(memory_space=pltpu.VMEM)
    return pl.pallas_call(
        functools.partial(arrange_body, per, chunks),
        out_shape=jax.ShapeDtypeStruct((rows // chunks, cols // (2 * per), chunks * 2 * per, chans), bf16),
        in_specs=[vmem],
        out_specs=vmem,
        compiler_params=pltpu.CompilerParams(vmem_limit_bytes=32 << 20),
        name="arrange",
    )(cotangent)


def mix_body(k, per, hidden_ref, next_ref, edge_ref, gain_ref, we_ref, wd_ref, wp_ref, x_ref, acted_ref, slope_ref, sent_ref, pad, acc, edge):
    height, width, _ = hidden_ref.shape
    step = pl.program_id(0)
    side = (edge_ref.shape[0] - width) // 2
    normed, _ = unit_norm(edge_ref[...].astype(f32))
    scaled = (normed * gain_ref[...]).astype(bf16)
    value, _ = gelu_parts(nn(scaled, we_ref[...]))
    edge[...] = value.astype(bf16).astype(f32)
    outer, inner = edge.at[0:width], next_ref.at[0]
    fill(
        pad,
        [hidden_ref],
        inner if k else outer,
        outer if k else inner,
        edge.at[width : width + side],
        edge.at[width + side : width + 2 * side],
    )
    for t in range(BLOCK // LANES):
        lanes = slice(t * LANES, (t + 1) * LANES)
        taps = [jnp.broadcast_to(wd_ref[k : k + 1, lanes], (8, LANES)) for k in range(9)]

        def row(i, carry):
            summed = None
            for p in range(3):
                for q in range(3):
                    piece = pad[t, i + p, 7 + q : 7 + q + width, :].reshape(width // 8, 8, LANES)
                    term = piece * taps[3 * p + q]
                    summed = term if summed is None else summed + term
            value, slope = gelu_parts(summed.reshape(width, LANES))
            acted_ref[i, :, lanes] = value.astype(bf16)
            slope_ref[i, :, lanes] = slope
            return carry

        lax.fori_loop(0, height, row, 0)
    chunk = 4

    def project(at, carry):
        rows = pl.ds(at * chunk, chunk)
        flat = acted_ref[rows].reshape(chunk * width, BLOCK)
        part = nn(flat, wp_ref[...]).reshape(chunk, width, -1)

        @pl.when(step == 0)
        def _():
            acc[rows] = x_ref[rows].astype(f32) + part

        @pl.when(step > 0)
        def _():
            acc[rows] += part

        return carry

    lax.fori_loop(0, height // chunk, project, 0)

    @pl.when(step == pl.num_programs(0) - 1)
    def _():
        for b, piece in enumerate(regroup(acc[...], per)):
            sent_ref[:, b] = piece.astype(bf16)


def mix(k, hidden, other, edges, gain, w_expand, w_depth, w_project, field_in, per):
    height, width, wide = hidden.shape
    chans = w_project.shape[1]
    near = height - 1 if k else 0
    grouped = (height, width // (2 * per), 2 * per, chans)
    return pl.pallas_call(
        functools.partial(mix_body, k, per),
        grid=(wide // BLOCK,),
        out_shape=(
            jax.ShapeDtypeStruct((height, width, wide), bf16),
            jax.ShapeDtypeStruct((height, width, wide), f32),
            jax.ShapeDtypeStruct(grouped, bf16),
        ),
        in_specs=[
            last((height, width, BLOCK)),
            pl.BlockSpec((1, width, BLOCK), lambda i: (near, 0, i)),
            whole(edges.shape),
            whole((1, chans)),
            last((chans, BLOCK)),
            last((9, BLOCK)),
            pl.BlockSpec((BLOCK, chans), lambda i: (i, 0)),
            pl.BlockSpec((height, width, chans), lambda i: (k, 0, 0)),
        ],
        out_specs=(last((height, width, BLOCK)), last((height, width, BLOCK)), whole(grouped)),
        scratch_shapes=[
            pltpu.VMEM((BLOCK // LANES, height + 2, width + 16, LANES), f32),
            pltpu.VMEM((height, width, chans), f32),
            pltpu.VMEM((edges.shape[0], BLOCK), f32),
        ],
        compiler_params=params(),
        cost_estimate=cost(13),
        name="mix",
    )(hidden, other, edges, gain, w_expand, w_depth, w_project, field_in)


def unmix_body(per, cot_ref, back_ref, slope_ref, wp_ref, gconv_ref, cols_ref, branch_ref, total):
    height, width, _ = slope_ref.shape

    @pl.when(pl.program_id(0) == 0)
    def _():
        branch = ungroup(back_ref[...], per)
        branch_ref[...] = branch.astype(bf16)
        total[...] = (cot_ref[...].astype(f32) + branch).astype(bf16)

    chunk = 4

    def step(at, carry):
        rows = pl.ds(at * chunk, chunk)
        flat = total[rows].reshape(chunk * width, -1)
        grad_acted = nt(flat, wp_ref[...]).astype(bf16).astype(f32).reshape(chunk, width, BLOCK)
        gconv_ref[rows] = (grad_acted * slope_ref[rows]).astype(bf16)
        return carry

    lax.fori_loop(0, height // chunk, step, 0)
    for i in range(height):
        cols_ref[0, i : i + 1, :] = gconv_ref[i, 0:1, :].astype(f32)
        cols_ref[1, i : i + 1, :] = gconv_ref[i, width - 1 : width, :].astype(f32)


def unmix(k, cotangent, returned, slope, w_project, per):
    height, width, wide = slope.shape
    chans = w_project.shape[1]
    return pl.pallas_call(
        functools.partial(unmix_body, per),
        grid=(wide // BLOCK,),
        out_shape=(
            jax.ShapeDtypeStruct((height, width, wide), bf16),
            jax.ShapeDtypeStruct((2, height, wide), f32),
            jax.ShapeDtypeStruct((height, width, chans), bf16),
        ),
        in_specs=[
            pl.BlockSpec((height, width, chans), lambda i: (k, 0, 0)),
            whole(returned.shape),
            last((height, width, BLOCK)),
            pl.BlockSpec((BLOCK, chans), lambda i: (i, 0)),
        ],
        out_specs=(last((height, width, BLOCK)), last((2, height, BLOCK)), whole((height, width, chans))),
        scratch_shapes=[pltpu.VMEM((height, width, chans), bf16)],
        compiler_params=params(),
        cost_estimate=cost(5),
        name="unmix",
    )(cotangent, returned, slope, w_project)


def project_grad_body(cot_ref, *refs):
    chunks = (len(refs) - 2) // 2
    actives, branches, gproj_ref, total = refs[:chunks], refs[chunks : 2 * chunks], refs[-2], refs[-1]
    height, width, chans = branches[0].shape

    @pl.when(pl.program_id(0) == 0)
    def _():
        for k in range(chunks):
            rows = slice(k * height, (k + 1) * height)
            total[rows] = (cot_ref[rows].astype(f32) + branches[k][...].astype(f32)).astype(bf16)

    gproj_ref[...] = jnp.zeros_like(gproj_ref)
    chunk = 4
    for k in range(chunks):

        def step(at, carry):
            flat = total[pl.ds(k * height + at * chunk, chunk)].reshape(chunk * width, chans)
            gproj_ref[...] += nn(actives[k][pl.ds(at * chunk, chunk)].reshape(chunk * width, BLOCK).T, flat)
            return carry

        lax.fori_loop(0, height // chunk, step, 0)


def project_grad(cotangent, actives, branches):
    height, width, wide = actives[0].shape
    chans = cotangent.shape[-1]
    return pl.pallas_call(
        project_grad_body,
        grid=(wide // BLOCK,),
        out_shape=jax.ShapeDtypeStruct((wide, chans), f32),
        in_specs=[whole(cotangent.shape)] + [last((height, width, BLOCK))] * len(actives) + [whole((height, width, chans))] * len(actives),
        out_specs=pl.BlockSpec((BLOCK, chans), lambda i: (i, 0)),
        scratch_shapes=[pltpu.VMEM(cotangent.shape, bf16)],
        compiler_params=params(),
        cost_estimate=cost(6),
        name="project_grad",
    )(cotangent, *actives, *branches)


def spread_body(*refs):
    gconvs, hiddens, slopes, backs = refs[0:2], refs[2:4], refs[4:6], refs[6:8]
    rows_ref, cols_ref, wd_ref, we_ref, x_ref, gain_ref, cot_ref = refs[8:15]
    field_ref, gexp_ref, gdepth_ref, ggain_ref, pad, grad_pre, acc, scaled_t = refs[15:]
    height, width, chans = x_ref.shape
    part = height // 2
    step = pl.program_id(0)
    chunk = 4

    @pl.when(step == 0)
    def _():
        def turn(at, carry):
            rows = x_ref[pl.ds(at * chunk, chunk)].reshape(chunk * width, chans).astype(f32)
            normed, _ = unit_norm(rows)
            cols = pl.ds(pl.multiple_of(at * chunk * width, chunk * width), chunk * width)
            scaled_t[:, cols] = (normed * gain_ref[...]).astype(bf16).T
            return carry

        lax.fori_loop(0, height // chunk, turn, 0)

    fill(pad, gconvs, rows_ref.at[0:width], rows_ref.at[width : 2 * width], cols_ref.at[0], cols_ref.at[1])
    for t in range(BLOCK // LANES):
        lanes = slice(t * LANES, (t + 1) * LANES)
        taps = [jnp.broadcast_to(wd_ref[k : k + 1, lanes], (8, LANES)) for k in range(9)]

        def row(k, j, sums):
            i = j + k * part
            summed, out = None, []
            own = hiddens[k][j, :, lanes].astype(f32).reshape(width // 8, 8, LANES)
            for p in range(3):
                for q in range(3):
                    piece = pad[t, i + 2 - p, 9 - q : 9 - q + width, :].reshape(width // 8, 8, LANES)
                    term = piece * taps[3 * p + q]
                    summed = term if summed is None else summed + term
                    out.append(sums[3 * p + q] + jnp.sum(piece * own, axis=0))
            value = summed.reshape(width, LANES) * slopes[k][j, :, lanes]
            grad_pre[i, :, lanes] = value.astype(bf16)
            return tuple(out)

        sums = (jnp.zeros((8, LANES), f32),) * 9
        for k in range(2):
            sums = lax.fori_loop(0, part, functools.partial(row, k), sums)
        for k in range(9):
            gdepth_ref[k : k + 1, lanes] = jnp.sum(sums[k], axis=0, keepdims=True)
    gexp_ref[...] = jnp.zeros_like(gexp_ref)

    def back(at, carry):
        rows = pl.ds(at * chunk, chunk)
        flat = grad_pre[rows].reshape(chunk * width, BLOCK)
        cols = pl.ds(pl.multiple_of(at * chunk * width, chunk * width), chunk * width)
        gexp_ref[...] += nn(scaled_t[:, cols], flat)
        part = nt(flat, we_ref[...]).reshape(chunk, width, chans)

        @pl.when(step == 0)
        def _():
            acc[rows] = part

        @pl.when(step > 0)
        def _():
            acc[rows] += part

        return carry

    lax.fori_loop(0, height // chunk, back, 0)

    @pl.when(step == pl.num_programs(0) - 1)
    def _():
        ggain_ref[...] = jnp.zeros_like(ggain_ref)
        size = 4

        def finish(k, at, carry):
            here = pl.ds(at * size, size)
            rows = pl.ds(k * part + at * size, size)
            total = cot_ref[rows].astype(f32) + backs[k][here].astype(f32)
            grad_scaled = acc[rows].reshape(size * width, chans)
            normed, inv_dev = unit_norm(x_ref[rows].astype(f32).reshape(size * width, chans))
            ggain_ref[...] += jnp.sum(grad_scaled * normed, axis=0, keepdims=True)
            grad_normed = grad_scaled * gain_ref[...]
            value = inv_dev * (
                grad_normed
                - jnp.mean(grad_normed, axis=-1, keepdims=True)
                - normed * jnp.mean(grad_normed * normed, axis=-1, keepdims=True)
            )
            field_ref[rows] = (total + value.reshape(size, width, chans)).astype(bf16)
            return carry

        for k in range(2):
            lax.fori_loop(0, part // size, functools.partial(finish, k), 0)


def spread(gconvs, hiddens, slopes, branches, edge_rows, edge_cols, w_depth, w_expand, field_in, gain, cotangent):
    height, width, chans = field_in.shape
    wide = w_expand.shape[1]
    part = last((height // 2, width, BLOCK))
    field = whole((height, width, chans))
    return pl.pallas_call(
        spread_body,
        grid=(wide // BLOCK,),
        out_shape=(
            jax.ShapeDtypeStruct((height, width, chans), bf16),
            jax.ShapeDtypeStruct((chans, wide), f32),
            jax.ShapeDtypeStruct((9, wide), f32),
            jax.ShapeDtypeStruct((1, chans), f32),
        ),
        in_specs=[part] * 6
        + [whole((height // 2, width, chans))] * 2
        + [
            last((edge_rows.shape[0], BLOCK)),
            last((2, edge_cols.shape[1], BLOCK)),
            last((9, BLOCK)),
            last((chans, BLOCK)),
            field,
            whole((1, chans)),
            field,
        ],
        out_specs=(field, last((chans, BLOCK)), last((9, BLOCK)), whole((1, chans))),
        scratch_shapes=[
            pltpu.VMEM((BLOCK // LANES, height + 2, width + 16, LANES), f32),
            pltpu.VMEM((height, width, BLOCK), bf16),
            pltpu.VMEM((height, width, chans), f32),
            pltpu.VMEM((chans, height * width), bf16),
        ],
        compiler_params=params(),
        cost_estimate=cost(30),
        name="spread",
    )(*gconvs, *hiddens, *slopes, *branches, edge_rows, edge_cols, w_depth, w_expand, field_in, gain, cotangent)


def outer_cycle(top, bottom, left, right):
    fill = -(-(left.shape[0] + 2) // 8) * 8 - left.shape[0] - 2

    def pairs(axis):
        forward = [(i, i + 1) for i in range(lax.axis_size(axis) - 1)]
        return forward, [(b, a) for a, b in forward]

    forward, backward = pairs("row")
    above = lax.ppermute(bottom, "row", forward)
    below = lax.ppermute(top, "row", backward)
    forward, backward = pairs("col")

    def column(own, at):
        ends = [above[at : at + 1], own, below[at : at + 1]]
        return jnp.concatenate(ends + [jnp.zeros((fill, own.shape[-1]), own.dtype)])

    beside_left = lax.ppermute(column(right, above.shape[0] - 1), "col", forward)
    beside_right = lax.ppermute(column(left, 0), "col", backward)
    return above, below, beside_left, beside_right


def swap(values):
    return lax.all_to_all(values, ("row", "col"), split_axis=0, concat_axis=0, tiled=True)


def to_tiles(part):
    rows, cols = part.shape
    return part.reshape(rows // 8, 8, cols // 128, 128).transpose(0, 2, 1, 3).reshape(-1, 8, 128)


def from_tiles(tiles, rows, cols):
    split = tiles.reshape(rows // 8, cols // 128, 8, 128)
    return split.transpose(0, 2, 1, 3).reshape(rows, cols)


class Bundle:
    def __init__(self, parts, devices):
        self.shapes = [p.shape for p in parts]
        tiled, flat = [], []
        for part in parts:
            if part.ndim == 2 and part.shape[0] % 8 == 0 and part.shape[1] % 128 == 0:
                tiled.append(to_tiles(part))
            else:
                flat.append(part.reshape(-1))
        self.counts = [t.shape[0] for t in tiled]
        used = sum(self.counts)
        extra = sum(f.size for f in flat)
        self.per = -(-(used * 1024 + extra) // (1024 * devices))
        spare = (self.per * devices - used) * 1024
        if spare:
            flat.append(jnp.zeros((spare - extra,), jnp.float32))
            tiled.append(jnp.concatenate(flat).reshape(-1, 8, 128))
        self.packed = jnp.concatenate(tiled).reshape(devices, self.per * 8, 128)

    def unpack(self, tiles):
        tiles = tiles.reshape(-1, 8, 128).astype(jnp.float32)
        flat = tiles[sum(self.counts) :].reshape(-1)
        out, at, flat_at, counts = [], 0, 0, list(self.counts)
        for shape in self.shapes:
            if len(shape) == 2 and shape[0] % 8 == 0 and shape[1] % 128 == 0:
                count = counts.pop(0)
                out.append(from_tiles(tiles[at : at + count], *shape))
                at += count
            else:
                size = 1
                for dim in shape:
                    size *= dim
                out.append(flat[flat_at : flat_at + size].reshape(shape))
                flat_at += size
        return out


def shards(field_in, cotangent, gain_conv, w_expand, w_depth, w_project, gain_attn, w_qkv, w_out):
    height, width, chans = field_in.shape
    wide = w_expand.shape[1]
    devices = lax.axis_size("row") * lax.axis_size("col")
    grad_scale = (height * width * devices) ** (-0.5)
    chunks = 2
    rows = height // chunks
    per = height * width // (GRID * GRID * chunks)
    gain_in = gain_conv.reshape(1, -1)
    taps = w_depth.reshape(9, wide)
    cots = arrange(cotangent, per, chunks)
    cots = swap(cots.reshape(devices, -1, chans))
    above, below, left, right = outer_cycle(field_in[0], field_in[-1], field_in[:, 0], field_in[:, -1])
    hiddens, slopes_pre = [], []
    for k in range(chunks):
        hidden, slope = expand(k, chunks, field_in.reshape(-1, chans), gain_in, w_expand)
        hiddens.append(hidden.reshape(rows, width, wide))
        slopes_pre.append(slope.reshape(rows, width, wide))
    side = left.shape[0] - (chunks - 1) * rows
    actives, slopes, branches, gconvs, gcols = [], [], [], [], []
    moved, sums = [], None
    for k in range(chunks):
        cols = slice(k * rows, k * rows + side)
        edges = jnp.concatenate([below if k else above, left[cols], right[cols]])
        acted, slope, sent = mix(
            k, hiddens[k], hiddens[1 - k], edges, gain_in, w_expand, taps, w_project, field_in, per
        )
        actives.append(acted)
        slopes.append(slope)
        if k == 0:
            sent, cots = lax.optimization_barrier((sent, cots))
        else:
            sent, moved[k - 1] = lax.optimization_barrier((sent, moved[k - 1]))
        moved.append(swap(sent.reshape(devices, -1, chans)))
    for k in range(chunks):
        branch, *parts = attention(moved[k], cots, k * 2 * per, gain_attn, w_qkv, w_out)
        sums = parts if sums is None else [a + b for a, b in zip(sums, parts)]
        if k == 0:
            branch, moved[1] = lax.optimization_barrier((branch, moved[1]))
        else:
            branch, branches[k - 1] = lax.optimization_barrier((branch, branches[k - 1]))
        branches.append(swap(branch).reshape(rows, -1, 2 * per, chans))
    grad_qkv, grad_out, grad_gain = sums
    for k in range(chunks):
        gconv, gcol, branches[k] = unmix(k, cotangent, branches[k], slopes[k], w_project, per)
        gconvs.append(gconv)
        gcols.append(gcol)
    grad_project = project_grad(cotangent, actives, branches)
    gcol = jnp.concatenate(gcols, axis=1).astype(jnp.bfloat16)
    above, below, left, right = outer_cycle(gconvs[0][0], gconvs[-1][-1], gcol[0], gcol[1])
    edge_rows = jnp.concatenate([above, below])
    edge_cols = jnp.stack([left, right]).astype(jnp.float32)
    early = Bundle([grad_project, grad_qkv, grad_out], devices)
    early_all = swap(early.packed)
    early_own = jnp.sum(early_all, axis=0)
    grad_field, grad_expand, grad_depth, grad_gain_conv = spread(
        gconvs, hiddens, slopes_pre, branches, edge_rows, edge_cols, taps, w_expand, field_in, gain_in, cotangent
    )
    late = Bundle([grad_expand, grad_depth, grad_gain_conv, grad_gain], devices)
    late_packed, early_own = lax.optimization_barrier((late.packed, early_own))
    late_own = jnp.sum(swap(late_packed), axis=0)
    own = (jnp.concatenate([early_own, late_own]) * grad_scale).astype(jnp.bfloat16)
    totals = swap(jnp.broadcast_to(own, (devices,) + own.shape))
    cut = early_own.shape[0]
    grad_project, grad_qkv, grad_out = early.unpack(totals[:, :cut])
    grad_expand, grad_depth, grad_gain_conv, grad_gain = late.unpack(totals[:, cut:])
    return (
        grad_field,
        grad_gain_conv.reshape(-1),
        grad_expand,
        grad_depth.reshape(w_depth.shape),
        grad_project,
        grad_gain.reshape(-1),
        grad_qkv,
        grad_out,
    )


def solution(mesh):
    in_specs = (P("row", "col", None), P("row", "col", None), P(), P(), P(), P(), P(), P(), P())
    out_specs = (P("row", "col", None), P(), P(), P(), P(), P(), P(), P())

    return jax.shard_map(shards, mesh=mesh, in_specs=in_specs, out_specs=out_specs, check_vma=False)
```

```python
import functools
import jax, jax.numpy as jnp
from jax import lax
from jax.experimental import pallas as pl
from jax.experimental.pallas import tpu as pltpu
from jax.sharding import PartitionSpec as P

GRID = 16
HEADS=8
norm_eps=1e-5
f32=jnp.float32; bf16=jnp.bfloat16


def cost(micros):
    return pl.CostEstimate(flops=micros * 10**9, bytes_accessed=micros * 3 * 10**6, transcendentals=0)


def nt(a,b): return lax.dot_general(a,b,(((1,),(1,)),((),())),preferred_element_type=f32)


def nn(a,b): return jnp.dot(a,b,preferred_element_type=f32)


def swap_order(size, inner):
    rows = lax.broadcasted_iota(jnp.int32, (size, size), 0)
    cols = lax.broadcasted_iota(jnp.int32, (size, size), 1)
    outer = size // inner
    return (cols == lax.rem(rows, outer) * inner + lax.div(rows, outer)).astype(f32).astype(bf16)


def attention_body(moved_ref, gain_ref, w_qkv_ref, w_out_ref, branch_ref, gqkv_ref, gout_ref, ggain_ref, mids, cots, outs):
    devices, lines, chans = moved_ref.shape
    windows = mids.shape[0]
    per = lines // 2
    group = 256 // per
    span = 256 // windows
    head = chans // HEADS
    scale = head ** -0.5
    order = swap_order(256, windows)

    def gather(step, carry):
        base = step * group
        at = pl.multiple_of(step * span, span)
        for low, dest in ((0, mids), (per, cots)):
            block = moved_ref[pl.ds(base, group), low : low + per, :].reshape(256, chans)
            dest[:, pl.ds(at, span), :] = nn(order, block).astype(bf16).reshape(windows, span, chans)
        return carry

    lax.fori_loop(0, devices // group, gather, 0, unroll=2)
    gqkv_ref[...] = jnp.zeros_like(gqkv_ref)
    gout_ref[...] = jnp.zeros_like(gout_ref)
    ggain_ref[...] = jnp.zeros_like(ggain_ref)
    gain = gain_ref[...]
    lane = lax.broadcasted_iota(jnp.int32, (1, chans), 1) // head

    def window(index, carry):
        wide = mids[index].astype(f32)
        cot = cots[index]
        centred = wide - jnp.mean(wide, axis=-1, keepdims=True)
        inv_dev = lax.rsqrt(jnp.mean(centred * centred, axis=-1, keepdims=True) + norm_eps)
        normed = centred * inv_dev
        scaled = (normed * gain).astype(bf16)
        qkv = nn(scaled, w_qkv_ref[...]).astype(bf16)
        query, keys, values = (qkv[:, i * chans : (i + 1) * chans] for i in range(3))
        grad_att = nt(cot, w_out_ref[...]).astype(bf16)
        keys_t = keys.T
        values_t = values.T
        att_t, grad_query_t = [], []
        grad_key = grad_value = None
        for h in range(HEADS):
            mask = (lane == h).astype(f32).astype(bf16)
            query_h = query * mask
            grad_att_h = grad_att * mask
            scores = nt(keys, query_h) * scale
            expons = jnp.exp(scores - jnp.max(scores, axis=0, keepdims=True))
            probs = expons * (1.0 / jnp.sum(expons, axis=0, keepdims=True))
            probs_b = probs.astype(bf16)
            grad_probs = nt(values, grad_att_h)
            row = jnp.sum(grad_probs * probs, axis=0, keepdims=True)
            grad_scores = (scale * probs * (grad_probs - row)).astype(bf16)
            rows = slice(h * head, (h + 1) * head)
            att_t.append(nn(values_t[rows], probs_b))
            grad_query_t.append(nn(keys_t[rows], grad_scores))
            part_key = nn(grad_scores, query_h)
            part_value = nn(probs_b, grad_att_h)
            grad_key = part_key if h == 0 else grad_key + part_key
            grad_value = part_value if h == 0 else grad_value + part_value
        att_t = jnp.concatenate(att_t, axis=0).astype(bf16)
        grad_query = jnp.concatenate(grad_query_t, axis=0).astype(bf16).T
        grad_proj = jnp.concatenate([grad_query, grad_key.astype(bf16), grad_value.astype(bf16)], axis=1)
        gout_ref[...] += nn(att_t, cot)
        gqkv_ref[...] += nn(scaled.T, grad_proj)
        grad_scaled = nt(grad_proj, w_qkv_ref[...])
        ggain_ref[...] += jnp.sum(grad_scaled * normed, axis=0, keepdims=True)
        grad_normed = grad_scaled * gain
        branch = inv_dev * (
            grad_normed
            - jnp.mean(grad_normed, axis=-1, keepdims=True)
            - normed * jnp.mean(grad_normed * normed, axis=-1, keepdims=True)
        )
        outs[index] = branch.astype(bf16)
        return carry

    lax.fori_loop(0, windows, window, 0, unroll=2)
    back = swap_order(256, span)

    def scatter(step, carry):
        at = pl.multiple_of(step * span, span)
        block = outs[:, pl.ds(at, span), :].reshape(256, chans)
        branch_ref[pl.ds(step * group, group)] = nn(back, block).astype(bf16).reshape(group, per, chans)
        return carry

    lax.fori_loop(0, devices // group, scatter, 0, unroll=2)


def attention(moved, gain_attn, w_qkv, w_out):
    devices, lines, chans = moved.shape
    tokens = devices * lines // 2
    windows = tokens // 256
    vmem = pl.BlockSpec(memory_space=pltpu.VMEM)
    return pl.pallas_call(
        attention_body,
        out_shape=(
            jax.ShapeDtypeStruct((devices, lines // 2, chans), bf16),
            jax.ShapeDtypeStruct(w_qkv.shape, f32),
            jax.ShapeDtypeStruct(w_out.shape, f32),
            jax.ShapeDtypeStruct((1, chans), f32),
        ),
        in_specs=[vmem] * 4,
        out_specs=(vmem,) * 4,
        scratch_shapes=[pltpu.VMEM((windows, 256, chans), bf16)] * 3,
        compiler_params=pltpu.CompilerParams(vmem_limit_bytes=48 << 20),
        cost_estimate=cost(20),
        name="attention",
    )(moved, gain_attn.reshape(1, -1), w_qkv, w_out)


root_half = 0.7071067811865476
inv_root_two_pi = 0.3989422804014327
BLOCK = 256
LANES = 128


def gelu_parts(values):
    half = 0.5 * (1.0 + lax.erf(values * root_half))
    return values * half, half + values * jnp.exp(-0.5 * values * values) * inv_root_two_pi


def unit_norm(values):
    centred = values - jnp.mean(values, axis=-1, keepdims=True)
    inv_dev = lax.rsqrt(jnp.mean(centred * centred, axis=-1, keepdims=True) + norm_eps)
    return centred * inv_dev, inv_dev


def expand_body(x_ref, gain_ref, w_ref, hidden_ref, slope_ref, scaled):
    tokens = x_ref.shape[0]
    chunk = 256

    @pl.when(pl.program_id(0) == 0)
    def _():
        def step(at, carry):
            rows = pl.ds(pl.multiple_of(at * chunk, chunk), chunk)
            normed, _ = unit_norm(x_ref[rows, :].astype(f32))
            scaled[rows, :] = (normed * gain_ref[...]).astype(bf16)
            return carry

        lax.fori_loop(0, tokens // chunk, step, 0, unroll=2)

    def step(at, carry):
        rows = pl.ds(pl.multiple_of(at * chunk, chunk), chunk)
        value, slope = gelu_parts(nn(scaled[rows, :], w_ref[...]))
        hidden_ref[rows, :] = value.astype(bf16)
        slope_ref[rows, :] = slope
        return carry

    lax.fori_loop(0, tokens // chunk, step, 0, unroll=4)


def whole(shape):
    return pl.BlockSpec(shape, lambda i: (0,) * len(shape))


def last(shape):
    return pl.BlockSpec(shape, lambda i: (0,) * (len(shape) - 1) + (i,))


def params(limit=56):
    return pltpu.CompilerParams(dimension_semantics=("arbitrary",), vmem_limit_bytes=limit << 20)


def expand(k, chunks, flat, gain, w_expand):
    tokens, chans = flat.shape
    tokens //= chunks
    wide = w_expand.shape[1]
    return pl.pallas_call(
        expand_body,
        grid=(wide // BLOCK,),
        out_shape=(jax.ShapeDtypeStruct((tokens, wide), bf16), jax.ShapeDtypeStruct((tokens, wide), f32)),
        in_specs=[pl.BlockSpec((tokens, chans), lambda i: (k, 0)), whole((1, chans)), last((chans, BLOCK))],
        out_specs=(last((tokens, BLOCK)), last((tokens, BLOCK))),
        scratch_shapes=[pltpu.VMEM((tokens, chans), bf16)],
        compiler_params=params(),
        cost_estimate=cost(7),
        name="expand",
    )(flat, gain, w_expand)


def fill(pad, cores, above, below, left, right):
    tiles, rows, cols, _ = pad.shape
    cols = cols - 16
    for t in range(tiles):
        lanes = slice(t * LANES, (t + 1) * LANES)
        at = 1
        for core in cores:
            for i in range(core.shape[0]):
                pad[t, at, 8 : 8 + cols, :] = core[i, :, lanes].astype(f32)
                at += 1
        pad[t, 0, 8 : 8 + cols, :] = above[:, lanes].astype(f32)
        pad[t, rows - 1, 8 : 8 + cols, :] = below[:, lanes].astype(f32)
        for i in range(rows):
            pad[t, i, 7:8, :] = left[i : i + 1, lanes]
            pad[t, i, 8 + cols : 9 + cols, :] = right[i : i + 1, lanes]


def regroup(values, per):
    _, cols, _ = values.shape
    half = cols // 2
    blocks = half // per
    return [
        jnp.concatenate([values[:, b * per : (b + 1) * per], values[:, half + b * per : half + (b + 1) * per]], axis=1)
        for b in range(blocks)
    ]


def ungroup(grouped, per):
    blocks = grouped.shape[1]
    wide = [grouped[:, b].astype(f32) for b in range(blocks)]
    return jnp.concatenate([w[:, :per] for w in wide] + [w[:, per:] for w in wide], axis=1)


def mix_body(k, per, hidden_ref, next_ref, edge_ref, gain_ref, we_ref, wd_ref, wp_ref, x_ref, cot_ref, acted_ref, slope_ref, sent_ref, pad, acc, edge):
    height, width, _ = hidden_ref.shape
    step = pl.program_id(0)
    side = (edge_ref.shape[0] - width) // 2
    normed, _ = unit_norm(edge_ref[...].astype(f32))
    scaled = (normed * gain_ref[...]).astype(bf16)
    value, _ = gelu_parts(nn(scaled, we_ref[...]))
    edge[...] = value.astype(bf16).astype(f32)
    outer, inner = edge.at[0:width], next_ref.at[0]
    fill(
        pad,
        [hidden_ref],
        inner if k else outer,
        outer if k else inner,
        edge.at[width : width + side],
        edge.at[width + side : width + 2 * side],
    )
    for t in range(BLOCK // LANES):
        lanes = slice(t * LANES, (t + 1) * LANES)
        taps = [jnp.broadcast_to(wd_ref[k : k + 1, lanes], (8, LANES)) for k in range(9)]

        def row(i, carry):
            summed = None
            for p in range(3):
                for q in range(3):
                    piece = pad[t, i + p, 7 + q : 7 + q + width, :].reshape(width // 8, 8, LANES)
                    term = piece * taps[3 * p + q]
                    summed = term if summed is None else summed + term
            value, slope = gelu_parts(summed.reshape(width, LANES))
            acted_ref[i, :, lanes] = value.astype(bf16)
            slope_ref[i, :, lanes] = slope
            return carry

        lax.fori_loop(0, height, row, 0, unroll=4)
    part = nn(acted_ref[...].reshape(height * width, BLOCK), wp_ref[...]).reshape(height, width, -1)

    @pl.when(step == 0)
    def _():
        acc[...] = x_ref[...].astype(f32) + part

    @pl.when(step > 0)
    def _():
        acc[...] += part

    @pl.when(step == pl.num_programs(0) - 1)
    def _():
        for kind, values in enumerate((acc[...], cot_ref[...].astype(f32))):
            for b, piece in enumerate(regroup(values, per)):
                sent_ref[:, b, kind * 2 * per : (kind + 1) * 2 * per, :] = piece.astype(bf16)


def mix(k, hidden, other, edges, gain, w_expand, w_depth, w_project, field_in, cotangent, per):
    height, width, wide = hidden.shape
    chans = w_project.shape[1]
    near = height - 1 if k else 0
    grouped = (height, width // (2 * per), 4 * per, chans)
    return pl.pallas_call(
        functools.partial(mix_body, k, per),
        grid=(wide // BLOCK,),
        out_shape=(
            jax.ShapeDtypeStruct((height, width, wide), bf16),
            jax.ShapeDtypeStruct((height, width, wide), f32),
            jax.ShapeDtypeStruct(grouped, bf16),
        ),
        in_specs=[
            last((height, width, BLOCK)),
            pl.BlockSpec((1, width, BLOCK), lambda i: (near, 0, i)),
            whole(edges.shape),
            whole((1, chans)),
            last((chans, BLOCK)),
            last((9, BLOCK)),
            pl.BlockSpec((BLOCK, chans), lambda i: (i, 0)),
            pl.BlockSpec((height, width, chans), lambda i: (k, 0, 0)),
            pl.BlockSpec((height, width, chans), lambda i: (k, 0, 0)),
        ],
        out_specs=(last((height, width, BLOCK)), last((height, width, BLOCK)), whole(grouped)),
        scratch_shapes=[
            pltpu.VMEM((BLOCK // LANES, height + 2, width + 16, LANES), f32),
            pltpu.VMEM((height, width, chans), f32),
            pltpu.VMEM((edges.shape[0], BLOCK), f32),
        ],
        compiler_params=params(),
        cost_estimate=cost(13),
        name="mix",
    )(hidden, other, edges, gain, w_expand, w_depth, w_project, field_in, cotangent)


def unmix_body(per, cot_ref, back_ref, slope_ref, wp_ref, gconv_ref, cols_ref, branch_ref, total):
    height, width, _ = slope_ref.shape

    @pl.when(pl.program_id(0) == 0)
    def _():
        branch = ungroup(back_ref[...], per)
        branch_ref[...] = branch.astype(bf16)
        total[...] = (cot_ref[...].astype(f32) + branch).astype(bf16)

    flat = total[...].reshape(height * width, -1)
    grad_acted = nt(flat, wp_ref[...]).astype(bf16).astype(f32).reshape(height, width, BLOCK)
    gconv_ref[...] = (grad_acted * slope_ref[...]).astype(bf16)
    for i in range(height):
        cols_ref[0, i : i + 1, :] = gconv_ref[i, 0:1, :].astype(f32)
        cols_ref[1, i : i + 1, :] = gconv_ref[i, width - 1 : width, :].astype(f32)


def unmix(k, cotangent, returned, slope, w_project, per):
    height, width, wide = slope.shape
    chans = w_project.shape[1]
    return pl.pallas_call(
        functools.partial(unmix_body, per),
        grid=(wide // BLOCK,),
        out_shape=(
            jax.ShapeDtypeStruct((height, width, wide), bf16),
            jax.ShapeDtypeStruct((2, height, wide), f32),
            jax.ShapeDtypeStruct((height, width, chans), bf16),
        ),
        in_specs=[
            pl.BlockSpec((height, width, chans), lambda i: (k, 0, 0)),
            whole(returned.shape),
            last((height, width, BLOCK)),
            pl.BlockSpec((BLOCK, chans), lambda i: (i, 0)),
        ],
        out_specs=(last((height, width, BLOCK)), last((2, height, BLOCK)), whole((height, width, chans))),
        scratch_shapes=[pltpu.VMEM((height, width, chans), bf16)],
        compiler_params=params(),
        cost_estimate=cost(5),
        name="unmix",
    )(cotangent, returned, slope, w_project)


def project_grad_body(chunks, cot_ref, *refs):
    actives, branches = refs[:chunks], refs[chunks : 2 * chunks]
    qkvs, outs, packed_ref, total_t = refs[2 * chunks : 3 * chunks], refs[3 * chunks : 4 * chunks], refs[-2], refs[-1]
    height, width, chans = branches[0].shape
    size = height * width

    @pl.when(pl.program_id(0) == 0)
    def _():
        for k in range(chunks):
            total = cot_ref[k * height : (k + 1) * height].astype(f32) + branches[k][...].astype(f32)
            total_t[:, k * size : (k + 1) * size] = total.astype(bf16).reshape(size, chans).T

    part = None
    for k in range(chunks):
        term = nn(total_t[:, k * size : (k + 1) * size], actives[k][...].reshape(size, BLOCK))
        part = term if part is None else part + term
    grad_project = part.T
    tiles = packed_ref.shape[0]
    for side in range(2):
        tile = grad_project[:, side * LANES : (side + 1) * LANES].reshape(tiles, packed_ref.shape[1], 8, LANES)
        packed_ref[:, :, 8 * side : 8 * side + 8, :] = tile
    attn = [sum(r[...] for r in qkvs), sum(r[...] for r in outs)]
    both = jnp.concatenate(attn, axis=1)
    for j in range(packed_ref.shape[1]):
        for side in range(2):
            at = (2 * j + side) * LANES
            tile = both[:, at : at + LANES].reshape(tiles, 8, LANES)
            packed_ref[:, j, 16 + 8 * side : 24 + 8 * side, :] = tile


def project_grad(cotangent, actives, branches, qkvs, outs):
    height, width, wide = actives[0].shape
    chans = cotangent.shape[-1]
    steps = wide // BLOCK
    tiles = wide // 8 // 4 // steps
    rows = chans // steps
    return pl.pallas_call(
        functools.partial(project_grad_body, len(actives)),
        grid=(steps,),
        out_shape=jax.ShapeDtypeStruct((tiles * steps, 4, 32, LANES), f32),
        in_specs=[whole(cotangent.shape)]
        + [last((height, width, BLOCK))] * len(actives)
        + [whole((height, width, chans))] * len(actives)
        + [pl.BlockSpec((rows, q.shape[1]), lambda i: (i, 0)) for q in (*qkvs, *outs)],
        out_specs=pl.BlockSpec((tiles, 4, 32, LANES), lambda i: (i, 0, 0, 0)),
        scratch_shapes=[pltpu.VMEM((chans, cotangent.shape[0] * width), bf16)],
        compiler_params=params(),
        cost_estimate=cost(6),
        name="project_grad",
    )(cotangent, *actives, *branches, *qkvs, *outs)


def spread_body(*refs):
    gconvs, hiddens, slopes, backs = refs[0:2], refs[2:4], refs[4:6], refs[6:8]
    rows_ref, cols_ref, wd_ref, we_ref, x_ref, gain_ref, cot_ref = refs[8:15]
    attn_gain_ref, field_ref, packed_ref, pad, grad_pre, acc, scaled_t, ggain_ref = refs[15:]
    height, width, chans = x_ref.shape
    part = height // 2
    step = pl.program_id(0)
    chunk = 4

    @pl.when(step == 0)
    def _():
        def turn(at, carry):
            rows = x_ref[pl.ds(at * chunk, chunk)].reshape(chunk * width, chans).astype(f32)
            normed, _ = unit_norm(rows)
            cols = pl.ds(pl.multiple_of(at * chunk * width, chunk * width), chunk * width)
            scaled_t[:, cols] = (normed * gain_ref[...]).astype(bf16).T
            return carry

        lax.fori_loop(0, height // chunk, turn, 0, unroll=2)

    fill(pad, gconvs, rows_ref.at[0:width], rows_ref.at[width : 2 * width], cols_ref.at[0], cols_ref.at[1])
    packed_ref[:, 0, 16:24, :] = jnp.zeros((packed_ref.shape[0], 8, LANES), f32)
    for t in range(BLOCK // LANES):
        lanes = slice(t * LANES, (t + 1) * LANES)
        taps = [jnp.broadcast_to(wd_ref[k : k + 1, lanes], (8, LANES)) for k in range(9)]

        def row(k, j, sums):
            i = j + k * part
            summed, out = None, []
            own = hiddens[k][j, :, lanes].astype(f32).reshape(width // 8, 8, LANES)
            for p in range(3):
                for q in range(3):
                    piece = pad[t, i + 2 - p, 9 - q : 9 - q + width, :].reshape(width // 8, 8, LANES)
                    term = piece * taps[3 * p + q]
                    summed = term if summed is None else summed + term
                    out.append(sums[3 * p + q] + jnp.sum(piece * own, axis=0))
            value = summed.reshape(width, LANES) * slopes[k][j, :, lanes]
            grad_pre[i, :, lanes] = value.astype(bf16)
            return tuple(out)

        sums = (jnp.zeros((8, LANES), f32),) * 9
        for k in range(2):
            sums = lax.fori_loop(0, part, functools.partial(row, k), sums, unroll=2)
        for k in range(9):
            packed_ref[2 * k + t, 0, 16:17, :] = jnp.sum(sums[k], axis=0, keepdims=True)
    flat = grad_pre[...].reshape(height * width, BLOCK)
    grad_expand = nn(scaled_t[...], flat)
    for t in range(BLOCK // LANES):
        tile = grad_expand[:, t * LANES : (t + 1) * LANES].reshape(-1, 8, LANES)
        packed_ref[:, 0, 8 * t : 8 * t + 8, :] = tile
    back = nt(flat, we_ref[...]).reshape(height, width, chans)

    @pl.when(step == 0)
    def _():
        acc[...] = back

    @pl.when(step > 0)
    def _():
        acc[...] += back

    @pl.when(step == pl.num_programs(0) - 1)
    def _():
        ggain_ref[...] = jnp.zeros_like(ggain_ref)
        size = 4

        def finish(k, at, carry):
            here = pl.ds(at * size, size)
            rows = pl.ds(k * part + at * size, size)
            total = cot_ref[rows].astype(f32) + backs[k][here].astype(f32)
            grad_scaled = acc[rows].reshape(size * width, chans)
            normed, inv_dev = unit_norm(x_ref[rows].astype(f32).reshape(size * width, chans))
            ggain_ref[...] += jnp.sum(grad_scaled * normed, axis=0, keepdims=True)
            grad_normed = grad_scaled * gain_ref[...]
            value = inv_dev * (
                grad_normed
                - jnp.mean(grad_normed, axis=-1, keepdims=True)
                - normed * jnp.mean(grad_normed * normed, axis=-1, keepdims=True)
            )
            field_ref[rows] = (total + value.reshape(size, width, chans)).astype(bf16)
            return carry

        for k in range(2):
            lax.fori_loop(0, part // size, functools.partial(finish, k), 0, unroll=2)
        for t in range(2):
            lanes = slice(t * LANES, (t + 1) * LANES)
            packed_ref[18 + t, 0, 16:17, :] = ggain_ref[:, lanes]
            packed_ref[20 + t, 0, 16:17, :] = attn_gain_ref[:, lanes]


def spread(gconvs, hiddens, slopes, branches, edge_rows, edge_cols, w_depth, w_expand, field_in, gain, cotangent, attn_gain):
    height, width, chans = field_in.shape
    wide = w_expand.shape[1]
    part = last((height // 2, width, BLOCK))
    field = whole((height, width, chans))
    return pl.pallas_call(
        spread_body,
        grid=(wide // BLOCK,),
        out_shape=(
            jax.ShapeDtypeStruct((height, width, chans), bf16),
            jax.ShapeDtypeStruct((chans // 8, wide // BLOCK, 24, LANES), f32),
        ),
        in_specs=[part] * 6
        + [whole((height // 2, width, chans))] * 2
        + [
            last((edge_rows.shape[0], BLOCK)),
            last((2, edge_cols.shape[1], BLOCK)),
            last((9, BLOCK)),
            last((chans, BLOCK)),
            field,
            whole((1, chans)),
            field,
            whole((1, chans)),
        ],
        out_specs=(field, pl.BlockSpec((chans // 8, 1, 24, LANES), lambda i: (0, i, 0, 0))),
        scratch_shapes=[
            pltpu.VMEM((BLOCK // LANES, height + 2, width + 16, LANES), f32),
            pltpu.VMEM((height, width, BLOCK), bf16),
            pltpu.VMEM((height, width, chans), f32),
            pltpu.VMEM((chans, height * width), bf16),
            pltpu.VMEM((1, chans), f32),
        ],
        compiler_params=params(),
        cost_estimate=cost(30),
        name="spread",
    )(*gconvs, *hiddens, *slopes, *branches, edge_rows, edge_cols, w_depth, w_expand, field_in, gain, cotangent, attn_gain)


def unpack_body(totals_ref, expand_ref, project_ref, qkv_ref, out_ref, depth_ref, gain_ref, attn_gain_ref):
    blocks = totals_ref.shape[1]
    small = totals_ref[:, :, 48:56, :].astype(f32)
    for side in range(2):
        here = slice(8 * side, 8 * side + 8)
        tile = totals_ref[:, :, here, :].astype(f32)
        project_ref[:, side * LANES : (side + 1) * LANES] = tile.reshape(-1, LANES)
        for j in range(blocks):
            lanes = slice((2 * j + side) * LANES, (2 * j + side + 1) * LANES)
            tile = totals_ref[:, j, 32 + 8 * side : 40 + 8 * side, :].astype(f32)
            expand_ref[:, lanes] = tile.reshape(-1, LANES)
            tile = totals_ref[:, j, 16 + 8 * side : 24 + 8 * side, :].astype(f32).reshape(-1, LANES)
            if j < blocks - 1:
                qkv_ref[:, lanes] = tile
            else:
                out_ref[:, side * LANES : (side + 1) * LANES] = tile
            for k in range(9):
                depth_ref[k : k + 1, lanes] = small[2 * k + side, j, 0:1, :]
        lanes = slice(side * LANES, (side + 1) * LANES)
        gain_ref[:, lanes] = small[18 + side, blocks - 1, 0:1, :]
        attn_gain_ref[:, lanes] = small[20 + side, blocks - 1, 0:1, :]


def unpack(totals, wide, chans):
    vmem = pl.BlockSpec(memory_space=pltpu.VMEM)
    shapes = [(chans, wide), (wide, chans), (chans, 3 * chans), (chans, chans), (9, wide), (1, chans), (1, chans)]
    return pl.pallas_call(
        unpack_body,
        out_shape=tuple(jax.ShapeDtypeStruct(shape, f32) for shape in shapes),
        in_specs=[vmem],
        out_specs=(vmem,) * len(shapes),
        compiler_params=pltpu.CompilerParams(vmem_limit_bytes=32 << 20),
        name="unpack",
    )(totals)


def outer_cycle(top, bottom, left, right):
    fill = -(-(left.shape[0] + 2) // 8) * 8 - left.shape[0] - 2

    def pairs(axis):
        forward = [(i, i + 1) for i in range(lax.axis_size(axis) - 1)]
        return forward, [(b, a) for a, b in forward]

    forward, backward = pairs("row")
    above = lax.ppermute(bottom, "row", forward)
    below = lax.ppermute(top, "row", backward)
    forward, backward = pairs("col")

    def column(own, at):
        ends = [above[at : at + 1], own, below[at : at + 1]]
        return jnp.concatenate(ends + [jnp.zeros((fill, own.shape[-1]), own.dtype)])

    beside_left = lax.ppermute(column(right, above.shape[0] - 1), "col", forward)
    beside_right = lax.ppermute(column(left, 0), "col", backward)
    return above, below, beside_left, beside_right


def swap(values):
    return lax.all_to_all(values, ("row", "col"), split_axis=0, concat_axis=0, tiled=True)


def shards(field_in, cotangent, gain_conv, w_expand, w_depth, w_project, gain_attn, w_qkv, w_out):
    height, width, chans = field_in.shape
    wide = w_expand.shape[1]
    devices = lax.axis_size("row") * lax.axis_size("col")
    grad_scale = (height * width * devices) ** (-0.5)
    chunks = 2
    rows = height // chunks
    per = height * width // (GRID * GRID * chunks)
    gain_in = gain_conv.reshape(1, -1)
    taps = w_depth.reshape(9, wide)
    above, below, left, right = outer_cycle(field_in[0], field_in[-1], field_in[:, 0], field_in[:, -1])
    hiddens, slopes_pre = [], []
    for k in range(chunks):
        hidden, slope = expand(k, chunks, field_in.reshape(-1, chans), gain_in, w_expand)
        hiddens.append(hidden.reshape(rows, width, wide))
        slopes_pre.append(slope.reshape(rows, width, wide))
    side = left.shape[0] - (chunks - 1) * rows
    actives, slopes, branches, gconvs, gcols = [], [], [], [], []
    moved, qkvs, outs, gains = [], [], [], []
    for k in range(chunks):
        cols = slice(k * rows, k * rows + side)
        edges = jnp.concatenate([below if k else above, left[cols], right[cols]])
        acted, slope, sent = mix(
            k, hiddens[k], hiddens[1 - k], edges, gain_in, w_expand, taps, w_project, field_in, cotangent, per
        )
        actives.append(acted)
        slopes.append(slope)
        if k > 0:
            sent, moved[k - 1] = lax.optimization_barrier((sent, moved[k - 1]))
        moved.append(swap(sent.reshape(devices, -1, chans)))
    for k in range(chunks):
        branch, qkv, out, gain = attention(moved[k], gain_attn, w_qkv, w_out)
        qkvs.append(qkv)
        outs.append(out)
        gains.append(gain)
        if k == 0:
            branch, moved[1] = lax.optimization_barrier((branch, moved[1]))
        else:
            branch, branches[k - 1] = lax.optimization_barrier((branch, branches[k - 1]))
        branches.append(swap(branch).reshape(rows, -1, 2 * per, chans))
    for k in range(chunks):
        gconv, gcol, branches[k] = unmix(k, cotangent, branches[k], slopes[k], w_project, per)
        gconvs.append(gconv)
        gcols.append(gcol)
    early = project_grad(cotangent, actives, branches, qkvs, outs)
    gcol = jnp.concatenate(gcols, axis=1).astype(jnp.bfloat16)
    above, below, left, right = outer_cycle(gconvs[0][0], gconvs[-1][-1], gcol[0], gcol[1])
    edge_rows = jnp.concatenate([above, below])
    edge_cols = jnp.stack([left, right]).astype(jnp.float32)
    early_all = swap(early.reshape(devices, -1, LANES))
    early_own = jnp.sum(early_all, axis=0)
    grad_field, late = spread(
        gconvs, hiddens, slopes_pre, branches, edge_rows, edge_cols, taps, w_expand, field_in, gain_in,
        cotangent, sum(gains),
    )
    late, early_own = lax.optimization_barrier((late, early_own))
    late_own = jnp.sum(swap(late.reshape(devices, -1, LANES)), axis=0)
    own = (jnp.concatenate([early_own, late_own]) * grad_scale).astype(jnp.bfloat16)
    totals = swap(jnp.broadcast_to(own, (devices,) + own.shape))
    totals = totals.reshape(chans // 8, wide // BLOCK, -1, LANES)
    grad_expand, grad_project, grad_qkv, grad_out, grad_depth, grad_gain_conv, grad_gain = unpack(totals, wide, chans)
    return (
        grad_field,
        grad_gain_conv.reshape(-1),
        grad_expand,
        grad_depth.reshape(w_depth.shape),
        grad_project,
        grad_gain.reshape(-1),
        grad_qkv,
        grad_out,
    )


def solution(mesh):
    in_specs = (P("row", "col", None), P("row", "col", None), P(), P(), P(), P(), P(), P(), P())
    out_specs = (P("row", "col", None), P(), P(), P(), P(), P(), P(), P())

    return jax.shard_map(shards, mesh=mesh, in_specs=in_specs, out_specs=out_specs, check_vma=False)
```

```python
import functools
import jax, jax.numpy as jnp
from jax import lax
from jax.experimental import pallas as pl
from jax.experimental.pallas import tpu as pltpu
from jax.sharding import PartitionSpec as P

GRID = 16
LOG2_E = 1.4426950408889634
HEADS=8
norm_eps=1e-5
f32=jnp.float32; bf16=jnp.bfloat16


def cost(micros):
    return pl.CostEstimate(flops=micros * 10**9, bytes_accessed=micros * 3 * 10**6, transcendentals=0)


def nt(a,b): return lax.dot_general(a,b,(((1,),(1,)),((),())),preferred_element_type=f32)


def nn(a,b): return jnp.dot(a,b,preferred_element_type=f32)


def swap_order(size, inner):
    rows = lax.broadcasted_iota(jnp.int32, (size, size), 0)
    cols = lax.broadcasted_iota(jnp.int32, (size, size), 1)
    outer = size // inner
    return (cols == lax.rem(rows, outer) * inner + lax.div(rows, outer)).astype(f32).astype(bf16)


def attention_body(moved_ref, gain_ref, w_qkv_ref, w_out_ref, branch_ref, gqkv_ref, gout_ref, ggain_ref, mids, cots, outs):
    devices, lines, chans = moved_ref.shape
    windows = mids.shape[0]
    per = lines // 2
    group = 256 // per
    span = 256 // windows
    head = chans // HEADS
    scale = head ** -0.5
    order = swap_order(256, windows)

    def gather(step, carry):
        base = step * group
        at = pl.multiple_of(step * span, span)
        for low, dest in ((0, mids), (per, cots)):
            block = moved_ref[pl.ds(base, group), low : low + per, :].reshape(256, chans)
            dest[:, pl.ds(at, span), :] = nn(order, block).astype(bf16).reshape(windows, span, chans)
        return carry

    lax.fori_loop(0, devices // group, gather, 0, unroll=2)
    gqkv_ref[...] = jnp.zeros_like(gqkv_ref)
    gout_ref[...] = jnp.zeros_like(gout_ref)
    ggain_ref[...] = jnp.zeros_like(ggain_ref)
    gain = gain_ref[...]
    lane = lax.broadcasted_iota(jnp.int32, (1, chans), 1) // head

    def window(index, carry):
        wide = mids[index].astype(f32)
        cot = cots[index]
        centred = wide - jnp.mean(wide, axis=-1, keepdims=True)
        inv_dev = lax.rsqrt(jnp.mean(centred * centred, axis=-1, keepdims=True) + norm_eps)
        normed = centred * inv_dev
        scaled = (normed * gain).astype(bf16)
        qkv = nn(scaled, w_qkv_ref[...]).astype(bf16)
        query, keys, values = (qkv[:, i * chans : (i + 1) * chans] for i in range(3))
        grad_att = nt(cot, w_out_ref[...]).astype(bf16)
        keys_t = keys.T
        values_t = values.T
        att_t, grad_query_t = [], []
        grads = [None, None]
        masks = [(lane == h).astype(f32).astype(bf16) for h in range(HEADS)]

        def first(h):
            query_h, grad_att_h = query * masks[h], grad_att * masks[h]
            return query_h, grad_att_h, nt(keys, query_h), nt(values, grad_att_h)

        def second(query_h, grad_att_h, scores, grad_probs):
            top = jnp.max(scores, axis=0, keepdims=True)
            expons = jnp.exp2((scores - top) * (scale * LOG2_E))
            probs = expons * (1.0 / jnp.sum(expons, axis=0, keepdims=True))
            row = jnp.sum(grad_probs * probs, axis=0, keepdims=True)
            grad_scores = (scale * probs * (grad_probs - row)).astype(bf16)
            return query_h, grad_att_h, probs.astype(bf16), grad_scores

        def third(h, query_h, grad_att_h, probs_b, grad_scores):
            rows = slice(h * head, (h + 1) * head)
            att_t.append(nn(values_t[rows], probs_b))
            grad_query_t.append(nn(keys_t[rows], grad_scores))
            parts = nn(grad_scores, query_h), nn(probs_b, grad_att_h)
            for i in range(2):
                grads[i] = parts[i] if h == 0 else grads[i] + parts[i]

        ahead = first(0)
        behind = None
        for h in range(HEADS):
            now = ahead
            if h + 1 < HEADS:
                ahead = first(h + 1)
            made = second(*now)
            if behind is not None:
                third(h - 1, *behind)
            behind = made
        third(HEADS - 1, *behind)

        grad_key, grad_value = grads
        att_t = jnp.concatenate(att_t, axis=0).astype(bf16)
        grad_query = jnp.concatenate(grad_query_t, axis=0).astype(bf16).T
        grad_proj = jnp.concatenate([grad_query, grad_key.astype(bf16), grad_value.astype(bf16)], axis=1)
        gout_ref[...] += nn(att_t, cot)
        gqkv_ref[...] += nn(scaled.T, grad_proj)
        grad_scaled = nt(grad_proj, w_qkv_ref[...])
        ggain_ref[...] += jnp.sum(grad_scaled * normed, axis=0, keepdims=True)
        grad_normed = grad_scaled * gain
        branch = inv_dev * (
            grad_normed
            - jnp.mean(grad_normed, axis=-1, keepdims=True)
            - normed * jnp.mean(grad_normed * normed, axis=-1, keepdims=True)
        )
        outs[index] = branch.astype(bf16)
        return carry

    lax.fori_loop(0, windows, window, 0, unroll=2)
    back = swap_order(256, span)

    def scatter(step, carry):
        at = pl.multiple_of(step * span, span)
        block = outs[:, pl.ds(at, span), :].reshape(256, chans)
        branch_ref[pl.ds(step * group, group)] = nn(back, block).astype(bf16).reshape(group, per, chans)
        return carry

    lax.fori_loop(0, devices // group, scatter, 0, unroll=2)


def attention(moved, gain_attn, w_qkv, w_out):
    devices, lines, chans = moved.shape
    tokens = devices * lines // 2
    windows = tokens // 256
    vmem = pl.BlockSpec(memory_space=pltpu.VMEM)
    return pl.pallas_call(
        attention_body,
        out_shape=(
            jax.ShapeDtypeStruct((devices, lines // 2, chans), bf16),
            jax.ShapeDtypeStruct(w_qkv.shape, f32),
            jax.ShapeDtypeStruct(w_out.shape, f32),
            jax.ShapeDtypeStruct((1, chans), f32),
        ),
        in_specs=[vmem] * 4,
        out_specs=(vmem,) * 4,
        scratch_shapes=[pltpu.VMEM((windows, 256, chans), bf16)] * 3,
        compiler_params=pltpu.CompilerParams(vmem_limit_bytes=48 << 20),
        cost_estimate=cost(20),
        name="attention",
    )(moved, gain_attn.reshape(1, -1), w_qkv, w_out)


root_half = 0.7071067811865476
inv_root_two_pi = 0.3989422804014327
BLOCK = 256
LANES = 128


def gelu_value(values):
    return 0.5 * values * (1.0 + lax.erf(values * root_half))


def gelu_slope(values):
    gauss = jnp.exp2(values * values * (-0.5 * LOG2_E))
    return 0.5 * (1.0 + lax.erf(values * root_half)) + values * gauss * inv_root_two_pi


def unit_norm(values):
    centred = values - jnp.mean(values, axis=-1, keepdims=True)
    inv_dev = lax.rsqrt(jnp.mean(centred * centred, axis=-1, keepdims=True) + norm_eps)
    return centred * inv_dev, inv_dev


def expand_body(x_ref, gain_ref, w_ref, hidden_ref, pre_ref, scaled):
    tokens = x_ref.shape[0]
    chunk = 256

    @pl.when(pl.program_id(0) == 0)
    def _():
        def step(at, carry):
            rows = pl.ds(pl.multiple_of(at * chunk, chunk), chunk)
            normed, _ = unit_norm(x_ref[rows, :].astype(f32))
            scaled[rows, :] = (normed * gain_ref[...]).astype(bf16)
            return carry

        lax.fori_loop(0, tokens // chunk, step, 0, unroll=2)

    def step(at, carry):
        rows = pl.ds(pl.multiple_of(at * chunk, chunk), chunk)
        pre_act = nn(scaled[rows, :], w_ref[...])
        hidden_ref[rows, :] = gelu_value(pre_act).astype(bf16)
        pre_ref[rows, :] = pre_act
        return carry

    lax.fori_loop(0, tokens // chunk, step, 0, unroll=4)


def whole(shape):
    return pl.BlockSpec(shape, lambda i: (0,) * len(shape))


def last(shape):
    return pl.BlockSpec(shape, lambda i: (0,) * (len(shape) - 1) + (i,))


def params(limit=56):
    return pltpu.CompilerParams(dimension_semantics=("arbitrary",), vmem_limit_bytes=limit << 20)


def expand(k, chunks, flat, gain, w_expand):
    tokens, chans = flat.shape
    tokens //= chunks
    wide = w_expand.shape[1]
    return pl.pallas_call(
        expand_body,
        grid=(wide // BLOCK,),
        out_shape=(jax.ShapeDtypeStruct((tokens, wide), bf16), jax.ShapeDtypeStruct((tokens, wide), f32)),
        in_specs=[pl.BlockSpec((tokens, chans), lambda i: (k, 0)), whole((1, chans)), last((chans, BLOCK))],
        out_specs=(last((tokens, BLOCK)), last((tokens, BLOCK))),
        scratch_shapes=[pltpu.VMEM((tokens, chans), bf16)],
        compiler_params=params(),
        cost_estimate=cost(7),
        name="expand",
    )(flat, gain, w_expand)


def fill(pad, cores, above, below, left, right):
    tiles, rows, cols, _ = pad.shape
    cols = cols - 16
    for t in range(tiles):
        lanes = slice(t * LANES, (t + 1) * LANES)
        at = 1
        for core in cores:
            for i in range(core.shape[0]):
                pad[t, at, 8 : 8 + cols, :] = core[i, :, lanes].astype(f32)
                at += 1
        pad[t, 0, 8 : 8 + cols, :] = above[:, lanes].astype(f32)
        pad[t, rows - 1, 8 : 8 + cols, :] = below[:, lanes].astype(f32)
        for i in range(rows):
            pad[t, i, 7:8, :] = left[i : i + 1, lanes]
            pad[t, i, 8 + cols : 9 + cols, :] = right[i : i + 1, lanes]


def regroup(values, per):
    _, cols, _ = values.shape
    half = cols // 2
    blocks = half // per
    return [
        jnp.concatenate([values[:, b * per : (b + 1) * per], values[:, half + b * per : half + (b + 1) * per]], axis=1)
        for b in range(blocks)
    ]


def ungroup(grouped, per):
    blocks = grouped.shape[1]
    wide = [grouped[:, b].astype(f32) for b in range(blocks)]
    return jnp.concatenate([w[:, :per] for w in wide] + [w[:, per:] for w in wide], axis=1)


def mix_body(per, hidden_ref, edge_ref, gain_ref, we_ref, wd_ref, wp_ref, x_ref, cot_ref, acted_ref, conv_ref, sent_ref, pad, acc, edge):
    height, width, _ = hidden_ref.shape
    step = pl.program_id(0)
    side = edge_ref.shape[0] // 2 - width
    normed, _ = unit_norm(edge_ref[...].astype(f32))
    scaled = (normed * gain_ref[...]).astype(bf16)
    edge[...] = gelu_value(nn(scaled, we_ref[...])).astype(bf16).astype(f32)
    low = 2 * width
    fill(
        pad,
        [hidden_ref],
        edge.at[0:width],
        edge.at[width:low],
        edge.at[low : low + side],
        edge.at[low + side : low + 2 * side],
    )
    for t in range(BLOCK // LANES):
        lanes = slice(t * LANES, (t + 1) * LANES)
        taps = [jnp.broadcast_to(wd_ref[k : k + 1, lanes], (8, LANES)) for k in range(9)]

        def row(i, carry):
            summed = None
            for p in range(3):
                for q in range(3):
                    piece = pad[t, i + p, 7 + q : 7 + q + width, :].reshape(width // 8, 8, LANES)
                    term = piece * taps[3 * p + q]
                    summed = term if summed is None else summed + term
            summed = summed.reshape(width, LANES)
            acted_ref[i, :, lanes] = gelu_value(summed).astype(bf16)
            conv_ref[i, :, lanes] = summed
            return carry

        lax.fori_loop(0, height, row, 0, unroll=4)
    part = nn(acted_ref[...].reshape(height * width, BLOCK), wp_ref[...]).reshape(height, width, -1)

    @pl.when(step == 0)
    def _():
        acc[...] = x_ref[...].astype(f32) + part

    @pl.when(step > 0)
    def _():
        acc[...] += part

    @pl.when(step == pl.num_programs(0) - 1)
    def _():
        for kind, values in enumerate((acc[...], cot_ref[...].astype(f32))):
            for b, piece in enumerate(regroup(values, per)):
                sent_ref[:, b, kind * 2 * per : (kind + 1) * 2 * per, :] = piece.astype(bf16)


def mix(k, hidden, edges, gain, w_expand, w_depth, w_project, field_in, cotangent, per):
    height, width, wide = hidden.shape
    chans = w_project.shape[1]
    grouped = (height, width // (2 * per), 4 * per, chans)
    return pl.pallas_call(
        functools.partial(mix_body, per),
        grid=(wide // BLOCK,),
        out_shape=(
            jax.ShapeDtypeStruct((height, width, wide), bf16),
            jax.ShapeDtypeStruct((height, width, wide), f32),
            jax.ShapeDtypeStruct(grouped, bf16),
        ),
        in_specs=[
            last((height, width, BLOCK)),
            whole(edges.shape),
            whole((1, chans)),
            last((chans, BLOCK)),
            last((9, BLOCK)),
            pl.BlockSpec((BLOCK, chans), lambda i: (i, 0)),
            pl.BlockSpec((height, width, chans), lambda i: (k, 0, 0)),
            pl.BlockSpec((height, width, chans), lambda i: (k, 0, 0)),
        ],
        out_specs=(last((height, width, BLOCK)), last((height, width, BLOCK)), whole(grouped)),
        scratch_shapes=[
            pltpu.VMEM((BLOCK // LANES, height + 2, width + 16, LANES), f32),
            pltpu.VMEM((height, width, chans), f32),
            pltpu.VMEM((edges.shape[0], BLOCK), f32),
        ],
        compiler_params=params(),
        cost_estimate=cost(13),
        name="mix",
    )(hidden, edges, gain, w_expand, w_depth, w_project, field_in, cotangent)


def unmix_body(per, cot_ref, back_ref, conv_ref, wp_ref, gconv_ref, cols_ref, branch_ref, total):
    height, width, _ = conv_ref.shape

    @pl.when(pl.program_id(0) == 0)
    def _():
        branch = ungroup(back_ref[...], per)
        branch_ref[...] = branch.astype(bf16)
        total[...] = (cot_ref[...].astype(f32) + branch).astype(bf16)

    flat = total[...].reshape(height * width, -1)
    grad_acted = nt(flat, wp_ref[...]).astype(bf16).astype(f32).reshape(height, width, BLOCK)
    gconv_ref[...] = (grad_acted * gelu_slope(conv_ref[...])).astype(bf16)
    for i in range(height):
        cols_ref[0, i : i + 1, :] = gconv_ref[i, 0:1, :].astype(f32)
        cols_ref[1, i : i + 1, :] = gconv_ref[i, width - 1 : width, :].astype(f32)


def unmix(k, cotangent, returned, conv, w_project, per):
    height, width, wide = conv.shape
    chans = w_project.shape[1]
    return pl.pallas_call(
        functools.partial(unmix_body, per),
        grid=(wide // BLOCK,),
        out_shape=(
            jax.ShapeDtypeStruct((height, width, wide), bf16),
            jax.ShapeDtypeStruct((2, height, wide), f32),
            jax.ShapeDtypeStruct((height, width, chans), bf16),
        ),
        in_specs=[
            pl.BlockSpec((height, width, chans), lambda i: (k, 0, 0)),
            whole(returned.shape),
            last((height, width, BLOCK)),
            pl.BlockSpec((BLOCK, chans), lambda i: (i, 0)),
        ],
        out_specs=(last((height, width, BLOCK)), last((2, height, BLOCK)), whole((height, width, chans))),
        scratch_shapes=[pltpu.VMEM((height, width, chans), bf16)],
        compiler_params=params(),
        cost_estimate=cost(5),
        name="unmix",
    )(cotangent, returned, conv, w_project)


def project_part_body(cot_ref, branch_ref, acted_ref, *refs):
    before, (part_ref, total_t) = refs[:-2], refs[-2:]
    height, width, chans = branch_ref.shape
    size = height * width

    @pl.when(pl.program_id(0) == 0)
    def _():
        total = cot_ref[...].astype(f32) + branch_ref[...].astype(f32)
        total_t[...] = total.astype(bf16).reshape(size, chans).T

    part = nn(total_t[...], acted_ref[...].reshape(size, BLOCK))
    for ref in before[:1]:
        part = part + ref[...]
    if not before:
        part_ref[...] = part
        return
    grad_project = part.T
    qkvs, outs = before[1:3], before[3:5]
    tiles, blocks = part_ref.shape[0], part_ref.shape[1]
    both = jnp.concatenate([sum(r[...] for r in qkvs), sum(r[...] for r in outs)], axis=1)
    for side in range(2):
        tile = grad_project[:, side * LANES : (side + 1) * LANES].reshape(tiles, blocks, 8, LANES)
        part_ref[:, :, 8 * side : 8 * side + 8, :] = tile
        for j in range(blocks):
            at = (2 * j + side) * LANES
            part_ref[:, j, 16 + 8 * side : 24 + 8 * side, :] = both[:, at : at + LANES].reshape(tiles, 8, LANES)


def project_part(k, cotangent, branch, acted, before=None, qkvs=(), outs=()):
    height, width, wide = acted.shape
    chans = cotangent.shape[-1]
    steps = wide // BLOCK
    tiles = wide // 8 // 4 // steps
    rows = chans // steps
    if before is None:
        extra, extra_specs = [], []
        out_shape, out_spec = (chans, wide), last((chans, BLOCK))
    else:
        extra = [before, *qkvs, *outs]
        extra_specs = [last((chans, BLOCK))]
        extra_specs += [pl.BlockSpec((rows, q.shape[1]), lambda i: (i, 0)) for q in extra[1:]]
        out_shape = (tiles * steps, 4, 32, LANES)
        out_spec = pl.BlockSpec((tiles, 4, 32, LANES), lambda i: (i, 0, 0, 0))
    return pl.pallas_call(
        project_part_body,
        grid=(steps,),
        out_shape=jax.ShapeDtypeStruct(out_shape, f32),
        in_specs=[
            pl.BlockSpec((height, width, chans), lambda i: (k, 0, 0)),
            whole((height, width, chans)),
            last((height, width, BLOCK)),
        ]
        + extra_specs,
        out_specs=out_spec,
        scratch_shapes=[pltpu.VMEM((chans, height * width), bf16)],
        compiler_params=params(),
        cost_estimate=cost(4),
        name="project_part",
    )(cotangent, branch, acted, *extra)


def spread_body(*refs):
    gconvs, hiddens, pres, backs = refs[0:2], refs[2:4], refs[4:6], refs[6:8]
    rows_ref, cols_ref, wd_ref, we_ref, x_ref, gain_ref, cot_ref = refs[8:15]
    attn_gain_ref, field_ref, packed_ref, pad, grad_pre, acc, scaled_t, ggain_ref = refs[15:]
    height, width, chans = x_ref.shape
    part = height // 2
    step = pl.program_id(0)
    chunk = 4

    @pl.when(step == 0)
    def _():
        def turn(at, carry):
            rows = x_ref[pl.ds(at * chunk, chunk)].reshape(chunk * width, chans).astype(f32)
            normed, _ = unit_norm(rows)
            cols = pl.ds(pl.multiple_of(at * chunk * width, chunk * width), chunk * width)
            scaled_t[:, cols] = (normed * gain_ref[...]).astype(bf16).T
            return carry

        lax.fori_loop(0, height // chunk, turn, 0, unroll=2)

    fill(pad, gconvs, rows_ref.at[0:width], rows_ref.at[width : 2 * width], cols_ref.at[0], cols_ref.at[1])
    packed_ref[:, 0, 16:24, :] = jnp.zeros((packed_ref.shape[0], 8, LANES), f32)
    for t in range(BLOCK // LANES):
        lanes = slice(t * LANES, (t + 1) * LANES)
        taps = [jnp.broadcast_to(wd_ref[k : k + 1, lanes], (8, LANES)) for k in range(9)]

        def row(k, j, sums):
            i = j + k * part
            summed, out = None, []
            own = hiddens[k][j, :, lanes].astype(f32).reshape(width // 8, 8, LANES)
            for p in range(3):
                for q in range(3):
                    piece = pad[t, i + 2 - p, 9 - q : 9 - q + width, :].reshape(width // 8, 8, LANES)
                    term = piece * taps[3 * p + q]
                    summed = term if summed is None else summed + term
                    out.append(sums[3 * p + q] + jnp.sum(piece * own, axis=0))
            value = summed.reshape(width, LANES) * gelu_slope(pres[k][j, :, lanes])
            grad_pre[i, :, lanes] = value.astype(bf16)
            return tuple(out)

        sums = (jnp.zeros((8, LANES), f32),) * 9
        for k in range(2):
            sums = lax.fori_loop(0, part, functools.partial(row, k), sums, unroll=2)
        for k in range(9):
            packed_ref[2 * k + t, 0, 16:17, :] = jnp.sum(sums[k], axis=0, keepdims=True)
    flat = grad_pre[...].reshape(height * width, BLOCK)
    grad_expand = nn(scaled_t[...], flat)
    for t in range(BLOCK // LANES):
        tile = grad_expand[:, t * LANES : (t + 1) * LANES].reshape(-1, 8, LANES)
        packed_ref[:, 0, 8 * t : 8 * t + 8, :] = tile
    back = nt(flat, we_ref[...]).reshape(height, width, chans)

    @pl.when(step == 0)
    def _():
        acc[...] = back

    @pl.when(step > 0)
    def _():
        acc[...] += back

    @pl.when(step == pl.num_programs(0) - 1)
    def _():
        ggain_ref[...] = jnp.zeros_like(ggain_ref)
        size = 4

        def finish(k, at, carry):
            here = pl.ds(at * size, size)
            rows = pl.ds(k * part + at * size, size)
            total = cot_ref[rows].astype(f32) + backs[k][here].astype(f32)
            grad_scaled = acc[rows].reshape(size * width, chans)
            normed, inv_dev = unit_norm(x_ref[rows].astype(f32).reshape(size * width, chans))
            ggain_ref[...] += jnp.sum(grad_scaled * normed, axis=0, keepdims=True)
            grad_normed = grad_scaled * gain_ref[...]
            value = inv_dev * (
                grad_normed
                - jnp.mean(grad_normed, axis=-1, keepdims=True)
                - normed * jnp.mean(grad_normed * normed, axis=-1, keepdims=True)
            )
            field_ref[rows] = (total + value.reshape(size, width, chans)).astype(bf16)
            return carry

        for k in range(2):
            lax.fori_loop(0, part // size, functools.partial(finish, k), 0, unroll=2)
        for t in range(2):
            lanes = slice(t * LANES, (t + 1) * LANES)
            packed_ref[18 + t, 0, 16:17, :] = ggain_ref[:, lanes]
            packed_ref[20 + t, 0, 16:17, :] = attn_gain_ref[:, lanes]


def spread(gconvs, hiddens, pres, branches, edge_rows, edge_cols, w_depth, w_expand, field_in, gain, cotangent, attn_gain):
    height, width, chans = field_in.shape
    wide = w_expand.shape[1]
    part = last((height // 2, width, BLOCK))
    field = whole((height, width, chans))
    return pl.pallas_call(
        spread_body,
        grid=(wide // BLOCK,),
        out_shape=(
            jax.ShapeDtypeStruct((height, width, chans), bf16),
            jax.ShapeDtypeStruct((chans // 8, wide // BLOCK, 24, LANES), f32),
        ),
        in_specs=[part] * 6
        + [whole((height // 2, width, chans))] * 2
        + [
            last((edge_rows.shape[0], BLOCK)),
            last((2, edge_cols.shape[1], BLOCK)),
            last((9, BLOCK)),
            last((chans, BLOCK)),
            field,
            whole((1, chans)),
            field,
            whole((1, chans)),
        ],
        out_specs=(field, pl.BlockSpec((chans // 8, 1, 24, LANES), lambda i: (0, i, 0, 0))),
        scratch_shapes=[
            pltpu.VMEM((BLOCK // LANES, height + 2, width + 16, LANES), f32),
            pltpu.VMEM((height, width, BLOCK), bf16),
            pltpu.VMEM((height, width, chans), f32),
            pltpu.VMEM((chans, height * width), bf16),
            pltpu.VMEM((1, chans), f32),
        ],
        compiler_params=params(),
        cost_estimate=cost(30),
        name="spread",
    )(*gconvs, *hiddens, *pres, *branches, edge_rows, edge_cols, w_depth, w_expand, field_in, gain, cotangent, attn_gain)


def unpack_body(totals_ref, expand_ref, project_ref, qkv_ref, out_ref, depth_ref, gain_ref, attn_gain_ref):
    blocks = totals_ref.shape[1]
    small = totals_ref[:, :, 48:56, :].astype(f32)
    for side in range(2):
        here = slice(8 * side, 8 * side + 8)
        tile = totals_ref[:, :, here, :].astype(f32)
        project_ref[:, side * LANES : (side + 1) * LANES] = tile.reshape(-1, LANES)
        for j in range(blocks):
            lanes = slice((2 * j + side) * LANES, (2 * j + side + 1) * LANES)
            tile = totals_ref[:, j, 32 + 8 * side : 40 + 8 * side, :].astype(f32)
            expand_ref[:, lanes] = tile.reshape(-1, LANES)
            tile = totals_ref[:, j, 16 + 8 * side : 24 + 8 * side, :].astype(f32).reshape(-1, LANES)
            if j < blocks - 1:
                qkv_ref[:, lanes] = tile
            else:
                out_ref[:, side * LANES : (side + 1) * LANES] = tile
            for k in range(9):
                depth_ref[k : k + 1, lanes] = small[2 * k + side, j, 0:1, :]
        lanes = slice(side * LANES, (side + 1) * LANES)
        gain_ref[:, lanes] = small[18 + side, blocks - 1, 0:1, :]
        attn_gain_ref[:, lanes] = small[20 + side, blocks - 1, 0:1, :]


def unpack(totals, wide, chans):
    vmem = pl.BlockSpec(memory_space=pltpu.VMEM)
    shapes = [(chans, wide), (wide, chans), (chans, 3 * chans), (chans, chans), (9, wide), (1, chans), (1, chans)]
    return pl.pallas_call(
        unpack_body,
        out_shape=tuple(jax.ShapeDtypeStruct(shape, f32) for shape in shapes),
        in_specs=[vmem],
        out_specs=(vmem,) * len(shapes),
        compiler_params=pltpu.CompilerParams(vmem_limit_bytes=32 << 20),
        name="unpack",
    )(totals)


def outer_cycle(top, bottom, left, right):
    fill = -(-(left.shape[0] + 2) // 8) * 8 - left.shape[0] - 2

    def pairs(axis):
        forward = [(i, i + 1) for i in range(lax.axis_size(axis) - 1)]
        return forward, [(b, a) for a, b in forward]

    forward, backward = pairs("row")
    above = lax.ppermute(bottom, "row", forward)
    below = lax.ppermute(top, "row", backward)
    forward, backward = pairs("col")

    def column(own, at):
        ends = [above[at : at + 1], own, below[at : at + 1]]
        return jnp.concatenate(ends + [jnp.zeros((fill, own.shape[-1]), own.dtype)])

    beside_left = lax.ppermute(column(right, above.shape[0] - 1), "col", forward)
    beside_right = lax.ppermute(column(left, 0), "col", backward)
    return above, below, beside_left, beside_right


def swap(values):
    return lax.all_to_all(values, ("row", "col"), split_axis=0, concat_axis=0, tiled=True)


def shards(field_in, cotangent, gain_conv, w_expand, w_depth, w_project, gain_attn, w_qkv, w_out):
    height, width, chans = field_in.shape
    wide = w_expand.shape[1]
    devices = lax.axis_size("row") * lax.axis_size("col")
    grad_scale = (height * width * devices) ** (-0.5)
    chunks = 2
    rows = height // chunks
    per = height * width // (GRID * GRID * chunks)
    gain_in = gain_conv.reshape(1, -1)
    taps = w_depth.reshape(9, wide)
    above, below, left, right = outer_cycle(field_in[0], field_in[-1], field_in[:, 0], field_in[:, -1])
    hiddens, pres = [], []
    for k in range(chunks):
        hidden, pre = expand(k, chunks, field_in.reshape(-1, chans), gain_in, w_expand)
        hiddens.append(hidden.reshape(rows, width, wide))
        pres.append(pre.reshape(rows, width, wide))
    side = left.shape[0] - (chunks - 1) * rows
    actives, convs, branches, gconvs, gcols = [], [], [], [], []
    moved, qkvs, outs, gains = [], [], [], []
    for k in range(chunks):
        cols = slice(k * rows, k * rows + side)
        upper = above if k == 0 else field_in[k * rows - 1]
        lower = below if k == chunks - 1 else field_in[(k + 1) * rows]
        edges = jnp.concatenate([upper, lower, left[cols], right[cols]])
        acted, conv, sent = mix(
            k, hiddens[k], edges, gain_in, w_expand, taps, w_project, field_in, cotangent, per
        )
        actives.append(acted)
        convs.append(conv)
        if k > 0:
            sent, moved[k - 1] = lax.optimization_barrier((sent, moved[k - 1]))
        moved.append(swap(sent.reshape(devices, -1, chans)))
    for k in range(chunks):
        branch, qkv, out, gain = attention(moved[k], gain_attn, w_qkv, w_out)
        qkvs.append(qkv)
        outs.append(out)
        gains.append(gain)
        if k == 0:
            branch, moved[1] = lax.optimization_barrier((branch, moved[1]))
        else:
            branch, branches[k - 1] = lax.optimization_barrier((branch, branches[k - 1]))
        branches.append(swap(branch).reshape(rows, -1, 2 * per, chans))
    for k in range(chunks):
        gconv, gcol, branches[k] = unmix(k, cotangent, branches[k], convs[k], w_project, per)
        gconvs.append(gconv)
        gcols.append(gcol)
    part = project_part(0, cotangent, branches[0], actives[0])
    early = project_part(1, cotangent, branches[1], actives[1], part, qkvs, outs)
    gcol = jnp.concatenate(gcols, axis=1).astype(jnp.bfloat16)
    above, below, left, right = outer_cycle(gconvs[0][0], gconvs[-1][-1], gcol[0], gcol[1])
    edge_rows = jnp.concatenate([above, below])
    edge_cols = jnp.stack([left, right]).astype(jnp.float32)
    early_all = swap(early.reshape(devices, -1, LANES))
    early_own = jnp.sum(early_all, axis=0)
    grad_field, late = spread(
        gconvs, hiddens, pres, branches, edge_rows, edge_cols, taps, w_expand, field_in, gain_in,
        cotangent, sum(gains),
    )
    late, early_own = lax.optimization_barrier((late, early_own))
    late_own = jnp.sum(swap(late.reshape(devices, -1, LANES)), axis=0)
    own = (jnp.concatenate([early_own, late_own]) * grad_scale).astype(jnp.bfloat16)
    totals = swap(jnp.broadcast_to(own, (devices,) + own.shape))
    totals = totals.reshape(chans // 8, wide // BLOCK, -1, LANES)
    grad_expand, grad_project, grad_qkv, grad_out, grad_depth, grad_gain_conv, grad_gain = unpack(totals, wide, chans)
    return (
        grad_field,
        grad_gain_conv.reshape(-1),
        grad_expand,
        grad_depth.reshape(w_depth.shape),
        grad_project,
        grad_gain.reshape(-1),
        grad_qkv,
        grad_out,
    )


def solution(mesh):
    in_specs = (P("row", "col", None), P("row", "col", None), P(), P(), P(), P(), P(), P(), P())
    out_specs = (P("row", "col", None), P(), P(), P(), P(), P(), P(), P())

    return jax.shard_map(shards, mesh=mesh, in_specs=in_specs, out_specs=out_specs, check_vma=False)
```

```python
import functools
import jax, jax.numpy as jnp
from jax import lax
from jax.experimental import pallas as pl
from jax.experimental.pallas import tpu as pltpu
from jax.sharding import PartitionSpec as P

GRID = 16
LOG2_E = 1.4426950408889634
HEADS=8
norm_eps=1e-5
f32=jnp.float32; bf16=jnp.bfloat16


def cost(micros):
    return pl.CostEstimate(flops=micros * 10**9, bytes_accessed=micros * 3 * 10**6, transcendentals=0)


def nt(a,b): return lax.dot_general(a,b,(((1,),(1,)),((),())),preferred_element_type=f32)


def nn(a,b): return jnp.dot(a,b,preferred_element_type=f32)


def swap_order(size, inner):
    rows = lax.broadcasted_iota(jnp.int32, (size, size), 0)
    cols = lax.broadcasted_iota(jnp.int32, (size, size), 1)
    outer = size // inner
    return (cols == lax.rem(rows, outer) * inner + lax.div(rows, outer)).astype(f32).astype(bf16)


def attention_body(moved_ref, gain_ref, w_qkv_ref, w_out_ref, branch_ref, gqkv_ref, gout_ref, ggain_ref, mids, cots, outs):
    devices, lines, chans = moved_ref.shape
    windows = mids.shape[0]
    per = lines // 2
    group = 256 // per
    span = 256 // windows
    head = chans // HEADS
    scale = head ** -0.5
    order = swap_order(256, windows)

    def gather(step, carry):
        base = step * group
        at = pl.multiple_of(step * span, span)
        for low, dest in ((0, mids), (per, cots)):
            block = moved_ref[pl.ds(base, group), low : low + per, :].reshape(256, chans)
            dest[:, pl.ds(at, span), :] = nn(order, block).astype(bf16).reshape(windows, span, chans)
        return carry

    lax.fori_loop(0, devices // group, gather, 0, unroll=2)
    gqkv_ref[...] = jnp.zeros_like(gqkv_ref)
    gout_ref[...] = jnp.zeros_like(gout_ref)
    ggain_ref[...] = jnp.zeros_like(ggain_ref)
    gain = gain_ref[...]
    lane = lax.broadcasted_iota(jnp.int32, (1, chans), 1) // head

    def window(index, carry):
        wide = mids[index].astype(f32)
        cot = cots[index]
        centred = wide - jnp.mean(wide, axis=-1, keepdims=True)
        inv_dev = lax.rsqrt(jnp.mean(centred * centred, axis=-1, keepdims=True) + norm_eps)
        normed = centred * inv_dev
        scaled = (normed * gain).astype(bf16)
        qkv = nn(scaled, w_qkv_ref[...]).astype(bf16)
        query, keys, values = (qkv[:, i * chans : (i + 1) * chans] for i in range(3))
        grad_att = nt(cot, w_out_ref[...]).astype(bf16)
        keys_t = keys.T
        values_t = values.T
        att_t, grad_query_t = [], []
        grads = [None, None]
        masks = [(lane == h).astype(f32).astype(bf16) for h in range(HEADS)]

        def first(h):
            query_h, grad_att_h = query * masks[h], grad_att * masks[h]
            return query_h, grad_att_h, nt(keys, query_h), nt(values, grad_att_h)

        def second(query_h, grad_att_h, scores, grad_probs):
            top = jnp.max(scores, axis=0, keepdims=True)
            expons = jnp.exp2((scores - top) * (scale * LOG2_E))
            probs = expons * (1.0 / jnp.sum(expons, axis=0, keepdims=True))
            row = jnp.sum(grad_probs * probs, axis=0, keepdims=True)
            grad_scores = (scale * probs * (grad_probs - row)).astype(bf16)
            return query_h, grad_att_h, probs.astype(bf16), grad_scores

        def third(h, query_h, grad_att_h, probs_b, grad_scores):
            rows = slice(h * head, (h + 1) * head)
            att_t.append(nn(values_t[rows], probs_b))
            grad_query_t.append(nn(keys_t[rows], grad_scores))
            parts = nn(grad_scores, query_h), nn(probs_b, grad_att_h)
            for i in range(2):
                grads[i] = parts[i] if h == 0 else grads[i] + parts[i]

        ahead = first(0)
        behind = None
        for h in range(HEADS):
            now = ahead
            if h + 1 < HEADS:
                ahead = first(h + 1)
            made = second(*now)
            if behind is not None:
                third(h - 1, *behind)
            behind = made
        third(HEADS - 1, *behind)

        grad_key, grad_value = grads
        att_t = jnp.concatenate(att_t, axis=0).astype(bf16)
        grad_query = jnp.concatenate(grad_query_t, axis=0).astype(bf16).T
        grad_proj = jnp.concatenate([grad_query, grad_key.astype(bf16), grad_value.astype(bf16)], axis=1)
        gout_ref[...] += nn(att_t, cot)
        gqkv_ref[...] += nn(scaled.T, grad_proj)
        grad_scaled = nt(grad_proj, w_qkv_ref[...])
        ggain_ref[...] += jnp.sum(grad_scaled * normed, axis=0, keepdims=True)
        grad_normed = grad_scaled * gain
        branch = inv_dev * (
            grad_normed
            - jnp.mean(grad_normed, axis=-1, keepdims=True)
            - normed * jnp.mean(grad_normed * normed, axis=-1, keepdims=True)
        )
        outs[index] = branch.astype(bf16)
        return carry

    lax.fori_loop(0, windows, window, 0, unroll=2)
    back = swap_order(256, span)

    def scatter(step, carry):
        at = pl.multiple_of(step * span, span)
        block = outs[:, pl.ds(at, span), :].reshape(256, chans)
        branch_ref[pl.ds(step * group, group)] = nn(back, block).astype(bf16).reshape(group, per, chans)
        return carry

    lax.fori_loop(0, devices // group, scatter, 0, unroll=2)


def attention(moved, gain_attn, w_qkv, w_out):
    devices, lines, chans = moved.shape
    tokens = devices * lines // 2
    windows = tokens // 256
    vmem = pl.BlockSpec(memory_space=pltpu.VMEM)
    return pl.pallas_call(
        attention_body,
        out_shape=(
            jax.ShapeDtypeStruct((devices, lines // 2, chans), bf16),
            jax.ShapeDtypeStruct(w_qkv.shape, f32),
            jax.ShapeDtypeStruct(w_out.shape, f32),
            jax.ShapeDtypeStruct((1, chans), f32),
        ),
        in_specs=[vmem] * 4,
        out_specs=(vmem,) * 4,
        scratch_shapes=[pltpu.VMEM((windows, 256, chans), bf16)] * 3,
        compiler_params=pltpu.CompilerParams(vmem_limit_bytes=48 << 20),
        cost_estimate=cost(20),
        name="attention",
    )(moved, gain_attn.reshape(1, -1), w_qkv, w_out)


root_half = 0.7071067811865476
inv_root_two_pi = 0.3989422804014327
BLOCK = 256
LANES = 128


def gelu_value(values):
    return 0.5 * values * (1.0 + lax.erf(values * root_half))


def gelu_slope(values):
    gauss = jnp.exp2(values * values * (-0.5 * LOG2_E))
    return 0.5 * (1.0 + lax.erf(values * root_half)) + values * gauss * inv_root_two_pi


def unit_norm(values):
    centred = values - jnp.mean(values, axis=-1, keepdims=True)
    inv_dev = lax.rsqrt(jnp.mean(centred * centred, axis=-1, keepdims=True) + norm_eps)
    return centred * inv_dev, inv_dev


def expand_body(x_ref, gain_ref, w_ref, hidden_ref, pre_ref, scaled):
    tokens = x_ref.shape[0]
    chunk = 256

    @pl.when(pl.program_id(0) == 0)
    def _():
        def step(at, carry):
            rows = pl.ds(pl.multiple_of(at * chunk, chunk), chunk)
            normed, _ = unit_norm(x_ref[rows, :].astype(f32))
            scaled[rows, :] = (normed * gain_ref[...]).astype(bf16)
            return carry

        lax.fori_loop(0, tokens // chunk, step, 0, unroll=2)

    def step(at, carry):
        rows = pl.ds(pl.multiple_of(at * chunk, chunk), chunk)
        pre_act = nn(scaled[rows, :], w_ref[...])
        hidden_ref[rows, :] = gelu_value(pre_act).astype(bf16)
        pre_ref[rows, :] = pre_act
        return carry

    lax.fori_loop(0, tokens // chunk, step, 0, unroll=4)


def whole(shape):
    return pl.BlockSpec(shape, lambda i: (0,) * len(shape))


def last(shape):
    return pl.BlockSpec(shape, lambda i: (0,) * (len(shape) - 1) + (i,))


def params(limit=56):
    return pltpu.CompilerParams(dimension_semantics=("arbitrary",), vmem_limit_bytes=limit << 20)


def expand(k, chunks, flat, gain, w_expand):
    tokens, chans = flat.shape
    tokens //= chunks
    wide = w_expand.shape[1]
    return pl.pallas_call(
        expand_body,
        grid=(wide // BLOCK,),
        out_shape=(jax.ShapeDtypeStruct((tokens, wide), bf16), jax.ShapeDtypeStruct((tokens, wide), f32)),
        in_specs=[pl.BlockSpec((tokens, chans), lambda i: (k, 0)), whole((1, chans)), last((chans, BLOCK))],
        out_specs=(last((tokens, BLOCK)), last((tokens, BLOCK))),
        scratch_shapes=[pltpu.VMEM((tokens, chans), bf16)],
        compiler_params=params(),
        cost_estimate=cost(7),
        name="expand",
    )(flat, gain, w_expand)


def fill(pad, cores, above, below, left, right):
    tiles, rows, cols, _ = pad.shape
    cols = cols - 16
    for t in range(tiles):
        lanes = slice(t * LANES, (t + 1) * LANES)
        at = 1
        for core in cores:
            for i in range(core.shape[0]):
                pad[t, at, 8 : 8 + cols, :] = core[i, :, lanes].astype(f32)
                at += 1
        pad[t, 0, 8 : 8 + cols, :] = above[:, lanes].astype(f32)
        pad[t, rows - 1, 8 : 8 + cols, :] = below[:, lanes].astype(f32)
        for i in range(rows):
            pad[t, i, 7:8, :] = left[i : i + 1, lanes]
            pad[t, i, 8 + cols : 9 + cols, :] = right[i : i + 1, lanes]


def regroup(values, per):
    _, cols, _ = values.shape
    half = cols // 2
    blocks = half // per
    return [
        jnp.concatenate([values[:, b * per : (b + 1) * per], values[:, half + b * per : half + (b + 1) * per]], axis=1)
        for b in range(blocks)
    ]


def ungroup(grouped, per):
    blocks = grouped.shape[1]
    wide = [grouped[:, b].astype(f32) for b in range(blocks)]
    return jnp.concatenate([w[:, :per] for w in wide] + [w[:, per:] for w in wide], axis=1)


def mix_body(k, per, hidden_ref, upper_ref, lower_ref, left_ref, right_ref, gain_ref, we_ref, wd_ref, wp_ref, x_ref, cot_ref, acted_ref, conv_ref, sent_ref, pad, acc, edge):
    height, width, _ = hidden_ref.shape
    step = pl.program_id(0)
    side = edge.shape[0] // 2 - width
    cols = slice(k * height, k * height + side)
    cells = [upper_ref[0], lower_ref[0], left_ref[cols], right_ref[cols]]
    normed, _ = unit_norm(jnp.concatenate([c.astype(f32) for c in cells]))
    scaled = (normed * gain_ref[...]).astype(bf16)
    edge[...] = gelu_value(nn(scaled, we_ref[...])).astype(bf16).astype(f32)
    low = 2 * width
    fill(
        pad,
        [hidden_ref],
        edge.at[0:width],
        edge.at[width:low],
        edge.at[low : low + side],
        edge.at[low + side : low + 2 * side],
    )
    for t in range(BLOCK // LANES):
        lanes = slice(t * LANES, (t + 1) * LANES)
        taps = [jnp.broadcast_to(wd_ref[p, q : q + 1, lanes], (8, LANES)) for p in range(3) for q in range(3)]

        def row(i, carry):
            summed = None
            for p in range(3):
                for q in range(3):
                    piece = pad[t, i + p, 7 + q : 7 + q + width, :].reshape(width // 8, 8, LANES)
                    term = piece * taps[3 * p + q]
                    summed = term if summed is None else summed + term
            summed = summed.reshape(width, LANES)
            acted_ref[i, :, lanes] = gelu_value(summed).astype(bf16)
            conv_ref[i, :, lanes] = summed
            return carry

        lax.fori_loop(0, height, row, 0, unroll=4)
    part = nn(acted_ref[...].reshape(height * width, BLOCK), wp_ref[...]).reshape(height, width, -1)

    @pl.when(step == 0)
    def _():
        acc[...] = x_ref[...].astype(f32) + part

    @pl.when(step > 0)
    def _():
        acc[...] += part

    @pl.when(step == pl.num_programs(0) - 1)
    def _():
        for kind, values in enumerate((acc[...], cot_ref[...].astype(f32))):
            for b, piece in enumerate(regroup(values, per)):
                sent_ref[:, b, kind * 2 * per : (kind + 1) * 2 * per, :] = piece.astype(bf16)


def mix(k, hidden, above, below, left, right, gain, w_expand, w_depth, w_project, field_in, cotangent, per):
    height, width, wide = hidden.shape
    chans = w_project.shape[1]
    grouped = (height, width // (2 * per), 4 * per, chans)
    chunks = field_in.shape[0] // height
    side = left.shape[0] - (chunks - 1) * height

    def beside(outer, ends, row):
        if ends:
            return outer.reshape(1, width, chans), whole((1, width, chans))
        return field_in, pl.BlockSpec((1, width, chans), lambda i: (row, 0, 0))

    upper, upper_spec = beside(above, k == 0, k * height - 1)
    lower, lower_spec = beside(below, k == chunks - 1, (k + 1) * height)
    return pl.pallas_call(
        functools.partial(mix_body, k, per),
        grid=(wide // BLOCK,),
        out_shape=(
            jax.ShapeDtypeStruct((height, width, wide), bf16),
            jax.ShapeDtypeStruct((height, width, wide), f32),
            jax.ShapeDtypeStruct(grouped, bf16),
        ),
        in_specs=[
            last((height, width, BLOCK)),
            upper_spec,
            lower_spec,
            whole(left.shape),
            whole(right.shape),
            whole((1, chans)),
            last((chans, BLOCK)),
            last((3, 3, BLOCK)),
            pl.BlockSpec((BLOCK, chans), lambda i: (i, 0)),
            pl.BlockSpec((height, width, chans), lambda i: (k, 0, 0)),
            pl.BlockSpec((height, width, chans), lambda i: (k, 0, 0)),
        ],
        out_specs=(last((height, width, BLOCK)), last((height, width, BLOCK)), whole(grouped)),
        scratch_shapes=[
            pltpu.VMEM((BLOCK // LANES, height + 2, width + 16, LANES), f32),
            pltpu.VMEM((height, width, chans), f32),
            pltpu.VMEM((2 * width + 2 * side, BLOCK), f32),
        ],
        compiler_params=params(),
        cost_estimate=cost(13),
        name="mix",
    )(hidden, upper, lower, left, right, gain, w_expand, w_depth, w_project, field_in, cotangent)


def unmix_body(k, per, cot_ref, back_ref, conv_ref, wp_ref, gconv_ref, cols_ref, row_ref, branch_ref, total):
    height, width, _ = conv_ref.shape

    @pl.when(pl.program_id(0) == 0)
    def _():
        branch = ungroup(back_ref[...], per)
        branch_ref[...] = branch.astype(bf16)
        total[...] = (cot_ref[...].astype(f32) + branch).astype(bf16)

    flat = total[...].reshape(height * width, -1)
    grad_acted = nt(flat, wp_ref[...]).astype(bf16).astype(f32).reshape(height, width, BLOCK)
    gconv_ref[...] = (grad_acted * gelu_slope(conv_ref[...])).astype(bf16)
    row_ref[...] = gconv_ref[(height - 1) * k]
    for i in range(height):
        cols_ref[0, i : i + 1, :] = gconv_ref[i, 0:1, :].astype(f32)
        cols_ref[1, i : i + 1, :] = gconv_ref[i, width - 1 : width, :].astype(f32)


def unmix(k, cotangent, returned, conv, w_project, per):
    height, width, wide = conv.shape
    chans = w_project.shape[1]
    return pl.pallas_call(
        functools.partial(unmix_body, k, per),
        grid=(wide // BLOCK,),
        out_shape=(
            jax.ShapeDtypeStruct((height, width, wide), bf16),
            jax.ShapeDtypeStruct((2, height, wide), f32),
            jax.ShapeDtypeStruct((width, wide), bf16),
            jax.ShapeDtypeStruct((height, width, chans), bf16),
        ),
        in_specs=[
            pl.BlockSpec((height, width, chans), lambda i: (k, 0, 0)),
            whole(returned.shape),
            last((height, width, BLOCK)),
            pl.BlockSpec((BLOCK, chans), lambda i: (i, 0)),
        ],
        out_specs=(last((height, width, BLOCK)), last((2, height, BLOCK)), last((width, BLOCK)), whole((height, width, chans))),
        scratch_shapes=[pltpu.VMEM((height, width, chans), bf16)],
        compiler_params=params(),
        cost_estimate=cost(5),
        name="unmix",
    )(cotangent, returned, conv, w_project)


def project_part_body(cot_ref, branch_ref, acted_ref, *refs):
    before, (part_ref, total_t) = refs[:-2], refs[-2:]
    height, width, chans = branch_ref.shape
    size = height * width

    @pl.when(pl.program_id(0) == 0)
    def _():
        total = cot_ref[...].astype(f32) + branch_ref[...].astype(f32)
        total_t[...] = total.astype(bf16).reshape(size, chans).T

    part = nn(total_t[...], acted_ref[...].reshape(size, BLOCK))
    for ref in before[:1]:
        part = part + ref[...]
    if not before:
        part_ref[...] = part
        return
    grad_project = part.T
    qkvs, outs = before[1:3], before[3:5]
    tiles, blocks = part_ref.shape[0], part_ref.shape[1]
    both = jnp.concatenate([sum(r[...] for r in qkvs), sum(r[...] for r in outs)], axis=1)
    for side in range(2):
        tile = grad_project[:, side * LANES : (side + 1) * LANES].reshape(tiles, blocks, 8, LANES)
        part_ref[:, :, 8 * side : 8 * side + 8, :] = tile
        for j in range(blocks):
            at = (2 * j + side) * LANES
            part_ref[:, j, 16 + 8 * side : 24 + 8 * side, :] = both[:, at : at + LANES].reshape(tiles, 8, LANES)


def project_part(k, cotangent, branch, acted, before=None, qkvs=(), outs=()):
    height, width, wide = acted.shape
    chans = cotangent.shape[-1]
    steps = wide // BLOCK
    tiles = wide // 8 // 4 // steps
    rows = chans // steps
    if before is None:
        extra, extra_specs = [], []
        out_shape, out_spec = (chans, wide), last((chans, BLOCK))
    else:
        extra = [before, *qkvs, *outs]
        extra_specs = [last((chans, BLOCK))]
        extra_specs += [pl.BlockSpec((rows, q.shape[1]), lambda i: (i, 0)) for q in extra[1:]]
        out_shape = (tiles * steps, 4, 32, LANES)
        out_spec = pl.BlockSpec((tiles, 4, 32, LANES), lambda i: (i, 0, 0, 0))
    return pl.pallas_call(
        project_part_body,
        grid=(steps,),
        out_shape=jax.ShapeDtypeStruct(out_shape, f32),
        in_specs=[
            pl.BlockSpec((height, width, chans), lambda i: (k, 0, 0)),
            whole((height, width, chans)),
            last((height, width, BLOCK)),
        ]
        + extra_specs,
        out_specs=out_spec,
        scratch_shapes=[pltpu.VMEM((chans, height * width), bf16)],
        compiler_params=params(),
        cost_estimate=cost(4),
        name="project_part",
    )(cotangent, branch, acted, *extra)


def spread_body(*refs):
    gconvs, hiddens, pres, backs = refs[0:2], refs[2:4], refs[4:6], refs[6:8]
    edges, (wd_ref, we_ref, x_ref, gain_ref, cot_ref) = refs[8:12], refs[12:17]
    attn_gain_ref, field_ref, packed_ref, pad, grad_pre, acc, scaled_t, ggain_ref = refs[17:]
    height, width, chans = x_ref.shape
    part = height // 2
    step = pl.program_id(0)
    chunk = 4

    @pl.when(step == 0)
    def _():
        def turn(at, carry):
            rows = x_ref[pl.ds(at * chunk, chunk)].reshape(chunk * width, chans).astype(f32)
            normed, _ = unit_norm(rows)
            cols = pl.ds(pl.multiple_of(at * chunk * width, chunk * width), chunk * width)
            scaled_t[:, cols] = (normed * gain_ref[...]).astype(bf16).T
            return carry

        lax.fori_loop(0, height // chunk, turn, 0, unroll=2)

    fill(pad, gconvs, *edges)
    packed_ref[:, 0, 16:24, :] = jnp.zeros((packed_ref.shape[0], 8, LANES), f32)
    for t in range(BLOCK // LANES):
        lanes = slice(t * LANES, (t + 1) * LANES)
        taps = [jnp.broadcast_to(wd_ref[p, q : q + 1, lanes], (8, LANES)) for p in range(3) for q in range(3)]

        def row(k, j, sums):
            i = j + k * part
            summed, out = None, []
            own = hiddens[k][j, :, lanes].astype(f32).reshape(width // 8, 8, LANES)
            for p in range(3):
                for q in range(3):
                    piece = pad[t, i + 2 - p, 9 - q : 9 - q + width, :].reshape(width // 8, 8, LANES)
                    term = piece * taps[3 * p + q]
                    summed = term if summed is None else summed + term
                    out.append(sums[3 * p + q] + jnp.sum(piece * own, axis=0))
            value = summed.reshape(width, LANES) * gelu_slope(pres[k][j, :, lanes])
            grad_pre[i, :, lanes] = value.astype(bf16)
            return tuple(out)

        sums = (jnp.zeros((8, LANES), f32),) * 9
        for k in range(2):
            sums = lax.fori_loop(0, part, functools.partial(row, k), sums, unroll=2)
        for k in range(9):
            packed_ref[2 * k + t, 0, 16:17, :] = jnp.sum(sums[k], axis=0, keepdims=True)
    flat = grad_pre[...].reshape(height * width, BLOCK)
    grad_expand = nn(scaled_t[...], flat)
    for t in range(BLOCK // LANES):
        tile = grad_expand[:, t * LANES : (t + 1) * LANES].reshape(-1, 8, LANES)
        packed_ref[:, 0, 8 * t : 8 * t + 8, :] = tile
    back = nt(flat, we_ref[...]).reshape(height, width, chans)

    @pl.when(step == 0)
    def _():
        acc[...] = back

    @pl.when(step > 0)
    def _():
        acc[...] += back

    @pl.when(step == pl.num_programs(0) - 1)
    def _():
        ggain_ref[...] = jnp.zeros_like(ggain_ref)
        size = 4

        def finish(k, at, carry):
            here = pl.ds(at * size, size)
            rows = pl.ds(k * part + at * size, size)
            total = cot_ref[rows].astype(f32) + backs[k][here].astype(f32)
            grad_scaled = acc[rows].reshape(size * width, chans)
            normed, inv_dev = unit_norm(x_ref[rows].astype(f32).reshape(size * width, chans))
            ggain_ref[...] += jnp.sum(grad_scaled * normed, axis=0, keepdims=True)
            grad_normed = grad_scaled * gain_ref[...]
            value = inv_dev * (
                grad_normed
                - jnp.mean(grad_normed, axis=-1, keepdims=True)
                - normed * jnp.mean(grad_normed * normed, axis=-1, keepdims=True)
            )
            field_ref[rows] = (total + value.reshape(size, width, chans)).astype(bf16)
            return carry

        for k in range(2):
            lax.fori_loop(0, part // size, functools.partial(finish, k), 0, unroll=2)
        for t in range(2):
            lanes = slice(t * LANES, (t + 1) * LANES)
            packed_ref[18 + t, 0, 16:17, :] = ggain_ref[:, lanes]
            packed_ref[20 + t, 0, 16:17, :] = attn_gain_ref[:, lanes]


def spread(gconvs, hiddens, pres, branches, edges, w_depth, w_expand, field_in, gain, cotangent, attn_gain):
    height, width, chans = field_in.shape
    wide = w_expand.shape[1]
    part = last((height // 2, width, BLOCK))
    field = whole((height, width, chans))
    return pl.pallas_call(
        spread_body,
        grid=(wide // BLOCK,),
        out_shape=(
            jax.ShapeDtypeStruct((height, width, chans), bf16),
            jax.ShapeDtypeStruct((chans // 8, wide // BLOCK, 24, LANES), f32),
        ),
        in_specs=[part] * 6
        + [whole((height // 2, width, chans))] * 2
        + [
            *[last((edge.shape[0], BLOCK)) for edge in edges],
            last((3, 3, BLOCK)),
            last((chans, BLOCK)),
            field,
            whole((1, chans)),
            field,
            whole((1, chans)),
        ],
        out_specs=(field, pl.BlockSpec((chans // 8, 1, 24, LANES), lambda i: (0, i, 0, 0))),
        scratch_shapes=[
            pltpu.VMEM((BLOCK // LANES, height + 2, width + 16, LANES), f32),
            pltpu.VMEM((height, width, BLOCK), bf16),
            pltpu.VMEM((height, width, chans), f32),
            pltpu.VMEM((chans, height * width), bf16),
            pltpu.VMEM((1, chans), f32),
        ],
        compiler_params=params(),
        cost_estimate=cost(30),
        name="spread",
    )(*gconvs, *hiddens, *pres, *branches, *edges, w_depth, w_expand, field_in, gain, cotangent, attn_gain)


def unpack_body(totals_ref, expand_ref, project_ref, qkv_ref, out_ref, depth_ref, gain_ref, attn_gain_ref):
    blocks = totals_ref.shape[1]
    small = totals_ref[:, :, 48:56, :].astype(f32)
    for side in range(2):
        here = slice(8 * side, 8 * side + 8)
        tile = totals_ref[:, :, here, :].astype(f32)
        project_ref[:, side * LANES : (side + 1) * LANES] = tile.reshape(-1, LANES)
        for j in range(blocks):
            lanes = slice((2 * j + side) * LANES, (2 * j + side + 1) * LANES)
            tile = totals_ref[:, j, 32 + 8 * side : 40 + 8 * side, :].astype(f32)
            expand_ref[:, lanes] = tile.reshape(-1, LANES)
            tile = totals_ref[:, j, 16 + 8 * side : 24 + 8 * side, :].astype(f32).reshape(-1, LANES)
            if j < blocks - 1:
                qkv_ref[:, lanes] = tile
            else:
                out_ref[:, side * LANES : (side + 1) * LANES] = tile
            for k in range(9):
                depth_ref[k // 3, k % 3 : k % 3 + 1, lanes] = small[2 * k + side, j, 0:1, :]
        lanes = slice(side * LANES, (side + 1) * LANES)
        gain_ref[:, lanes] = small[18 + side, blocks - 1, 0:1, :]
        attn_gain_ref[:, lanes] = small[20 + side, blocks - 1, 0:1, :]


def unpack(totals, wide, chans):
    vmem = pl.BlockSpec(memory_space=pltpu.VMEM)
    shapes = [(chans, wide), (wide, chans), (chans, 3 * chans), (chans, chans), (3, 3, wide), (1, chans), (1, chans)]
    return pl.pallas_call(
        unpack_body,
        out_shape=tuple(jax.ShapeDtypeStruct(shape, f32) for shape in shapes),
        in_specs=[vmem],
        out_specs=(vmem,) * len(shapes),
        compiler_params=pltpu.CompilerParams(vmem_limit_bytes=32 << 20),
        name="unpack",
    )(totals)


def outer_cycle(top, bottom, left, right):
    fill = -(-(left.shape[0] + 2) // 8) * 8 - left.shape[0] - 2

    def pairs(axis):
        forward = [(i, i + 1) for i in range(lax.axis_size(axis) - 1)]
        return forward, [(b, a) for a, b in forward]

    forward, backward = pairs("row")
    above = lax.ppermute(bottom, "row", forward)
    below = lax.ppermute(top, "row", backward)
    forward, backward = pairs("col")

    def column(own, at):
        ends = [above[at : at + 1].astype(own.dtype), own, below[at : at + 1].astype(own.dtype)]
        return jnp.concatenate(ends + [jnp.zeros((fill, own.shape[-1]), own.dtype)])

    beside_left = lax.ppermute(column(right, above.shape[0] - 1), "col", forward)
    beside_right = lax.ppermute(column(left, 0), "col", backward)
    return above, below, beside_left, beside_right


def swap(values):
    return lax.all_to_all(values, ("row", "col"), split_axis=0, concat_axis=0, tiled=True)


def shards(field_in, cotangent, gain_conv, w_expand, w_depth, w_project, gain_attn, w_qkv, w_out):
    height, width, chans = field_in.shape
    wide = w_expand.shape[1]
    devices = lax.axis_size("row") * lax.axis_size("col")
    grad_scale = (height * width * devices) ** (-0.5)
    chunks = 2
    rows = height // chunks
    per = height * width // (GRID * GRID * chunks)
    gain_in = gain_conv.reshape(1, -1)
    above, below, left, right = outer_cycle(field_in[0], field_in[-1], field_in[:, 0], field_in[:, -1])
    hiddens, pres = [], []
    for k in range(chunks):
        hidden, pre = expand(k, chunks, field_in.reshape(-1, chans), gain_in, w_expand)
        hiddens.append(hidden.reshape(rows, width, wide))
        pres.append(pre.reshape(rows, width, wide))
    actives, convs, branches, gconvs, gcols, grows = [], [], [], [], [], []
    moved, qkvs, outs, gains = [], [], [], []
    for k in range(chunks):
        acted, conv, sent = mix(
            k, hiddens[k], above, below, left, right, gain_in, w_expand, w_depth, w_project, field_in, cotangent, per
        )
        actives.append(acted)
        convs.append(conv)
        if k > 0:
            sent, moved[k - 1] = lax.optimization_barrier((sent, moved[k - 1]))
        moved.append(swap(sent.reshape(devices, -1, chans)))
    for k in range(chunks):
        branch, qkv, out, gain = attention(moved[k], gain_attn, w_qkv, w_out)
        qkvs.append(qkv)
        outs.append(out)
        gains.append(gain)
        if k == 0:
            branch, moved[1] = lax.optimization_barrier((branch, moved[1]))
        else:
            branch, branches[k - 1] = lax.optimization_barrier((branch, branches[k - 1]))
        branches.append(swap(branch).reshape(rows, -1, 2 * per, chans))
    for k in range(chunks):
        gconv, gcol, grow, branches[k] = unmix(k, cotangent, branches[k], convs[k], w_project, per)
        gconvs.append(gconv)
        gcols.append(gcol)
        grows.append(grow)
    part = project_part(0, cotangent, branches[0], actives[0])
    early = project_part(1, cotangent, branches[1], actives[1], part, qkvs, outs)
    gcol = jnp.concatenate(gcols, axis=1)
    above, below, left, right = outer_cycle(grows[0], grows[-1], gcol[0], gcol[1])
    edge_rows = [above, below]
    edge_cols = [left, right]
    early_all = swap(early.reshape(devices, -1, LANES))
    early_own = jnp.sum(early_all, axis=0)
    grad_field, late = spread(
        gconvs, hiddens, pres, branches, [*edge_rows, *edge_cols], w_depth, w_expand, field_in, gain_in,
        cotangent, sum(gains),
    )
    late, early_own = lax.optimization_barrier((late, early_own))
    late_own = jnp.sum(swap(late.reshape(devices, -1, LANES)), axis=0)
    own = (jnp.concatenate([early_own, late_own]) * grad_scale).astype(jnp.bfloat16)
    totals = swap(jnp.broadcast_to(own, (devices,) + own.shape))
    totals = totals.reshape(chans // 8, wide // BLOCK, -1, LANES)
    grad_expand, grad_project, grad_qkv, grad_out, grad_depth, grad_gain_conv, grad_gain = unpack(totals, wide, chans)
    return (
        grad_field,
        grad_gain_conv.reshape(-1),
        grad_expand,
        grad_depth,
        grad_project,
        grad_gain.reshape(-1),
        grad_qkv,
        grad_out,
    )


def solution(mesh):
    in_specs = (P("row", "col", None), P("row", "col", None), P(), P(), P(), P(), P(), P(), P())
    out_specs = (P("row", "col", None), P(), P(), P(), P(), P(), P(), P())

    return jax.shard_map(shards, mesh=mesh, in_specs=in_specs, out_specs=out_specs, check_vma=False)
```

```python
import functools
import jax, jax.numpy as jnp
from jax import lax
from jax.experimental import pallas as pl
from jax.experimental.pallas import tpu as pltpu
from jax.sharding import PartitionSpec as P

GRID = 16
LOG2_E = 1.4426950408889634
HEADS=8
norm_eps=1e-5
f32=jnp.float32; bf16=jnp.bfloat16


def cost(micros):
    return pl.CostEstimate(flops=micros * 10**9, bytes_accessed=micros * 3 * 10**6, transcendentals=0)


def nt(a,b): return lax.dot_general(a,b,(((1,),(1,)),((),())),preferred_element_type=f32)


def nn(a,b): return jnp.dot(a,b,preferred_element_type=f32)


def swap_order(size, inner):
    rows = lax.broadcasted_iota(jnp.int32, (size, size), 0)
    cols = lax.broadcasted_iota(jnp.int32, (size, size), 1)
    outer = size // inner
    return (cols == lax.rem(rows, outer) * inner + lax.div(rows, outer)).astype(f32).astype(bf16)


def attention_body(moved_ref, gain_ref, w_qkv_ref, w_out_ref, branch_ref, gqkv_ref, gout_ref, ggain_ref, mids, cots, outs):
    devices, lines, chans = moved_ref.shape
    windows = mids.shape[0]
    per = lines // 2
    group = 256 // per
    span = 256 // windows
    head = chans // HEADS
    scale = head ** -0.5
    order = swap_order(256, windows)

    def gather(step, carry):
        base = step * group
        at = pl.multiple_of(step * span, span)
        for low, dest in ((0, mids), (per, cots)):
            block = moved_ref[pl.ds(base, group), low : low + per, :].reshape(256, chans)
            dest[:, pl.ds(at, span), :] = nn(order, block).astype(bf16).reshape(windows, span, chans)
        return carry

    lax.fori_loop(0, devices // group, gather, 0, unroll=2)
    gqkv_ref[...] = jnp.zeros_like(gqkv_ref)
    gout_ref[...] = jnp.zeros_like(gout_ref)
    ggain_ref[...] = jnp.zeros_like(ggain_ref)
    gain = gain_ref[...]
    lane = lax.broadcasted_iota(jnp.int32, (1, chans), 1) // head

    def window(index, carry):
        wide = mids[index].astype(f32)
        cot = cots[index]
        centred = wide - jnp.mean(wide, axis=-1, keepdims=True)
        inv_dev = lax.rsqrt(jnp.mean(centred * centred, axis=-1, keepdims=True) + norm_eps)
        normed = centred * inv_dev
        scaled = (normed * gain).astype(bf16)
        qkv = nn(scaled, w_qkv_ref[...]).astype(bf16)
        query, keys, values = (qkv[:, i * chans : (i + 1) * chans] for i in range(3))
        grad_att = nt(cot, w_out_ref[...]).astype(bf16)
        keys_t = keys.T
        values_t = values.T
        att_t, grad_query_t = [], []
        grads = [None, None]
        masks = [(lane == h).astype(f32).astype(bf16) for h in range(HEADS)]

        def first(h):
            query_h, grad_att_h = query * masks[h], grad_att * masks[h]
            return query_h, grad_att_h, nt(keys, query_h), nt(values, grad_att_h)

        def second(query_h, grad_att_h, scores, grad_probs):
            top = jnp.max(scores, axis=0, keepdims=True)
            expons = jnp.exp2((scores - top) * (scale * LOG2_E))
            probs = expons * (1.0 / jnp.sum(expons, axis=0, keepdims=True))
            row = jnp.sum(grad_probs * probs, axis=0, keepdims=True)
            grad_scores = (scale * probs * (grad_probs - row)).astype(bf16)
            return query_h, grad_att_h, probs.astype(bf16), grad_scores

        def third(h, query_h, grad_att_h, probs_b, grad_scores):
            rows = slice(h * head, (h + 1) * head)
            att_t.append(nn(values_t[rows], probs_b))
            grad_query_t.append(nn(keys_t[rows], grad_scores))
            parts = nn(grad_scores, query_h), nn(probs_b, grad_att_h)
            for i in range(2):
                grads[i] = parts[i] if h == 0 else grads[i] + parts[i]

        ahead = first(0)
        behind = None
        for h in range(HEADS):
            now = ahead
            if h + 1 < HEADS:
                ahead = first(h + 1)
            made = second(*now)
            if behind is not None:
                third(h - 1, *behind)
            behind = made
        third(HEADS - 1, *behind)

        grad_key, grad_value = grads
        att_t = jnp.concatenate(att_t, axis=0).astype(bf16)
        grad_query = jnp.concatenate(grad_query_t, axis=0).astype(bf16).T
        grad_proj = jnp.concatenate([grad_query, grad_key.astype(bf16), grad_value.astype(bf16)], axis=1)
        gout_ref[...] += nn(att_t, cot)
        gqkv_ref[...] += nn(scaled.T, grad_proj)
        grad_scaled = nt(grad_proj, w_qkv_ref[...])
        ggain_ref[...] += jnp.sum(grad_scaled * normed, axis=0, keepdims=True)
        grad_normed = grad_scaled * gain
        branch = inv_dev * (
            grad_normed
            - jnp.mean(grad_normed, axis=-1, keepdims=True)
            - normed * jnp.mean(grad_normed * normed, axis=-1, keepdims=True)
        )
        outs[index] = branch.astype(bf16)
        return carry

    lax.fori_loop(0, windows, window, 0, unroll=2)
    back = swap_order(256, span)

    def scatter(step, carry):
        at = pl.multiple_of(step * span, span)
        block = outs[:, pl.ds(at, span), :].reshape(256, chans)
        branch_ref[pl.ds(step * group, group)] = nn(back, block).astype(bf16).reshape(group, per, chans)
        return carry

    lax.fori_loop(0, devices // group, scatter, 0, unroll=2)


def attention(moved, gain_attn, w_qkv, w_out):
    devices, lines, chans = moved.shape
    tokens = devices * lines // 2
    windows = tokens // 256
    vmem = pl.BlockSpec(memory_space=pltpu.VMEM)
    return pl.pallas_call(
        attention_body,
        out_shape=(
            jax.ShapeDtypeStruct((devices, lines // 2, chans), bf16),
            jax.ShapeDtypeStruct(w_qkv.shape, f32),
            jax.ShapeDtypeStruct(w_out.shape, f32),
            jax.ShapeDtypeStruct((1, chans), f32),
        ),
        in_specs=[vmem] * 4,
        out_specs=(vmem,) * 4,
        scratch_shapes=[pltpu.VMEM((windows, 256, chans), bf16)] * 3,
        compiler_params=pltpu.CompilerParams(vmem_limit_bytes=48 << 20),
        cost_estimate=cost(20),
        name="attention",
    )(moved, gain_attn.reshape(1, -1), w_qkv, w_out)


root_half = 0.7071067811865476
inv_root_two_pi = 0.3989422804014327
BLOCK = 256
LANES = 128


def gelu_value(values):
    return 0.5 * values * (1.0 + lax.erf(values * root_half))


def gelu_slope(values):
    gauss = jnp.exp2(values * values * (-0.5 * LOG2_E))
    return 0.5 * (1.0 + lax.erf(values * root_half)) + values * gauss * inv_root_two_pi


def unit_norm(values):
    centred = values - jnp.mean(values, axis=-1, keepdims=True)
    inv_dev = lax.rsqrt(jnp.mean(centred * centred, axis=-1, keepdims=True) + norm_eps)
    return centred * inv_dev, inv_dev


def expand_body(x_ref, gain_ref, w_ref, hidden_ref, pre_ref, scaled):
    tokens = x_ref.shape[0]
    chunk = 256

    @pl.when(pl.program_id(0) == 0)
    def _():
        def step(at, carry):
            rows = pl.ds(pl.multiple_of(at * chunk, chunk), chunk)
            normed, _ = unit_norm(x_ref[rows, :].astype(f32))
            scaled[rows, :] = (normed * gain_ref[...]).astype(bf16)
            return carry

        lax.fori_loop(0, tokens // chunk, step, 0, unroll=2)

    def step(at, carry):
        rows = pl.ds(pl.multiple_of(at * chunk, chunk), chunk)
        pre_act = nn(scaled[rows, :], w_ref[...])
        hidden_ref[rows, :] = gelu_value(pre_act).astype(bf16)
        pre_ref[rows, :] = pre_act
        return carry

    lax.fori_loop(0, tokens // chunk, step, 0, unroll=4)


def whole(shape):
    return pl.BlockSpec(shape, lambda i: (0,) * len(shape))


def last(shape):
    return pl.BlockSpec(shape, lambda i: (0,) * (len(shape) - 1) + (i,))


def params(limit=56):
    return pltpu.CompilerParams(dimension_semantics=("arbitrary",), vmem_limit_bytes=limit << 20)


def expand(k, chunks, flat, gain, w_expand):
    tokens, chans = flat.shape
    tokens //= chunks
    wide = w_expand.shape[1]
    return pl.pallas_call(
        expand_body,
        grid=(wide // BLOCK,),
        out_shape=(jax.ShapeDtypeStruct((tokens, wide), bf16), jax.ShapeDtypeStruct((tokens, wide), f32)),
        in_specs=[pl.BlockSpec((tokens, chans), lambda i: (k, 0)), whole((1, chans)), last((chans, BLOCK))],
        out_specs=(last((tokens, BLOCK)), last((tokens, BLOCK))),
        scratch_shapes=[pltpu.VMEM((tokens, chans), bf16)],
        compiler_params=params(),
        cost_estimate=cost(7),
        name="expand",
    )(flat, gain, w_expand)


def fill(pad, cores, above, below, left, right):
    tiles, rows, cols, _ = pad.shape
    cols = cols - 16
    for t in range(tiles):
        lanes = slice(t * LANES, (t + 1) * LANES)
        at = 1
        for core in cores:
            for i in range(core.shape[0]):
                pad[t, at, 8 : 8 + cols, :] = core[i, :, lanes].astype(f32)
                at += 1
        pad[t, 0, 8 : 8 + cols, :] = above[:, lanes].astype(f32)
        pad[t, rows - 1, 8 : 8 + cols, :] = below[:, lanes].astype(f32)
        for i in range(rows):
            pad[t, i, 7:8, :] = left[i : i + 1, lanes]
            pad[t, i, 8 + cols : 9 + cols, :] = right[i : i + 1, lanes]


def regroup(values, per):
    _, cols, _ = values.shape
    half = cols // 2
    blocks = half // per
    return [
        jnp.concatenate([values[:, b * per : (b + 1) * per], values[:, half + b * per : half + (b + 1) * per]], axis=1)
        for b in range(blocks)
    ]


def ungroup(grouped, per):
    blocks = grouped.shape[1]
    wide = [grouped[:, b].astype(f32) for b in range(blocks)]
    return jnp.concatenate([w[:, :per] for w in wide] + [w[:, per:] for w in wide], axis=1)


def mix_body(k, per, hidden_ref, upper_ref, lower_ref, left_ref, right_ref, gain_ref, we_ref, wd_ref, wp_ref, x_ref, cot_ref, acted_ref, conv_ref, sent_ref, pad, acc, edge):
    height, width, _ = hidden_ref.shape
    step = pl.program_id(0)
    side = edge.shape[0] // 2 - width
    cols = slice(k * height, k * height + side)
    cells = [upper_ref[0], lower_ref[0], left_ref[cols], right_ref[cols]]
    normed, _ = unit_norm(jnp.concatenate([c.astype(f32) for c in cells]))
    scaled = (normed * gain_ref[...]).astype(bf16)
    edge[...] = gelu_value(nn(scaled, we_ref[...])).astype(bf16).astype(f32)
    low = 2 * width
    fill(
        pad,
        [hidden_ref],
        edge.at[0:width],
        edge.at[width:low],
        edge.at[low : low + side],
        edge.at[low + side : low + 2 * side],
    )
    for t in range(BLOCK // LANES):
        lanes = slice(t * LANES, (t + 1) * LANES)
        taps = [jnp.broadcast_to(wd_ref[p, q : q + 1, lanes], (8, LANES)) for p in range(3) for q in range(3)]

        def row(i, carry):
            summed = None
            for p in range(3):
                for q in range(3):
                    piece = pad[t, i + p, 7 + q : 7 + q + width, :].reshape(width // 8, 8, LANES)
                    term = piece * taps[3 * p + q]
                    summed = term if summed is None else summed + term
            summed = summed.reshape(width, LANES)
            acted_ref[i, :, lanes] = gelu_value(summed).astype(bf16)
            conv_ref[i, :, lanes] = summed
            return carry

        lax.fori_loop(0, height, row, 0, unroll=4)
    part = nn(acted_ref[...].reshape(height * width, BLOCK), wp_ref[...]).reshape(height, width, -1)

    @pl.when(step == 0)
    def _():
        acc[...] = x_ref[...].astype(f32) + part

    @pl.when(step > 0)
    def _():
        acc[...] += part

    @pl.when(step == pl.num_programs(0) - 1)
    def _():
        for kind, values in enumerate((acc[...], cot_ref[...].astype(f32))):
            for b, piece in enumerate(regroup(values, per)):
                sent_ref[:, b, kind * 2 * per : (kind + 1) * 2 * per, :] = piece.astype(bf16)


def mix(k, hidden, above, below, left, right, gain, w_expand, w_depth, w_project, field_in, cotangent, per):
    height, width, wide = hidden.shape
    chans = w_project.shape[1]
    grouped = (height, width // (2 * per), 4 * per, chans)
    chunks = field_in.shape[0] // height
    side = left.shape[0] - (chunks - 1) * height

    def beside(outer, ends, row):
        if ends:
            return outer.reshape(1, width, chans), whole((1, width, chans))
        return field_in, pl.BlockSpec((1, width, chans), lambda i: (row, 0, 0))

    upper, upper_spec = beside(above, k == 0, k * height - 1)
    lower, lower_spec = beside(below, k == chunks - 1, (k + 1) * height)
    return pl.pallas_call(
        functools.partial(mix_body, k, per),
        grid=(wide // BLOCK,),
        out_shape=(
            jax.ShapeDtypeStruct((height, width, wide), bf16),
            jax.ShapeDtypeStruct((height, width, wide), f32),
            jax.ShapeDtypeStruct(grouped, bf16),
        ),
        in_specs=[
            last((height, width, BLOCK)),
            upper_spec,
            lower_spec,
            whole(left.shape),
            whole(right.shape),
            whole((1, chans)),
            last((chans, BLOCK)),
            last((3, 3, BLOCK)),
            pl.BlockSpec((BLOCK, chans), lambda i: (i, 0)),
            pl.BlockSpec((height, width, chans), lambda i: (k, 0, 0)),
            pl.BlockSpec((height, width, chans), lambda i: (k, 0, 0)),
        ],
        out_specs=(last((height, width, BLOCK)), last((height, width, BLOCK)), whole(grouped)),
        scratch_shapes=[
            pltpu.VMEM((BLOCK // LANES, height + 2, width + 16, LANES), f32),
            pltpu.VMEM((height, width, chans), f32),
            pltpu.VMEM((2 * width + 2 * side, BLOCK), f32),
        ],
        compiler_params=params(),
        cost_estimate=cost(13),
        name="mix",
    )(hidden, upper, lower, left, right, gain, w_expand, w_depth, w_project, field_in, cotangent)


def unmix_body(k, per, cot_ref, back_ref, conv_ref, wp_ref, gconv_ref, cols_ref, row_ref, branch_ref, total):
    height, width, _ = conv_ref.shape

    @pl.when(pl.program_id(0) == 0)
    def _():
        branch = ungroup(back_ref[...], per)
        branch_ref[...] = branch.astype(bf16)
        total[...] = (cot_ref[...].astype(f32) + branch).astype(bf16)

    flat = total[...].reshape(height * width, -1)
    grad_acted = nt(flat, wp_ref[...]).astype(bf16).astype(f32).reshape(height, width, BLOCK)
    gconv_ref[...] = (grad_acted * gelu_slope(conv_ref[...])).astype(bf16)
    row_ref[...] = gconv_ref[(height - 1) * k]
    for i in range(height):
        cols_ref[0, i : i + 1, :] = gconv_ref[i, 0:1, :].astype(f32)
        cols_ref[1, i : i + 1, :] = gconv_ref[i, width - 1 : width, :].astype(f32)


def unmix(k, cotangent, returned, conv, w_project, per):
    height, width, wide = conv.shape
    chans = w_project.shape[1]
    return pl.pallas_call(
        functools.partial(unmix_body, k, per),
        grid=(wide // BLOCK,),
        out_shape=(
            jax.ShapeDtypeStruct((height, width, wide), bf16),
            jax.ShapeDtypeStruct((2, height, wide), f32),
            jax.ShapeDtypeStruct((width, wide), bf16),
            jax.ShapeDtypeStruct((height, width, chans), bf16),
        ),
        in_specs=[
            pl.BlockSpec((height, width, chans), lambda i: (k, 0, 0)),
            whole(returned.shape),
            last((height, width, BLOCK)),
            pl.BlockSpec((BLOCK, chans), lambda i: (i, 0)),
        ],
        out_specs=(last((height, width, BLOCK)), last((2, height, BLOCK)), last((width, BLOCK)), whole((height, width, chans))),
        scratch_shapes=[pltpu.VMEM((height, width, chans), bf16)],
        compiler_params=params(),
        cost_estimate=cost(5),
        name="unmix",
    )(cotangent, returned, conv, w_project)


def project_part_body(cot_ref, branch_ref, acted_ref, *refs):
    before, (part_ref, total_t) = refs[:-2], refs[-2:]
    height, width, chans = branch_ref.shape
    size = height * width

    @pl.when(pl.program_id(0) == 0)
    def _():
        total = cot_ref[...].astype(f32) + branch_ref[...].astype(f32)
        total_t[...] = total.astype(bf16).reshape(size, chans).T

    part = nn(total_t[...], acted_ref[...].reshape(size, BLOCK))
    for ref in before[:1]:
        part = part + ref[...]
    if not before:
        part_ref[...] = part
        return
    grad_project = part.T
    qkvs, outs = before[1:3], before[3:5]
    tiles, blocks = part_ref.shape[0], part_ref.shape[1]
    both = jnp.concatenate([sum(r[...] for r in qkvs), sum(r[...] for r in outs)], axis=1)
    for side in range(2):
        tile = grad_project[:, side * LANES : (side + 1) * LANES].reshape(tiles, blocks, 8, LANES)
        part_ref[:, :, 8 * side : 8 * side + 8, :] = tile
        for j in range(blocks):
            at = (2 * j + side) * LANES
            part_ref[:, j, 16 + 8 * side : 24 + 8 * side, :] = both[:, at : at + LANES].reshape(tiles, 8, LANES)


def project_part(k, cotangent, branch, acted, before=None, qkvs=(), outs=()):
    height, width, wide = acted.shape
    chans = cotangent.shape[-1]
    steps = wide // BLOCK
    tiles = wide // 8 // 4 // steps
    rows = chans // steps
    if before is None:
        extra, extra_specs = [], []
        out_shape, out_spec = (chans, wide), last((chans, BLOCK))
    else:
        extra = [before, *qkvs, *outs]
        extra_specs = [last((chans, BLOCK))]
        extra_specs += [pl.BlockSpec((rows, q.shape[1]), lambda i: (i, 0)) for q in extra[1:]]
        out_shape = (tiles * steps, 4, 32, LANES)
        out_spec = pl.BlockSpec((tiles, 4, 32, LANES), lambda i: (i, 0, 0, 0))
    return pl.pallas_call(
        project_part_body,
        grid=(steps,),
        out_shape=jax.ShapeDtypeStruct(out_shape, f32),
        in_specs=[
            pl.BlockSpec((height, width, chans), lambda i: (k, 0, 0)),
            whole((height, width, chans)),
            last((height, width, BLOCK)),
        ]
        + extra_specs,
        out_specs=out_spec,
        scratch_shapes=[pltpu.VMEM((chans, height * width), bf16)],
        compiler_params=params(),
        cost_estimate=cost(4),
        name="project_part",
    )(cotangent, branch, acted, *extra)


def spread_body(*refs):
    gconvs, hiddens, pres, backs = refs[0:2], refs[2:4], refs[4:6], refs[6:8]
    edges, (wd_ref, we_ref, x_ref, gain_ref, cot_ref) = refs[8:12], refs[12:17]
    gains, (field_ref, packed_ref, pad, grad_pre, acc, scaled_t, ggain_ref) = refs[17:19], refs[19:]
    height, width, chans = x_ref.shape
    part = height // 2
    step = pl.program_id(0)
    chunk = 4

    @pl.when(step == 0)
    def _():
        def turn(at, carry):
            rows = x_ref[pl.ds(at * chunk, chunk)].reshape(chunk * width, chans).astype(f32)
            normed, _ = unit_norm(rows)
            cols = pl.ds(pl.multiple_of(at * chunk * width, chunk * width), chunk * width)
            scaled_t[:, cols] = (normed * gain_ref[...]).astype(bf16).T
            return carry

        lax.fori_loop(0, height // chunk, turn, 0, unroll=2)

    fill(pad, gconvs, *edges)
    packed_ref[:, 0, 16:24, :] = jnp.zeros((packed_ref.shape[0], 8, LANES), f32)
    for t in range(BLOCK // LANES):
        lanes = slice(t * LANES, (t + 1) * LANES)
        taps = [jnp.broadcast_to(wd_ref[p, q : q + 1, lanes], (8, LANES)) for p in range(3) for q in range(3)]

        def row(k, j, sums):
            i = j + k * part
            summed, out = None, []
            own = hiddens[k][j, :, lanes].astype(f32).reshape(width // 8, 8, LANES)
            for p in range(3):
                for q in range(3):
                    piece = pad[t, i + 2 - p, 9 - q : 9 - q + width, :].reshape(width // 8, 8, LANES)
                    term = piece * taps[3 * p + q]
                    summed = term if summed is None else summed + term
                    out.append(sums[3 * p + q] + jnp.sum(piece * own, axis=0))
            value = summed.reshape(width, LANES) * gelu_slope(pres[k][j, :, lanes])
            grad_pre[i, :, lanes] = value.astype(bf16)
            return tuple(out)

        sums = (jnp.zeros((8, LANES), f32),) * 9
        for k in range(2):
            sums = lax.fori_loop(0, part, functools.partial(row, k), sums, unroll=4)
        for k in range(9):
            packed_ref[2 * k + t, 0, 16:17, :] = jnp.sum(sums[k], axis=0, keepdims=True)
    flat = grad_pre[...].reshape(height * width, BLOCK)
    grad_expand = nn(scaled_t[...], flat)
    for t in range(BLOCK // LANES):
        tile = grad_expand[:, t * LANES : (t + 1) * LANES].reshape(-1, 8, LANES)
        packed_ref[:, 0, 8 * t : 8 * t + 8, :] = tile
    back = nt(flat, we_ref[...]).reshape(height, width, chans)

    @pl.when(step == 0)
    def _():
        acc[...] = back

    @pl.when(step > 0)
    def _():
        acc[...] += back

    @pl.when(step == pl.num_programs(0) - 1)
    def _():
        ggain_ref[...] = jnp.zeros_like(ggain_ref)
        size = 4

        def finish(k, at, carry):
            here = pl.ds(at * size, size)
            rows = pl.ds(k * part + at * size, size)
            total = cot_ref[rows].astype(f32) + backs[k][here].astype(f32)
            grad_scaled = acc[rows].reshape(size * width, chans)
            normed, inv_dev = unit_norm(x_ref[rows].astype(f32).reshape(size * width, chans))
            ggain_ref[...] += jnp.sum(grad_scaled * normed, axis=0, keepdims=True)
            grad_normed = grad_scaled * gain_ref[...]
            value = inv_dev * (
                grad_normed
                - jnp.mean(grad_normed, axis=-1, keepdims=True)
                - normed * jnp.mean(grad_normed * normed, axis=-1, keepdims=True)
            )
            field_ref[rows] = (total + value.reshape(size, width, chans)).astype(bf16)
            return carry

        for k in range(2):
            lax.fori_loop(0, part // size, functools.partial(finish, k), 0, unroll=2)
        for t in range(2):
            lanes = slice(t * LANES, (t + 1) * LANES)
            packed_ref[18 + t, 0, 16:17, :] = ggain_ref[:, lanes]
            packed_ref[20 + t, 0, 16:17, :] = gains[0][:, lanes] + gains[1][:, lanes]


def spread(gconvs, hiddens, pres, branches, edges, w_depth, w_expand, field_in, gain, cotangent, attn_gains):
    height, width, chans = field_in.shape
    wide = w_expand.shape[1]
    part = last((height // 2, width, BLOCK))
    field = whole((height, width, chans))
    return pl.pallas_call(
        spread_body,
        grid=(wide // BLOCK,),
        out_shape=(
            jax.ShapeDtypeStruct((height, width, chans), bf16),
            jax.ShapeDtypeStruct((chans // 8, wide // BLOCK, 24, LANES), f32),
        ),
        in_specs=[part] * 6
        + [whole((height // 2, width, chans))] * 2
        + [
            *[last((edge.shape[0], BLOCK)) for edge in edges],
            last((3, 3, BLOCK)),
            last((chans, BLOCK)),
            field,
            whole((1, chans)),
            field,
            whole((1, chans)),
            whole((1, chans)),
        ],
        out_specs=(field, pl.BlockSpec((chans // 8, 1, 24, LANES), lambda i: (0, i, 0, 0))),
        scratch_shapes=[
            pltpu.VMEM((BLOCK // LANES, height + 2, width + 16, LANES), f32),
            pltpu.VMEM((height, width, BLOCK), bf16),
            pltpu.VMEM((height, width, chans), f32),
            pltpu.VMEM((chans, height * width), bf16),
            pltpu.VMEM((1, chans), f32),
        ],
        compiler_params=params(),
        cost_estimate=cost(30),
        name="spread",
    )(*gconvs, *hiddens, *pres, *branches, *edges, w_depth, w_expand, field_in, gain, cotangent, *attn_gains)


def unpack_body(totals_ref, expand_ref, project_ref, qkv_ref, out_ref, depth_ref, gain_ref, attn_gain_ref):
    blocks = totals_ref.shape[1]
    small = totals_ref[:, :, 48:56, :].astype(f32)
    for side in range(2):
        here = slice(8 * side, 8 * side + 8)
        tile = totals_ref[:, :, here, :].astype(f32)
        project_ref[:, side * LANES : (side + 1) * LANES] = tile.reshape(-1, LANES)
        for j in range(blocks):
            lanes = slice((2 * j + side) * LANES, (2 * j + side + 1) * LANES)
            tile = totals_ref[:, j, 32 + 8 * side : 40 + 8 * side, :].astype(f32)
            expand_ref[:, lanes] = tile.reshape(-1, LANES)
            tile = totals_ref[:, j, 16 + 8 * side : 24 + 8 * side, :].astype(f32).reshape(-1, LANES)
            if j < blocks - 1:
                qkv_ref[:, lanes] = tile
            else:
                out_ref[:, side * LANES : (side + 1) * LANES] = tile
            for k in range(9):
                depth_ref[k // 3, k % 3 : k % 3 + 1, lanes] = small[2 * k + side, j, 0:1, :]
        lanes = slice(side * LANES, (side + 1) * LANES)
        gain_ref[:, lanes] = small[18 + side, blocks - 1, 0:1, :]
        attn_gain_ref[:, lanes] = small[20 + side, blocks - 1, 0:1, :]


def unpack(totals, wide, chans):
    vmem = pl.BlockSpec(memory_space=pltpu.VMEM)
    shapes = [(chans, wide), (wide, chans), (chans, 3 * chans), (chans, chans), (3, 3, wide), (1, chans), (1, chans)]
    return pl.pallas_call(
        unpack_body,
        out_shape=tuple(jax.ShapeDtypeStruct(shape, f32) for shape in shapes),
        in_specs=[vmem],
        out_specs=(vmem,) * len(shapes),
        compiler_params=pltpu.CompilerParams(vmem_limit_bytes=32 << 20),
        name="unpack",
    )(totals)


def outer_cycle(top, bottom, left, right):
    height = sum(piece.shape[0] for piece in left)
    fill = -(-(height + 2) // 8) * 8 - height - 2

    def pairs(axis):
        forward = [(i, i + 1) for i in range(lax.axis_size(axis) - 1)]
        return forward, [(b, a) for a, b in forward]

    forward, backward = pairs("row")
    above = lax.ppermute(bottom, "row", forward)
    below = lax.ppermute(top, "row", backward)
    forward, backward = pairs("col")

    def column(own, at):
        kind = own[0].dtype
        ends = [above[at : at + 1].astype(kind), *own, below[at : at + 1].astype(kind)]
        return jnp.concatenate(ends + [jnp.zeros((fill, above.shape[-1]), kind)])

    beside_left = lax.ppermute(column(right, above.shape[0] - 1), "col", forward)
    beside_right = lax.ppermute(column(left, 0), "col", backward)
    return above, below, beside_left, beside_right


def swap(values):
    return lax.all_to_all(values, ("row", "col"), split_axis=0, concat_axis=0, tiled=True)


def shards(field_in, cotangent, gain_conv, w_expand, w_depth, w_project, gain_attn, w_qkv, w_out):
    height, width, chans = field_in.shape
    wide = w_expand.shape[1]
    devices = lax.axis_size("row") * lax.axis_size("col")
    grad_scale = (height * width * devices) ** (-0.5)
    chunks = 2
    rows = height // chunks
    per = height * width // (GRID * GRID * chunks)
    gain_in = gain_conv.reshape(1, -1)
    above, below, left, right = outer_cycle(field_in[0], field_in[-1], [field_in[:, 0]], [field_in[:, -1]])
    hiddens, pres = [], []
    for k in range(chunks):
        hidden, pre = expand(k, chunks, field_in.reshape(-1, chans), gain_in, w_expand)
        hiddens.append(hidden.reshape(rows, width, wide))
        pres.append(pre.reshape(rows, width, wide))
    actives, convs, branches, gconvs, gcols, grows = [], [], [], [], [], []
    moved, qkvs, outs, gains = [], [], [], []
    for k in range(chunks):
        acted, conv, sent = mix(
            k, hiddens[k], above, below, left, right, gain_in, w_expand, w_depth, w_project, field_in, cotangent, per
        )
        actives.append(acted)
        convs.append(conv)
        if k > 0:
            sent, moved[k - 1] = lax.optimization_barrier((sent, moved[k - 1]))
        moved.append(swap(sent.reshape(devices, -1, chans)))
    for k in range(chunks):
        branch, qkv, out, gain = attention(moved[k], gain_attn, w_qkv, w_out)
        qkvs.append(qkv)
        outs.append(out)
        gains.append(gain)
        if k == 0:
            branch, moved[1] = lax.optimization_barrier((branch, moved[1]))
        else:
            branch, branches[k - 1] = lax.optimization_barrier((branch, branches[k - 1]))
        branches.append(swap(branch).reshape(rows, -1, 2 * per, chans))
    for k in range(chunks):
        gconv, gcol, grow, branches[k] = unmix(k, cotangent, branches[k], convs[k], w_project, per)
        gconvs.append(gconv)
        gcols.append(gcol)
        grows.append(grow)
    part = project_part(0, cotangent, branches[0], actives[0])
    early = project_part(1, cotangent, branches[1], actives[1], part, qkvs, outs)
    left, right = ([gcol[side] for gcol in gcols] for side in range(2))
    above, below, left, right = outer_cycle(grows[0], grows[-1], left, right)
    edge_rows = [above, below]
    edge_cols = [left, right]
    early_all = swap(early.reshape(devices, -1, LANES))
    early_own = jnp.sum(early_all, axis=0)
    grad_field, late = spread(
        gconvs, hiddens, pres, branches, [*edge_rows, *edge_cols], w_depth, w_expand, field_in, gain_in,
        cotangent, gains,
    )
    late, early_own = lax.optimization_barrier((late, early_own))
    late_own = jnp.sum(swap(late.reshape(devices, -1, LANES)), axis=0)
    own = (jnp.concatenate([early_own, late_own]) * grad_scale).astype(jnp.bfloat16)
    totals = swap(jnp.broadcast_to(own, (devices,) + own.shape))
    totals = totals.reshape(chans // 8, wide // BLOCK, -1, LANES)
    grad_expand, grad_project, grad_qkv, grad_out, grad_depth, grad_gain_conv, grad_gain = unpack(totals, wide, chans)
    return (
        grad_field,
        grad_gain_conv.reshape(-1),
        grad_expand,
        grad_depth,
        grad_project,
        grad_gain.reshape(-1),
        grad_qkv,
        grad_out,
    )


def solution(mesh):
    in_specs = (P("row", "col", None), P("row", "col", None), P(), P(), P(), P(), P(), P(), P())
    out_specs = (P("row", "col", None), P(), P(), P(), P(), P(), P(), P())

    return jax.shard_map(shards, mesh=mesh, in_specs=in_specs, out_specs=out_specs, check_vma=False)
```
